32 devices in a mesh: gx: 4 (over y, x), gy: 8 (over z, core).
Axes of the slice: x: 2, y: 2, z: 4, core: 2. Of those that a mesh axis runs over, the one named last changes fastest.
Arguments:
- features: bfloat16 [64, 512, 128], P(('gx', 'gy')), may hold values from -11 to 11
- brick_pos: int32 [64], P(('gx', 'gy')), may hold values from 0 to 4, as said below
- cotangent: bfloat16 [64, 512, 128], P(('gx', 'gy')), may hold values from -40 to 40
- first_kernel: bfloat16 [27, 128, 128], replicated, may hold values from -0.109375 to 0.109375
- second_kernel: bfloat16 [27, 128, 128], replicated, may hold values from -0.109375 to 0.109375
- norm_gain: float32 [128], replicated, may hold values from 0.1 to 1.9
Outputs:
- block_out: bfloat16 [64, 512, 128], P(('gx', 'gy'))
- feature_grad: bfloat16 [64, 512, 128], P(('gx', 'gy'))
- kernel_update: float32 [2, 27, 128, 128], replicated
- gain_update: float32 [128], replicated
The draws below stay inside these ranges and needn't reach their ends.
Inputs may be any that keep to these rules, and one draw needn't show every extreme that they name: `brick_pos`: on each device block the first k slots (k between max(1, 0) and 2, and k = 2 on at least one block) hold distinct positions below 4; the remaining slots hold 4.
All inputs are finite; a program needn't handle non-finite values.
Results may differ from the reference program's by a relative error of at most 0.0029.
Values may be sent and summed in bfloat16 or wider, within the bound.
No kernel may reach another device: no remote copies, remote signals or barrier semaphores. Data moves between devices by JAX's collectives and lax.ppermute only.
A program may use at most 128 MiB of HBM per device.

```python
import math
import jax
import jax.numpy as jnp
from jax import lax

CHANNEL_COUNT = 128
TAPS = 27
BX = 2
BY = 2
BZ = 1
BRICK_VOXELS = 512
POS = 4
BLOCK_SLOTS = 2
TOTAL_SLOTS = 64
N_GX = 4
N_GY = 8


def draw_brick_pos(key, part):
    device_blocks = TOTAL_SLOTS // BLOCK_SLOTS
    key_orders = jax.random.fold_in(key, 11)
    key_counts = jax.random.fold_in(key, 12)
    key_chosen = jax.random.fold_in(key, 13)
    order_keys = jax.random.split(key_orders, device_blocks)
    orders = jax.vmap(lambda single: jax.random.permutation(single, POS))(order_keys)[:, :BLOCK_SLOTS]
    fewest = max(1, BLOCK_SLOTS // 4)
    counts = jax.random.randint(key_counts, (device_blocks,), fewest, BLOCK_SLOTS + 1)
    chosen = jax.random.randint(key_chosen, (), 0, device_blocks)
    counts = jnp.where(jnp.arange(device_blocks) == chosen, BLOCK_SLOTS, counts)
    slot_index = jnp.arange(BLOCK_SLOTS)[None, :]
    placed = jnp.where(slot_index < counts[:, None], orders, POS)
    return placed.reshape(-1).astype(jnp.int32)


def draw_features(key, part):
    key_channel = jax.random.fold_in(key, 21)
    noise_key = jax.random.fold_in(key, 22)
    channel = jnp.exp(jax.random.uniform(key_channel, (CHANNEL_COUNT,), minval=math.log(0.3), maxval=math.log(3.0)))
    random_noise = jnp.clip(jax.random.normal(noise_key, (TOTAL_SLOTS, BRICK_VOXELS, CHANNEL_COUNT)), -3.5, 3.5)
    return (random_noise * channel).astype(jnp.bfloat16)


def draw_cotangent(key, part):
    device_blocks = TOTAL_SLOTS // BLOCK_SLOTS
    key_channel = jax.random.fold_in(key, 31)
    noise_key = jax.random.fold_in(key, 32)
    key_block = jax.random.fold_in(key, 33)
    channel = jnp.exp(jax.random.uniform(key_channel, (CHANNEL_COUNT,), minval=math.log(0.3), maxval=math.log(3.0)))
    ramp = jnp.arange(device_blocks, dtype=jnp.float32) / max(device_blocks - 1, 1) - 0.5
    jitter = jax.random.uniform(key_block, (device_blocks,), minval=0.8, maxval=1.25)
    factor = jnp.exp(ramp * math.log(3.0)) * jitter
    random_noise = jnp.clip(jax.random.normal(noise_key, (TOTAL_SLOTS, BRICK_VOXELS, CHANNEL_COUNT)), -3.5, 3.5)
    rows = jnp.repeat(factor, BLOCK_SLOTS)
    return (random_noise * channel[None, None, :] * rows[:, None, None]).astype(jnp.bfloat16)


def centred(key, shape, deviation, limit, kind=jnp.bfloat16):
    return jnp.clip(deviation * jax.random.normal(key, shape, jnp.float32), -limit, limit).astype(kind)


def setup_inputs(seed: int = 0) -> dict:
    splits = jax.random.split(jax.random.key(seed), 7)
    features = draw_features(jax.random.fold_in(splits[6], 71), 0)
    brick_pos = draw_brick_pos(jax.random.fold_in(splits[6], 71), 0)
    cotangent = draw_cotangent(jax.random.fold_in(splits[6], 71), 0)
    first_kernel = centred(splits[3], (TAPS, CHANNEL_COUNT, CHANNEL_COUNT), (TAPS * CHANNEL_COUNT) ** -0.5, 0.109375)
    second_kernel = centred(splits[4], (TAPS, CHANNEL_COUNT, CHANNEL_COUNT), (TAPS * CHANNEL_COUNT) ** -0.5, 0.109375)
    norm_gain = jnp.clip(1.0 + 0.18 * jax.random.normal(splits[5], (CHANNEL_COUNT,), jnp.float32), 0.1, 1.9)
    return {"features": features, "brick_pos": brick_pos, "cotangent": cotangent, "first_kernel": first_kernel, "second_kernel": second_kernel, "norm_gain": norm_gain}


clip_level = 0.5

def brick_coords(position):
    brick_x = position // (BY * BZ)
    brick_y = position // BZ % BY
    brick_z = position % BZ
    return (brick_x, brick_y, brick_z)

def activate(pre, norm_gain):
    average = lax.optimization_barrier(jnp.mean(pre, axis=-1, keepdims=True))
    center = pre - average
    spread = lax.optimization_barrier(jnp.mean(center * center, axis=-1, keepdims=True))
    normed = center * lax.rsqrt(spread + 1e-05) * norm_gain
    return normed * jax.nn.sigmoid(normed)

def apply_taps(tile_set, kernel, flipped):
    slot_count, channels = (tile_set.shape[0], tile_set.shape[-1])
    summed = jnp.zeros((slot_count * 512, channels), jnp.float32)
    for step_x in range(3):
        for step_y in range(3):
            for step_z in range(3):
                tap_index = (step_x * 3 + step_y) * 3 + step_z
                if flipped:
                    start_x, start_y, start_z = (2 - step_x, 2 - step_y, 2 - step_z)
                else:
                    start_x, start_y, start_z = (step_x, step_y, step_z)
                window = tile_set[:, start_x:start_x + 8, start_y:start_y + 8, start_z:start_z + 8, :]
                window = window.reshape(slot_count * 512, channels)
                if flipped:
                    summed = summed + lax.dot_general(window, kernel[tap_index], (((1,), (1,)), ((), ())), preferred_element_type=jnp.float32)
                else:
                    summed = summed + jnp.dot(window, kernel[tap_index], preferred_element_type=jnp.float32)
    return summed.reshape(slot_count, 512, channels)

def tap_grads(tile_set, upstream):
    slot_count, channels = (tile_set.shape[0], tile_set.shape[-1])
    flat_rows = upstream.reshape(slot_count * 512, channels)
    result = []
    for step_x in range(3):
        for step_y in range(3):
            for step_z in range(3):
                window = tile_set[:, step_x:step_x + 8, step_y:step_y + 8, step_z:step_z + 8, :]
                window = window.reshape(slot_count * 512, channels)
                result.append(lax.dot_general(window, flat_rows, (((0,), (0,)), ((), ())), preferred_element_type=jnp.float32))
    return jnp.stack(result)

def to_grid(values, put_x, put_y, put_z, bricks_x, bricks_y):
    slot_count, channels = (values.shape[0], values.shape[-1])
    bricks = jnp.zeros((bricks_x, bricks_y, BZ, 8, 8, 8, channels), values.dtype)
    bricks = bricks.at[put_x, put_y, put_z].set(values.reshape(slot_count, 8, 8, 8, channels), mode='drop')
    return bricks.transpose(0, 3, 1, 4, 2, 5, 6).reshape(bricks_x * 8, bricks_y * 8, BZ * 8, channels)

def cut_tiles(padded, brick_x, brick_y, brick_z):
    channels = padded.shape[-1]

    def take_tile(start_x, start_y, start_z):
        return lax.dynamic_slice(padded, (start_x * 8, start_y * 8, start_z * 8, start_x * 0), (10, 10, 10, channels))
    return jax.vmap(take_tile)(brick_x, brick_y, brick_z)

def reference(features, brick_pos, cotangent, first_kernel, second_kernel, norm_gain):
    bricks_x = BX * N_GX
    bricks_y = BY * N_GY
    slot_index = jnp.arange(TOTAL_SLOTS, dtype=jnp.int32)
    device = slot_index // BLOCK_SLOTS
    is_live = brick_pos < POS
    brick_x, brick_y, brick_z = brick_coords(jnp.minimum(brick_pos, POS - 1).astype(jnp.int32))
    whole_x = (device // N_GY * BX + brick_x).astype(jnp.int32)
    whole_y = (device % N_GY * BY + brick_y).astype(jnp.int32)
    brick_z = brick_z.astype(jnp.int32)
    put_x = jnp.where(is_live, whole_x, bricks_x).astype(jnp.int32)
    live_mask = is_live[:, None, None]
    given_rows = jnp.where(live_mask, features, jnp.zeros_like(features))
    upstream = jnp.where(live_mask, cotangent, jnp.zeros_like(cotangent))

    def tiles_for(values):
        dense_grid = to_grid(values, put_x, whole_y, brick_z, bricks_x, bricks_y)
        padded = jnp.pad(dense_grid, ((1, 1), (1, 1), (1, 1), (0, 0)))
        return cut_tiles(padded, whole_x, whole_y, brick_z)
    given_tiles = tiles_for(given_rows)
    first_pre = jnp.where(live_mask, apply_taps(given_tiles, first_kernel, False), 0.0)
    hidden_full, pullback = jax.vjp(activate, first_pre, norm_gain)
    hidden = jnp.where(live_mask, hidden_full, 0.0).astype(jnp.bfloat16)
    hidden_tiles = tiles_for(hidden)
    second_pre = jnp.where(live_mask, apply_taps(hidden_tiles, second_kernel, False), 0.0)
    block_out = (given_rows.astype(jnp.float32) + second_pre).astype(jnp.bfloat16)
    second_grad = tap_grads(hidden_tiles, upstream)
    hidden_grad = jnp.where(live_mask, apply_taps(tiles_for(upstream), second_kernel, True), 0.0)
    pre_full, gain_grad = pullback(hidden_grad)
    pre_grad = jnp.where(live_mask, pre_full, 0.0).astype(jnp.bfloat16)
    first_grad = tap_grads(given_tiles, pre_grad)
    back_conv = apply_taps(tiles_for(pre_grad), first_kernel, True)
    feature_grad = jnp.where(live_mask, upstream.astype(jnp.float32) + back_conv, 0.0).astype(jnp.bfloat16)
    stacked = jnp.stack([first_grad, second_grad])
    squares = jnp.sum(stacked * stacked) + jnp.sum(gain_grad * gain_grad)
    entries = 54.0 * CHANNEL_COUNT * CHANNEL_COUNT + CHANNEL_COUNT
    shrink = jnp.minimum(1.0, clip_level / jnp.sqrt(squares / entries + 1e-06))
    return (block_out, feature_grad, shrink * stacked, shrink * gain_grad)
```

```python
import functools

import jax
import jax.numpy as jnp
from jax import lax
from jax.experimental import pallas as pl
from jax.experimental.pallas import tpu as pltpu
from jax.sharding import PartitionSpec as P

BY = 2
POS = 4
TAPS = 27
P_ROWS = 1040
FACES = (128, 128, 144, 144)
C = 128
clip_level = 0.5
f32, bf16 = jnp.float32, jnp.bfloat16
VMEM = pl.BlockSpec(memory_space=pltpu.VMEM)
SMEM = pl.BlockSpec(memory_space=pltpu.SMEM)
PARAMS = pltpu.CompilerParams(vmem_limit_bytes=56 << 20)


def sds(shape, dtype):
    return jax.ShapeDtypeStruct(shape, dtype)


def place(pos_ref, slot):
    p = pos_ref[slot]
    q = jnp.minimum(p, POS - 1)
    return p < POS, q // BY, q % BY


def call(body, outs, scratch, args, n_smem):
    return pl.pallas_call(
        body,
        out_shape=outs,
        in_specs=[SMEM] * n_smem + [VMEM] * (len(args) - n_smem),
        out_specs=[VMEM] * len(outs),
        scratch_shapes=scratch,
        compiler_params=PARAMS,
    )(*args)


def pack_x_body(pos, a, b, lo, hi):
    lo[...] = jnp.zeros_like(lo)
    hi[...] = jnp.zeros_like(hi)
    for f, src in enumerate((a, b)):
        for s in range(2):
            live, bx, by = place(pos, s)
            rows = pl.ds(pl.multiple_of(by * 64, 64), 64)

            @pl.when(live & (bx == 0))
            def _():
                lo[f, rows, :] = src[s, 0:64, :]

            @pl.when(live & (bx == 1))
            def _():
                hi[f, rows, :] = src[s, 448:512, :]


def pack_y_body(pos, a, b, xl, xr, lo, hi, tmp):
    for f, src in enumerate((a, b)):
        for d, out in enumerate((lo, hi)):
            tmp[...] = jnp.zeros_like(tmp)
            at = 120 * d
            tmp[0] = xl[f, :, :].astype(f32)[at : at + 8]
            tmp[17] = xr[f, :, :].astype(f32)[at : at + 8]
            for s in range(2):
                live, bx, by = place(pos, s)

                @pl.when(live & (by == d))
                def _():
                    cube = src[s].astype(f32).reshape(8, 8, 8, C)
                    tmp[pl.ds(1 + bx * 8, 8)] = cube[:, 7 * d]

            out[f] = tmp[...].reshape(144, C).astype(bf16)


def build(grid, f, pos, src, xl, xr, yl, yr):
    grid[f] = jnp.zeros(grid.shape[1:], f32)
    for s in range(2):
        live, bx, by = place(pos, s)

        @pl.when(live)
        def _():
            grid[f, pl.ds(1 + bx * 8, 8), pl.ds(1 + by * 8, 8)] = (
                src[s].astype(f32).reshape(8, 8, 8, C)
            )

    grid[f, 0, 1:17] = xl[f].astype(f32).reshape(16, 8, C)
    grid[f, 17, 1:17] = xr[f].astype(f32).reshape(16, 8, C)
    grid[f, :, 0] = yl[f].astype(f32).reshape(18, 8, C)
    grid[f, :, 17] = yr[f].astype(f32).reshape(18, 8, C)


def window(grid, f, bx, by, j):
    sx, sy = j // 3, j % 3
    w = grid[f, pl.ds(bx * 8 + sx, 8), pl.ds(by * 8 + sy, 8)]
    return w.reshape(512, C).astype(bf16)


def up_z(v):
    z = lax.broadcasted_iota(jnp.int32, v.shape, 1)
    return jnp.where(z == 7, 0.0, pltpu.roll(v, 7, 1))


def down_z(v):
    z = lax.broadcasted_iota(jnp.int32, v.shape, 1)
    return jnp.where(z == 0, 0.0, pltpu.roll(v, 1, 1))


def fill_weights(w, k, flipped):
    for j in range(9):
        for oz in range(3):
            if flipped:
                w[oz * C : (oz + 1) * C, j * C : (j + 1) * C] = k[3 * (8 - j) + oz]
            else:
                w[j * C : (j + 1) * C, oz * C : (oz + 1) * C] = k[3 * j + oz]


def convolve(grid, f, bx, by, cols, w, flipped):
    for j in range(9):
        cols[:, j * C : (j + 1) * C] = window(grid, f, bx, by, j)
    dims = (((1,), (1,)), ((), ())) if flipped else (((1,), (0,)), ((), ()))
    y = lax.dot_general(cols[...], w[...], dims, preferred_element_type=f32)
    lower, mid, upper = (y[:, i * C : (i + 1) * C].reshape(64, 8, C) for i in range(3))
    if flipped:
        out = mid + up_z(lower) + down_z(upper)
    else:
        out = mid + down_z(lower) + up_z(upper)
    return out.reshape(512, C)


def split3(v):
    hi = v.astype(bf16).astype(f32)
    rest = v - hi
    mid = rest.astype(bf16).astype(f32)
    return hi, mid, rest - mid


def main_body(
    pos, meta, a, b, xl, xr, yl, yr, k1, k2, gain,
    hid, pre, msg, gain_part, grid, cols, w1, w2, hg
):
    core = meta[0]
    for f, src in enumerate((a, b)):
        build(grid, f, pos, src, xl, xr, yl, yr)
    fill_weights(w1, k1, False)
    fill_weights(w2, k2, True)
    at = P_ROWS
    for ref in (xl, xr, yl, yr):
        msg[at : at + ref.shape[1]] = ref[1 - core]
        at += ref.shape[1]
    g = gain[...]
    total = jnp.zeros((1, C), f32)
    for s in range(2):
        live, bx, by = place(pos, s)
        hg[...] = convolve(grid, 1, bx, by, cols, w2, True)
        first = convolve(grid, 0, bx, by, cols, w1, False)
        center = first - jnp.mean(first, axis=1, keepdims=True)
        spread = jnp.mean(center * center, axis=1, keepdims=True)
        inv = lax.rsqrt(spread + 1e-05)
        n = center * inv
        v = n * g
        sig = jax.nn.sigmoid(v)
        on = jnp.where(live, 1.0, 0.0)
        h = jnp.where(live, v * sig, 0.0).astype(bf16)
        grad = jnp.where(live, hg[...], 0.0)
        dv = grad * (sig * (1.0 + v * (1.0 - sig)))
        total = total + jnp.sum(dv * n, axis=0, keepdims=True)
        dn = dv * g
        m1 = jnp.mean(dn, axis=1, keepdims=True)
        m2 = jnp.mean(dn * n, axis=1, keepdims=True)
        p = (inv * (dn - m1 - n * m2)).astype(bf16)
        hid[s] = h
        pre[s] = p
        msg[s * 512 : (s + 1) * 512] = jnp.where(core == 0, h, p)
    gain_part[...] = jnp.broadcast_to(total, (8, C))
    msg[1024:P_ROWS] = pack3(total)


def out_body(pos, src, xl, xr, yl, yr, k, base, out, grid, cols, w, *, field):
    build(grid, 0, pos, src, *(e.at[field : field + 1] for e in (xl, xr, yl, yr)))
    fill_weights(w, k, field == 1)
    for s in range(2):
        live, bx, by = place(pos, s)
        y = convolve(grid, 0, bx, by, cols, w, field == 1)
        out[s] = jnp.where(live, base[s].astype(f32) + y, 0.0).astype(bf16)


def grads_body(
    pos, ppos, meta, a, b, xl, xr, yl, yr, other, hid, pre, msg, gain_part,
    low, out, gsum, grid, cols, pt, acc, *, chunks
):
    core, mine = meta[0], meta[1]

    @pl.when(core == 0)
    def _():
        build(grid, 0, pos, a, xl, xr, yl, yr)

    @pl.when(core != 0)
    def _():
        build(grid, 0, pos, b, *(e.at[1:2] for e in (xl, xr, yl, yr)))

    faces, at = [], P_ROWS
    for rows in FACES:
        faces.append(msg.at[pl.ds(at, rows)].reshape(1, rows, C))
        at += rows
    build(grid.at[1:2], 0, ppos, other, *faces)
    for k in range(4):
        s = k % 2
        _, bx, by = place(pos if k < 2 else ppos, s)
        rows = slice(k * 512, (k + 1) * 512)
        for j in range(9):
            cols[rows, j * C : (j + 1) * C] = window(grid, k // 2, bx, by, j)
        if k < 2:
            v = jnp.where(core == 0, pre[s], hid[s])
        else:
            v = msg[s * 512 : (s + 1) * 512]
        v = v.astype(f32).reshape(64, 8, C)
        for i, t in enumerate((up_z(v), v, down_z(v))):
            pt[i * C : (i + 1) * C, rows] = t.reshape(512, C).T.astype(bf16)
    y = jnp.dot(pt[...], cols[...], preferred_element_type=f32)
    for j in range(9):
        acc[j * 384 : (j + 1) * 384] = y[:, j * C : (j + 1) * C]
    size = acc.shape[0] // chunks
    half = chunks // 2
    for p in range(half):
        at = pl.multiple_of((mine ^ p) * size, 8)
        low[p * size : (p + 1) * size] = acc[pl.ds(at, size)]
    for p in range(0, half, 2):
        at = pl.multiple_of((mine ^ (p + half)) * size, 8)
        nxt = pl.multiple_of((mine ^ (p + half + 1)) * size, 8)
        two = jnp.concatenate([acc[pl.ds(at, size)], acc[pl.ds(nxt, size)]])
        out[p * size : (p + 2) * size] = two.astype(bf16)
    tile = msg[1024:P_ROWS].astype(f32)
    total = gain_part[0:1] + ((tile[2:3] + tile[1:2]) + tile[0:1])
    gsum[...] = jnp.broadcast_to(total, (8, C))
    out[half * size :] = pack3(total)


def pack3(v):
    hi, mid, low = split3(v)
    row = lax.broadcasted_iota(jnp.int32, (16, C), 0)
    return jnp.where(row == 0, hi, jnp.where(row == 1, mid, jnp.where(row == 2, low, 0.0))).astype(bf16)


def step_body(low, got, g, low_out, msg, g_out):
    rows = low.shape[0]
    tile = got[rows : rows + 16].astype(f32)
    total = g[0:1] + ((tile[2:3] + tile[1:2]) + tile[0:1])
    g_out[...] = jnp.broadcast_to(total, (8, C))
    added = low[...] + got[0:rows].astype(f32)
    if low_out is None:
        msg[0:rows] = added.astype(msg.dtype)
    else:
        keep = low_out.shape[0]
        low_out[...] = added[0:keep]
        msg[0 : rows - keep] = added[keep:].astype(msg.dtype)
        rows -= keep
    msg[rows : rows + 16] = pack3(total).astype(msg.dtype)


def final_body(meta, own, part, own_g, part_g, k_out, g_out, first, second, *, chunks):
    core, mine, theirs = meta[0], meta[1], meta[2]
    n = TAPS * C
    size = n // chunks

    def spread(dst, src, me):
        for p in range(chunks):
            at = pl.multiple_of((me ^ p) * size, 8)
            dst[pl.ds(at, size)] = src[p * size : (p + 1) * size].astype(f32)

    @pl.when(core == 0)
    def _():
        spread(first, own, mine)
        spread(second, part, theirs)

    @pl.when(core != 0)
    def _():
        spread(first, part, theirs)
        spread(second, own, mine)

    g = jnp.where(core == 0, own_g[0:1], part_g[0:1])
    total = jnp.sum(g * g)
    for ref in (first, second):
        v = ref[...].reshape(n // 8, 8, C)
        total = total + jnp.sum(jnp.sum(v * v, axis=0))
    entries = 2.0 * n * C + C
    norm = jnp.full((8, C), total / entries + 1e-06, f32)
    shrink = jnp.minimum(1.0, clip_level / jnp.sqrt(norm))[0:1]
    g_out[...] = g * shrink
    for t in range(TAPS):
        k_out[0, t] = first[t * C : (t + 1) * C].T * shrink
        u = TAPS - 1 - t
        k_out[1, t] = second[u * C : (u + 1) * C] * shrink


def shift(lo, hi, axis):
    n = lax.axis_size(axis)
    from_left = lax.ppermute(hi, axis, [(i, i + 1) for i in range(n - 1)])
    from_right = lax.ppermute(lo, axis, [(i + 1, i) for i in range(n - 1)])
    return from_left, from_right


def halos(pos, a, b):
    lo, hi = call(pack_x_body, [sds((2, 128, C), bf16)] * 2, [], (pos, a, b), 1)
    xl, xr = shift(lo, hi, "gx")
    lo, hi = call(
        pack_y_body,
        [sds((2, 144, C), bf16)] * 2,
        [pltpu.VMEM((18, 8, C), f32)],
        (pos, a, b, xl, xr),
        1,
    )
    yl, yr = shift(lo, hi, "gy")
    return xl, xr, yl, yr


def stages():
    nx, ny = lax.axis_size("gx"), lax.axis_size("gy")
    xs = [(1 << i, 0) for i in range(nx.bit_length() - 1)]
    zs = [(0, 1 << i) for i in range(1, ny.bit_length() - 1)]
    orders = (xs + zs, xs[1:] + xs[:1] + zs)
    perms = []
    for step in zip(*orders):
        pairs = []
        for i in range(nx):
            for j in range(ny):
                dx, dy = step[j % 2]
                pairs.append((i * ny + j, (i ^ dx) * ny + (j ^ dy)))
        perms.append(pairs)
    return orders, perms


def chunk_index(order, halvings, ix, iy):
    out = 0
    for s, (dx, dy) in enumerate(order[:halvings]):
        bit = ((ix & dx) | (iy & dy)) != 0
        out = out + bit.astype(jnp.int32) * (1 << (halvings - 1 - s))
    return jnp.asarray(out, jnp.int32)


def after(value, *done):
    return lax.optimization_barrier((value, *done))[0]


def per_device(features, brick_pos, cotangent, first_kernel, second_kernel, norm_gain):
    both = ("gx", "gy")
    ny = lax.axis_size("gy")
    ix, iy = lax.axis_index("gx"), lax.axis_index("gy")
    core = iy % 2
    orders, perms = stages()
    halvings = min(len(perms), 4)
    chunks = 1 << halvings
    me_a = chunk_index(orders[0], halvings, ix, iy)
    me_b = chunk_index(orders[1], halvings, ix, iy)
    meta = jnp.stack([core, jnp.where(core == 0, me_a, me_b), jnp.where(core == 0, me_b, me_a)])
    partner = [(i, i ^ 1) for i in range(ny)]
    n = TAPS * C

    ppos = lax.ppermute(brick_pos, "gy", partner)
    other = lax.ppermute(jnp.where(core == 0, cotangent, features), "gy", partner)
    edge = halos(brick_pos, features, cotangent)
    grid = pltpu.VMEM((2, 18, 18, 8, C), f32)
    cols = pltpu.VMEM((512, 9 * C), bf16)
    straight, turned = pltpu.VMEM((9 * C, 3 * C), bf16), pltpu.VMEM((3 * C, 9 * C), bf16)
    hid, pre, msg, gain_part = call(
        main_body,
        [sds((2, 512, C), bf16)] * 2 + [sds((P_ROWS + sum(FACES), C), bf16), sds((8, C), f32)],
        [grid, cols, straight, turned, pltpu.VMEM((512, C), f32)],
        (brick_pos, meta, features, cotangent, *edge, first_kernel, second_kernel, norm_gain.reshape(1, C)),
        2,
    )
    pmsg = lax.ppermute(msg, "gy", partner)
    low, out, g = call(
        functools.partial(grads_body, chunks=chunks),
        [sds((n // 2, C), f32), sds((n // 2 + 16, C), bf16), sds((8, C), f32)],
        [
            grid,
            pltpu.VMEM((2048, 9 * C), bf16),
            pltpu.VMEM((3 * C, 2048), bf16),
            pltpu.VMEM((n, C), f32),
        ],
        (brick_pos, ppos, meta, features, cotangent, *edge, other, hid, pre, pmsg, gain_part),
        3,
    )

    def work():
        ready = yield
        lo, hi = call(
            pack_x_body, [sds((2, 128, C), bf16)] * 2, [], (brick_pos, after(hid, ready), pre), 1
        )
        xl, xr = shift(lo, hi, "gx")
        ready = yield lo
        lo, hi = call(
            pack_y_body,
            [sds((2, 144, C), bf16)] * 2,
            [pltpu.VMEM((18, 8, C), f32)],
            (brick_pos, after(hid, ready), pre, xl, xr),
            1,
        )
        yl, yr = shift(lo, hi, "gy")
        ready = yield lo
        results = []
        for f, (src, k, base, w) in enumerate(
            ((hid, second_kernel, features, straight), (pre, first_kernel, cotangent, turned))
        ):
            (res,) = call(
                functools.partial(out_body, field=f),
                [sds((2, 512, C), bf16)],
                [pltpu.VMEM((1, 18, 18, 8, C), f32), cols, w],
                (brick_pos, after(src, ready), xl, xr, yl, yr, k, base),
                1,
            )
            results.append(res)
            ready = yield res
        yield results

    side = work()
    next(side)
    rows = n // 2
    for s in range(len(perms)):
        done = side.send(out) if s < 4 else None
        got = lax.ppermute(out, both, perms[s])
        last = s == len(perms) - 1
        wide = s + 2 >= len(perms)
        halve = s + 1 < halvings
        keep = rows // 2 if halve else 0
        outs = [sds((rows - keep + 16, C), bf16 if halve and not wide else f32), sds((8, C), f32)]
        if halve:
            outs = [sds((keep, C), f32)] + outs
            body = step_body
        else:
            body = lambda low, got, g, *rest: step_body(low, got, g, None, *rest)
        res = call(body, outs, [], (low, got, g), 0)
        if halve:
            low, out, g = res
            rows = keep
        else:
            out, g = res
            low = out[:rows]
        if done is not None:
            out = after(out, done)
    results = side.send(out)
    full = out[:rows].astype(bf16)
    for perm in reversed(perms[:halvings]):
        full = jnp.concatenate([full, lax.ppermute(full, both, perm)])
    part = lax.ppermute(full, "gy", partner)
    gain = lax.ppermute(g, "gy", partner)
    k_up, g_up = call(
        functools.partial(final_body, chunks=chunks),
        [sds((2, TAPS, C, C), f32), sds((1, C), f32)],
        [pltpu.VMEM((n, C), f32), pltpu.VMEM((n, C), f32)],
        (meta, full, part, g, gain),
        1,
    )
    return (*results, k_up, g_up.reshape(C))


def solution(mesh):
    rows = P(("gx", "gy"), None, None)
    return jax.shard_map(
        per_device,
        mesh=mesh,
        in_specs=(rows, P(("gx", "gy")), rows, P(), P(), P()),
        out_specs=(rows, rows, P(), P()),
        check_vma=False,
    )
```

```python
import functools

import jax
import jax.numpy as jnp
from jax import lax
from jax.experimental import pallas as pl
from jax.experimental.pallas import tpu as pltpu
from jax.sharding import PartitionSpec as P


BY = 2
POS = 4
TAPS = 27
P_ROWS = 1040
FACES = (128, 128, 144, 144)
C = 128
clip_level = 0.5
f32, bf16 = jnp.float32, jnp.bfloat16
VMEM = pl.BlockSpec(memory_space=pltpu.VMEM)
SMEM = pl.BlockSpec(memory_space=pltpu.SMEM)
PARAMS = pltpu.CompilerParams(vmem_limit_bytes=28 << 20)


def sds(shape, dtype):
    return jax.ShapeDtypeStruct(shape, dtype)


def place(pos_ref, slot):
    p = pos_ref[slot]
    q = jnp.minimum(p, POS - 1)
    return p < POS, q // BY, q % BY


def call(body, outs, scratch, args, n_smem):
    return pl.pallas_call(
        body,
        out_shape=outs,
        in_specs=[SMEM] * n_smem + [VMEM] * (len(args) - n_smem),
        out_specs=[VMEM] * len(outs),
        scratch_shapes=scratch,
        compiler_params=PARAMS,
    )(*args)


def pack_x(pos, src, f, lo, hi):
    for s in range(2):
        live, bx, by = place(pos, s)
        rows = pl.ds(pl.multiple_of(by * 64, 64), 64)

        @pl.when(live & (bx == 0))
        def _():
            lo[f, rows] = src[s, 0:64]

        @pl.when(live & (bx == 1))
        def _():
            hi[f, rows] = src[s, 448:512]


def pack_x_body(pos, a, b, lo, hi):
    lo[...] = jnp.zeros_like(lo)
    hi[...] = jnp.zeros_like(hi)
    pack_x(pos, a, 0, lo, hi)
    pack_x(pos, b, 1, lo, hi)


def load_body(pos, core, a, b, a_out, b_out, sent, lo, hi):
    pack_x_body(pos, a, b, lo, hi)
    a_out[...] = a[...]
    b_out[...] = b[...]
    sent[...] = jnp.where(core[0] == 0, b[...], a[...])


def pack_y_body(pos, a, b, xl, xr, lo, hi, tmp):
    for f, src in enumerate((a, b)):
        for d, out in enumerate((lo, hi)):
            tmp[...] = jnp.zeros_like(tmp)
            at = 112 * d
            tmp[0] = xl[f, at : at + 16].astype(f32)[8 * d : 8 * d + 8]
            tmp[17] = xr[f, at : at + 16].astype(f32)[8 * d : 8 * d + 8]
            for s in range(2):
                live, bx, by = place(pos, s)

                @pl.when(live & (by == d))
                def _():
                    for x in range(8):
                        at = x * 64 + 48 * d
                        tmp[1 + bx * 8 + x] = src[s, at : at + 16].astype(f32)[8 * d : 8 * d + 8]

            out[f] = tmp[...].reshape(144, C).astype(bf16)


def build(grid, f, pos, src, xl, xr, yl, yr):
    grid[f] = jnp.zeros(grid.shape[1:], f32)
    for s in range(2):
        live, bx, by = place(pos, s)

        @pl.when(live)
        def _():
            grid[f, pl.ds(1 + bx * 8, 8), pl.ds(1 + by * 8, 8)] = (
                src[s].astype(f32).reshape(8, 8, 8, C)
            )

    grid[f, 0, 1:17] = xl[f].astype(f32).reshape(16, 8, C)
    grid[f, 17, 1:17] = xr[f].astype(f32).reshape(16, 8, C)
    grid[f, :, 0] = yl[f].astype(f32).reshape(18, 8, C)
    grid[f, :, 17] = yr[f].astype(f32).reshape(18, 8, C)


def window(grid, f, bx, by, j):
    sx, sy = j // 3, j % 3
    w = grid[f, pl.ds(bx * 8 + sx, 8), pl.ds(by * 8 + sy, 8)]
    return w.reshape(512, C).astype(bf16)


def up_z(v):
    z = lax.broadcasted_iota(jnp.int32, v.shape, 1)
    return jnp.where(z == 7, 0.0, pltpu.roll(v, 7, 1))


def down_z(v):
    z = lax.broadcasted_iota(jnp.int32, v.shape, 1)
    return jnp.where(z == 0, 0.0, pltpu.roll(v, 1, 1))


def prep_body(k1, k2, gain, w1, w2, t1, t2, gain_out):
    for k, w, t in ((k1, w1, t1), (k2, w2, t2)):
        for j in range(9):
            for oz in range(3):
                w[j * C : (j + 1) * C, oz * C : (oz + 1) * C] = k[3 * j + oz]
                t[oz * C : (oz + 1) * C, j * C : (j + 1) * C] = k[3 * (8 - j) + oz]
    gain_out[...] = gain[...]


def convolve(grid, f, bx, by, cols, w, flipped):
    for j in range(9):
        cols[:, j * C : (j + 1) * C] = window(grid, f, bx, by, j)
    dims = (((1,), (1,)), ((), ())) if flipped else (((1,), (0,)), ((), ()))
    y = lax.dot_general(cols[...], w[...], dims, preferred_element_type=f32)
    lower, mid, upper = (y[:, i * C : (i + 1) * C].reshape(64, 8, C) for i in range(3))
    if flipped:
        out = mid + up_z(lower) + down_z(upper)
    else:
        out = mid + down_z(lower) + up_z(upper)
    return out.reshape(512, C)


def split3(v):
    hi = v.astype(bf16).astype(f32)
    rest = v - hi
    mid = rest.astype(bf16).astype(f32)
    return hi, mid, rest - mid


def main_body(
    pos, meta, a, b, xl, xr, yl, yr, w1, w2, gain,
    hid, pre, msg, gain_part, grid, cols, hg
):
    core = meta[0]
    for f, src in enumerate((a, b)):
        build(grid, f, pos, src, xl, xr, yl, yr)
    at = P_ROWS
    for ref in (xl, xr, yl, yr):
        msg[at : at + ref.shape[1]] = ref[1 - core]
        at += ref.shape[1]
    g = gain[...]
    total = jnp.zeros((1, C), f32)
    for s in range(2):
        live, bx, by = place(pos, s)
        hg[...] = convolve(grid, 1, bx, by, cols, w2, True)
        first = convolve(grid, 0, bx, by, cols, w1, False)
        center = first - jnp.mean(first, axis=1, keepdims=True)
        spread = jnp.mean(center * center, axis=1, keepdims=True)
        inv = lax.rsqrt(spread + 1e-05)
        n = center * inv
        v = n * g
        sig = jax.nn.sigmoid(v)
        on = jnp.where(live, 1.0, 0.0)
        h = jnp.where(live, v * sig, 0.0).astype(bf16)
        grad = jnp.where(live, hg[...], 0.0)
        dv = grad * (sig * (1.0 + v * (1.0 - sig)))
        total = total + jnp.sum(dv * n, axis=0, keepdims=True)
        dn = dv * g
        m1 = jnp.mean(dn, axis=1, keepdims=True)
        m2 = jnp.mean(dn * n, axis=1, keepdims=True)
        p = (inv * (dn - m1 - n * m2)).astype(bf16)
        hid[s] = h
        pre[s] = p
        msg[s * 512 : (s + 1) * 512] = jnp.where(core == 0, h, p)
    gain_part[...] = jnp.broadcast_to(total, (8, C))
    msg[1024:P_ROWS] = pack3(total)


def out_body(pos, src, xl, xr, yl, yr, w, base, out, grid, cols, *, field):
    build(grid, 0, pos, src, *(e.at[field : field + 1] for e in (xl, xr, yl, yr)))
    for s in range(2):
        live, bx, by = place(pos, s)
        y = convolve(grid, 0, bx, by, cols, w, field == 1)
        out[s] = jnp.where(live, base[s].astype(f32) + y, 0.0).astype(bf16)


def grads_body(
    pos, ppos, meta, a, b, xl, xr, yl, yr, other, hid, pre, msg, gain_part,
    low, out, gsum, grid, cols, pt, acc, *, chunks
):
    core, mine = meta[0], meta[1]

    @pl.when(core == 0)
    def _():
        build(grid, 0, pos, a, xl, xr, yl, yr)

    @pl.when(core != 0)
    def _():
        build(grid, 0, pos, b, *(e.at[1:2] for e in (xl, xr, yl, yr)))

    faces, at = [], P_ROWS
    for rows in FACES:
        faces.append(msg.at[pl.ds(at, rows)].reshape(1, rows, C))
        at += rows
    build(grid.at[1:2], 0, ppos, other, *faces)
    for k in range(4):
        s = k % 2
        _, bx, by = place(pos if k < 2 else ppos, s)
        rows = slice(k * 512, (k + 1) * 512)
        for j in range(9):
            cols[rows, j * C : (j + 1) * C] = window(grid, k // 2, bx, by, j)
        if k < 2:
            v = jnp.where(core == 0, pre[s], hid[s])
        else:
            v = msg[s * 512 : (s + 1) * 512]
        v = v.astype(f32).reshape(64, 8, C)
        for i, t in enumerate((up_z(v), v, down_z(v))):
            pt[i * C : (i + 1) * C, rows] = t.reshape(512, C).T.astype(bf16)
    y = jnp.dot(pt[...], cols[...], preferred_element_type=f32)
    for j in range(9):
        acc[j * 384 : (j + 1) * 384] = y[:, j * C : (j + 1) * C]
    size = acc.shape[0] // chunks
    half = chunks // 2
    for p in range(half):
        at = pl.multiple_of((mine ^ p) * size, 8)
        low[p * size : (p + 1) * size] = acc[pl.ds(at, size)]
    for p in range(0, half, 2):
        at = pl.multiple_of((mine ^ (p + half)) * size, 8)
        nxt = pl.multiple_of((mine ^ (p + half + 1)) * size, 8)
        two = jnp.concatenate([acc[pl.ds(at, size)], acc[pl.ds(nxt, size)]])
        out[p * size : (p + 2) * size] = two.astype(bf16)
    tile = msg[1024:P_ROWS].astype(f32)
    total = gain_part[0:1] + ((tile[2:3] + tile[1:2]) + tile[0:1])
    gsum[...] = jnp.broadcast_to(total, (8, C))


def pack3(v):
    hi, mid, low = split3(v)
    row = lax.broadcasted_iota(jnp.int32, (16, C), 0)
    return jnp.where(row == 0, hi, jnp.where(row == 1, mid, jnp.where(row == 2, low, 0.0))).astype(bf16)


def final_body(meta, own0, own1, part0, part1, k_out, g_out, first, second, gains, *, chunks):
    core, mine, theirs = meta[0], meta[1], meta[2]
    n = TAPS * C
    size = n // chunks
    half = chunks // 2

    def spread(dst, srcs, me, gain):
        for p in range(chunks):
            src, q = srcs[p // half], p % half
            piece = src[q * (size + 8) : (q + 1) * (size + 8)].astype(f32)
            dst[pl.ds(pl.multiple_of((me ^ p) * size, 8), size)] = piece[:size]
            if gain:
                t = piece[size:]
                gains[me ^ p] = jnp.broadcast_to((t[2:3] + t[1:2]) + t[0:1], (8, C))

    @pl.when(core == 0)
    def _():
        spread(first, (own0, own1), mine, True)
        spread(second, (part0, part1), theirs, False)

    @pl.when(core != 0)
    def _():
        spread(first, (part0, part1), theirs, True)
        spread(second, (own0, own1), mine, False)

    g = jnp.sum(gains[...], axis=0)[0:1]
    total = jnp.sum(g * g)
    for ref in (first, second):
        v = ref[...].reshape(n // 8, 8, C)
        total = total + jnp.sum(jnp.sum(v * v, axis=0))
    entries = 2.0 * n * C + C
    norm = jnp.full((8, C), total / entries + 1e-06, f32)
    shrink = jnp.minimum(1.0, clip_level / jnp.sqrt(norm))[0:1]
    g_out[...] = g * shrink
    for t in range(TAPS):
        k_out[0, t] = first[t * C : (t + 1) * C].T * shrink
        u = TAPS - 1 - t
        k_out[1, t] = second[u * C : (u + 1) * C] * shrink


def shift(lo, hi, axis):
    n = lax.axis_size(axis)
    from_left = lax.ppermute(hi, axis, [(i, i + 1) for i in range(n - 1)])
    from_right = lax.ppermute(lo, axis, [(i + 1, i) for i in range(n - 1)])
    return from_left, from_right


def y_faces(pos, a, b, xl, xr):
    return call(
        pack_y_body,
        [sds((2, 144, C), bf16)] * 2,
        [pltpu.VMEM((18, 8, C), f32)],
        (pos, a, b, xl, xr),
        1,
    )


def stages():
    nx, ny = lax.axis_size("gx"), lax.axis_size("gy")
    xs = [(1 << i, 0) for i in range(nx.bit_length() - 1)]
    zs = [(0, 1 << i) for i in range(1, ny.bit_length() - 1)]
    orders = (xs + zs, xs[1:] + xs[:1] + zs)
    perms = []
    for step in zip(*orders):
        pairs = []
        for i in range(nx):
            for j in range(ny):
                dx, dy = step[j % 2]
                pairs.append((i * ny + j, (i ^ dx) * ny + (j ^ dy)))
        perms.append(pairs)
    return orders, perms


def chunk_index(order, halvings, ix, iy):
    out = 0
    for s, (dx, dy) in enumerate(order[:halvings]):
        bit = ((ix & dx) | (iy & dy)) != 0
        out = out + bit.astype(jnp.int32) * (1 << (halvings - 1 - s))
    return jnp.asarray(out, jnp.int32)


def gain_tile(g):
    rows, rest = [], g
    for _ in range(3):
        part = lax.reduce_precision(rest, 8, 7)
        rows.append(part)
        rest = rest - part
    return jnp.concatenate(rows + [jnp.zeros((5, C), f32)]).astype(bf16)


def after(value, *done):
    return lax.optimization_barrier((value, *done))[0]


def per_device(features, brick_pos, cotangent, first_kernel, second_kernel, norm_gain):
    both = ("gx", "gy")
    ny = lax.axis_size("gy")
    ix, iy = lax.axis_index("gx"), lax.axis_index("gy")
    core = iy % 2
    orders, perms = stages()
    halvings = min(len(perms), 4)
    chunks = 1 << halvings
    me_a = chunk_index(orders[0], halvings, ix, iy)
    me_b = chunk_index(orders[1], halvings, ix, iy)
    meta = jnp.stack([core, jnp.where(core == 0, me_a, me_b), jnp.where(core == 0, me_b, me_a)])
    partner = [(i, i ^ 1) for i in range(ny)]
    n = TAPS * C
    size = n // chunks

    hbm = lambda v: pltpu.with_memory_space_constraint(v, pltpu.HBM)
    features, cotangent, sent, lo, hi = call(
        load_body,
        [sds((2, 512, C), bf16)] * 3 + [sds((2, 128, C), bf16)] * 2,
        [],
        (brick_pos, core.reshape(1), hbm(features), hbm(cotangent)),
        2,
    )
    xl, xr = shift(lo, hi, "gx")
    ppos = lax.ppermute(brick_pos, "gy", partner)
    other = lax.ppermute(sent, "gy", partner)
    straight, turned = sds((9 * C, 3 * C), bf16), sds((3 * C, 9 * C), bf16)
    w1, w2, t1, t2, gain = call(
        prep_body,
        [straight, straight, turned, turned, sds((1, C), f32)],
        [],
        (hbm(first_kernel), hbm(second_kernel), hbm(norm_gain.reshape(1, C))),
        0,
    )
    lo, hi = y_faces(brick_pos, after(features, gain), cotangent, xl, xr)
    lo = after(lo, ppos, other, meta)
    edge = xl, xr, *shift(lo, hi, "gy")
    grid = pltpu.VMEM((2, 18, 18, 8, C), f32)
    cols = pltpu.VMEM((512, 9 * C), bf16)
    hid, pre, msg, gain_part = call(
        main_body,
        [sds((2, 512, C), bf16)] * 2 + [sds((P_ROWS + sum(FACES), C), bf16), sds((8, C), f32)],
        [grid, cols, pltpu.VMEM((512, C), f32)],
        (brick_pos, meta, features, cotangent, *edge, w1, t2, gain),
        2,
    )
    pmsg = lax.ppermute(msg, "gy", partner)
    low, out, g = call(
        functools.partial(grads_body, chunks=chunks),
        [sds((n // 2, C), f32), sds((n // 2, C), bf16), sds((8, C), f32)],
        [
            grid,
            pltpu.VMEM((2048, 9 * C), bf16),
            pltpu.VMEM((3 * C, 2048), bf16),
            pltpu.VMEM((n, C), f32),
        ],
        (brick_pos, ppos, meta, features, cotangent, *edge, other, hid, pre, pmsg, gain_part),
        3,
    )
    g = g[0:1]

    lo, hi = call(pack_x_body, [sds((2, 128, C), bf16)] * 2, [], (brick_pos, after(hid, out), pre), 1)
    xl, xr = shift(lo, hi, "gx")
    lo, hi = y_faces(brick_pos, hid, pre, xl, xr)
    around = xl, xr, *shift(lo, hi, "gy")
    results = []
    for f, (src, w, base) in enumerate(((hid, w2, features), (pre, t1, cotangent))):
        (res,) = call(
            functools.partial(out_body, field=f),
            [sds((2, 512, C), bf16)],
            [pltpu.VMEM((1, 18, 18, 8, C), f32), cols],
            (brick_pos, src, *around, w, base),
            1,
        )
        results.append(res)

    for s in range(halvings):
        got = lax.ppermute(out, both, perms[s])
        low = low + got.astype(f32)
        if s + 1 < halvings:
            half = low.shape[0] // 2
            low, out = low[:half], low[half:]
            if s + 2 < halvings:
                out = out.astype(bf16)
    for s in range(halvings, len(perms)):
        got = lax.ppermute(jnp.concatenate([low, jnp.broadcast_to(g, (8, C))]), both, perms[s])
        low, g = low + got[:size], g + got[size : size + 1]

    full = jnp.concatenate([low.astype(bf16), gain_tile(g)])
    for s in reversed(range(halvings)):
        got = lax.ppermute(full, both, perms[s])
        if s:
            full = jnp.concatenate([full, got])
    early = lax.ppermute(full, "gy", partner)
    late = lax.ppermute(got, "gy", partner)
    k_up, g_up = call(
        functools.partial(final_body, chunks=chunks),
        [sds((2, TAPS, C, C), f32), sds((1, C), f32)],
        [pltpu.VMEM((n, C), f32), pltpu.VMEM((n, C), f32), pltpu.VMEM((chunks, 8, C), f32)],
        (meta, full, got, early, late),
        1,
    )
    return (*results, k_up, g_up.reshape(C))


def solution(mesh):
    rows = P(("gx", "gy"), None, None)

    return jax.shard_map(
        per_device,
        mesh=mesh,
        in_specs=(rows, P(("gx", "gy")), rows, P(), P(), P()),
        out_specs=(rows, rows, P(), P()),
        check_vma=False,
    )
```

```python
import functools

import jax
import jax.numpy as jnp
from jax import lax
from jax.experimental import pallas as pl
from jax.experimental.pallas import tpu as pltpu
from jax.sharding import PartitionSpec as P


BY = 2
POS = 4
TAPS = 27
P_ROWS = 1040
FACES = (128, 128, 144, 144)
C = 128
clip_level = 0.5
f32, bf16 = jnp.float32, jnp.bfloat16
VMEM = pl.BlockSpec(memory_space=pltpu.VMEM)
SMEM = pl.BlockSpec(memory_space=pltpu.SMEM)


def sds(shape, dtype):
    return jax.ShapeDtypeStruct(shape, dtype)


def place(pos_ref, slot):
    p = pos_ref[slot]
    q = jnp.minimum(p, POS - 1)
    return p < POS, q // BY, q % BY


def call(body, outs, scratch, args, n_smem, mib=4):
    return pl.pallas_call(
        body,
        out_shape=outs,
        in_specs=[SMEM] * n_smem + [VMEM] * (len(args) - n_smem),
        out_specs=[VMEM] * len(outs),
        scratch_shapes=scratch,
        compiler_params=pltpu.CompilerParams(vmem_limit_bytes=mib << 20),
    )(*args)


def pack_x(pos, src, f, lo, hi):
    for s in range(2):
        live, bx, by = place(pos, s)
        rows = pl.ds(pl.multiple_of(by * 64, 64), 64)

        @pl.when(live & (bx == 0))
        def _():
            lo[f, rows] = src[s, 0:64]

        @pl.when(live & (bx == 1))
        def _():
            hi[f, rows] = src[s, 448:512]


def pack_x_body(pos, a, b, lo, hi):
    lo[...] = jnp.zeros_like(lo)
    hi[...] = jnp.zeros_like(hi)
    pack_x(pos, a, 0, lo, hi)
    pack_x(pos, b, 1, lo, hi)


def load_body(pos, core, a, b, a_out, b_out, sent, lo, hi):
    pack_x_body(pos, a, b, lo, hi)
    a_out[...] = a[...]
    b_out[...] = b[...]
    sent[...] = jnp.where(core[0] == 0, b[...], a[...])


def pack_y_body(pos, a, b, xl, xr, lo, hi, tmp):
    for f, src in enumerate((a, b)):
        for d, out in enumerate((lo, hi)):
            tmp[...] = jnp.zeros_like(tmp)
            at = 112 * d
            tmp[0] = xl[f, at : at + 16].astype(f32)[8 * d : 8 * d + 8]
            tmp[17] = xr[f, at : at + 16].astype(f32)[8 * d : 8 * d + 8]
            for s in range(2):
                live, bx, by = place(pos, s)

                @pl.when(live & (by == d))
                def _():
                    for x in range(8):
                        at = x * 64 + 48 * d
                        tmp[1 + bx * 8 + x] = src[s, at : at + 16].astype(f32)[8 * d : 8 * d + 8]

            out[f] = tmp[...].reshape(144, C).astype(bf16)


def build(grid, f, pos, src, xl, xr, yl, yr):
    grid[f] = jnp.zeros(grid.shape[1:], f32)
    for s in range(2):
        live, bx, by = place(pos, s)

        @pl.when(live)
        def _():
            grid[f, pl.ds(1 + bx * 8, 8), pl.ds(1 + by * 8, 8)] = (
                src[s].astype(f32).reshape(8, 8, 8, C)
            )

    grid[f, 0, 1:17] = xl[f].astype(f32).reshape(16, 8, C)
    grid[f, 17, 1:17] = xr[f].astype(f32).reshape(16, 8, C)
    grid[f, :, 0] = yl[f].astype(f32).reshape(18, 8, C)
    grid[f, :, 17] = yr[f].astype(f32).reshape(18, 8, C)


def window(grid, f, bx, by, j):
    sx, sy = j // 3, j % 3
    w = grid[f, pl.ds(bx * 8 + sx, 8), pl.ds(by * 8 + sy, 8)]
    return w.reshape(512, C).astype(bf16)


def up_z(v):
    z = lax.broadcasted_iota(jnp.int32, v.shape, 1)
    return jnp.where(z == 7, 0.0, pltpu.roll(v, 7, 1))


def down_z(v):
    z = lax.broadcasted_iota(jnp.int32, v.shape, 1)
    return jnp.where(z == 0, 0.0, pltpu.roll(v, 1, 1))


def prep_body(k1, k2, gain, w1, w2, t1, t2, gain_out):
    for k, w, t in ((k1, w1, t1), (k2, w2, t2)):
        for j in range(9):
            for oz in range(3):
                w[j * C : (j + 1) * C, oz * C : (oz + 1) * C] = k[3 * j + oz]
                t[oz * C : (oz + 1) * C, j * C : (j + 1) * C] = k[3 * (8 - j) + oz]
    gain_out[...] = gain[...]


def convolve(grid, f, bx, by, cols, w, flipped):
    for j in range(9):
        cols[:, j * C : (j + 1) * C] = window(grid, f, bx, by, j)
    dims = (((1,), (1,)), ((), ())) if flipped else (((1,), (0,)), ((), ()))
    y = lax.dot_general(cols[...], w[...], dims, preferred_element_type=f32)
    lower, mid, upper = (y[:, i * C : (i + 1) * C].reshape(64, 8, C) for i in range(3))
    if flipped:
        out = mid + up_z(lower) + down_z(upper)
    else:
        out = mid + down_z(lower) + up_z(upper)
    return out.reshape(512, C)


def split3(v):
    hi = v.astype(bf16).astype(f32)
    rest = v - hi
    mid = rest.astype(bf16).astype(f32)
    return hi, mid, rest - mid


def main_body(
    pos, meta, a, b, xl, xr, yl, yr, w1, w2, gain,
    hid, pre, msg, gain_part, grid, cols, hg
):
    core = meta[0]
    for f, src in enumerate((a, b)):
        build(grid, f, pos, src, xl, xr, yl, yr)
    at = P_ROWS
    for ref in (xl, xr, yl, yr):
        msg[at : at + ref.shape[1]] = ref[1 - core]
        at += ref.shape[1]
    g = gain[...]
    total = jnp.zeros((1, C), f32)
    for s in range(2):
        live, bx, by = place(pos, s)
        hg[...] = convolve(grid, 1, bx, by, cols, w2, True)
        first = convolve(grid, 0, bx, by, cols, w1, False)
        center = first - jnp.mean(first, axis=1, keepdims=True)
        spread = jnp.mean(center * center, axis=1, keepdims=True)
        inv = lax.rsqrt(spread + 1e-05)
        n = center * inv
        v = n * g
        sig = jax.nn.sigmoid(v)
        on = jnp.where(live, 1.0, 0.0)
        h = jnp.where(live, v * sig, 0.0).astype(bf16)
        grad = jnp.where(live, hg[...], 0.0)
        dv = grad * (sig * (1.0 + v * (1.0 - sig)))
        total = total + jnp.sum(dv * n, axis=0, keepdims=True)
        dn = dv * g
        m1 = jnp.mean(dn, axis=1, keepdims=True)
        m2 = jnp.mean(dn * n, axis=1, keepdims=True)
        p = (inv * (dn - m1 - n * m2)).astype(bf16)
        hid[s] = h
        pre[s] = p
        msg[s * 512 : (s + 1) * 512] = jnp.where(core == 0, h, p)
    gain_part[...] = jnp.broadcast_to(total, (8, C))
    msg[1024:P_ROWS] = pack3(total)


def out_body(pos, src, xl, xr, yl, yr, w, base, out, grid, cols, *, field):
    build(grid, 0, pos, src, *(e.at[field : field + 1] for e in (xl, xr, yl, yr)))
    for s in range(2):
        live, bx, by = place(pos, s)
        y = convolve(grid, 0, bx, by, cols, w, field == 1)
        out[s] = jnp.where(live, base[s].astype(f32) + y, 0.0).astype(bf16)


def grads_body(
    pos, ppos, meta, a, b, xl, xr, yl, yr, other, hid, pre, msg, gain_part,
    keep_b, keep_a, out_b, out_a, gsum, grid, cols, pt, acc, *, chunks
):
    core, mine = meta[0], meta[1]

    @pl.when(core == 0)
    def _():
        build(grid, 0, pos, a, xl, xr, yl, yr)

    @pl.when(core != 0)
    def _():
        build(grid, 0, pos, b, *(e.at[1:2] for e in (xl, xr, yl, yr)))

    faces, at = [], P_ROWS
    for rows in FACES:
        faces.append(msg.at[pl.ds(at, rows)].reshape(1, rows, C))
        at += rows
    build(grid.at[1:2], 0, ppos, other, *faces)
    for k in range(4):
        s = k % 2
        _, bx, by = place(pos if k < 2 else ppos, s)
        rows = slice(k * 512, (k + 1) * 512)
        for j in range(9):
            cols[rows, j * C : (j + 1) * C] = window(grid, k // 2, bx, by, j)
        if k < 2:
            v = jnp.where(core == 0, pre[s], hid[s])
        else:
            v = msg[s * 512 : (s + 1) * 512]
        v = v.astype(f32).reshape(64, 8, C)
        for i, t in enumerate((up_z(v), v, down_z(v))):
            pt[i * C : (i + 1) * C, rows] = t.reshape(512, C).T.astype(bf16)
    y = jnp.dot(pt[...], cols[...], preferred_element_type=f32)
    for j in range(9):
        acc[j * 384 : (j + 1) * 384] = y[:, j * C : (j + 1) * C]
    size = acc.shape[0] // chunks
    quarter = chunks // 4
    for k, dst in enumerate((keep_b, keep_a, out_b, out_a)):
        for p in range(0, quarter, 2):
            at = [pl.multiple_of((mine ^ (k * quarter + p + i)) * size, 8) for i in range(2)]
            two = jnp.concatenate([acc[pl.ds(a, size)] for a in at])
            dst[p * size : (p + 2) * size] = two.astype(dst.dtype)
    tile = msg[1024:P_ROWS].astype(f32)
    total = gain_part[0:1] + ((tile[2:3] + tile[1:2]) + tile[0:1])
    gsum[...] = jnp.broadcast_to(total, (8, C))


def pack3(v):
    hi, mid, low = split3(v)
    row = lax.broadcasted_iota(jnp.int32, (16, C), 0)
    return jnp.where(row == 0, hi, jnp.where(row == 1, mid, jnp.where(row == 2, low, 0.0))).astype(bf16)


def seal_body(low, g, out):
    hi, mid, rest = split3(g[0:1])
    row = lax.broadcasted_iota(jnp.int32, (8, C), 0)
    tile = jnp.where(row == 0, hi, jnp.where(row == 1, mid, jnp.where(row == 2, rest, 0.0)))
    out[...] = jnp.concatenate([low[...], tile]).astype(bf16)


def join_body(a, b, out):
    n = a.shape[0]
    out[0:n] = a[...]
    out[n:] = b[...]


def join(a, b):
    (out,) = call(join_body, [sds((a.shape[0] + b.shape[0], C), bf16)], [], (a, b), 0)
    return out


def final_body(meta, o0, o1, o2, o3, p0, p1, p2, p3, k_out, g_out, first, second, gains, *, chunks):
    own, part = (o0, o1, o2, o3), (p0, p1, p2, p3)
    core, mine, theirs = meta[0], meta[1], meta[2]
    n = TAPS * C
    size = n // chunks
    quarter = chunks // 4

    def spread(dst, srcs, me, gain):
        for p in range(chunks):
            src, q = srcs[p // quarter], p % quarter
            piece = src[q * (size + 8) : (q + 1) * (size + 8)].astype(f32)
            dst[pl.ds(pl.multiple_of((me ^ p) * size, 8), size)] = piece[:size]
            if gain:
                t = piece[size:]
                gains[me ^ p] = jnp.broadcast_to((t[2:3] + t[1:2]) + t[0:1], (8, C))

    @pl.when(core == 0)
    def _():
        spread(first, own, mine, True)
        spread(second, part, theirs, False)

    @pl.when(core != 0)
    def _():
        spread(first, part, theirs, True)
        spread(second, own, mine, False)

    g = jnp.sum(gains[...], axis=0)[0:1]
    total = jnp.sum(g * g)
    for ref in (first, second):
        v = ref[...].reshape(n // 8, 8, C)
        total = total + jnp.sum(jnp.sum(v * v, axis=0))
    entries = 2.0 * n * C + C
    norm = jnp.full((8, C), total / entries + 1e-06, f32)
    shrink = jnp.minimum(1.0, clip_level / jnp.sqrt(norm))[0:1]
    g_out[...] = g * shrink
    for t in range(TAPS):
        k_out[0, t] = first[t * C : (t + 1) * C].T * shrink
        u = TAPS - 1 - t
        k_out[1, t] = second[u * C : (u + 1) * C] * shrink


def shift(lo, hi, axis):
    n = lax.axis_size(axis)
    from_left = lax.ppermute(hi, axis, [(i, i + 1) for i in range(n - 1)])
    from_right = lax.ppermute(lo, axis, [(i + 1, i) for i in range(n - 1)])
    return from_left, from_right


def y_faces(pos, a, b, xl, xr):
    return call(
        pack_y_body,
        [sds((2, 144, C), bf16)] * 2,
        [pltpu.VMEM((18, 8, C), f32)],
        (pos, a, b, xl, xr),
        1,
    )


def stages():
    nx, ny = lax.axis_size("gx"), lax.axis_size("gy")
    xs = [(1 << i, 0) for i in range(nx.bit_length() - 1)]
    zs = [(0, 1 << i) for i in range(1, ny.bit_length() - 1)]
    orders = (xs + zs, xs[1:] + xs[:1] + zs)
    perms = []
    for step in zip(*orders):
        pairs = []
        for i in range(nx):
            for j in range(ny):
                dx, dy = step[j % 2]
                pairs.append((i * ny + j, (i ^ dx) * ny + (j ^ dy)))
        perms.append(pairs)
    return orders, perms


def chunk_index(order, halvings, ix, iy):
    out = 0
    for s, (dx, dy) in enumerate(order[:halvings]):
        bit = ((ix & dx) | (iy & dy)) != 0
        out = out + bit.astype(jnp.int32) * (1 << (halvings - 1 - s))
    return jnp.asarray(out, jnp.int32)


def after(value, *done):
    return lax.optimization_barrier((value, *done))[0]


def per_device(features, brick_pos, cotangent, first_kernel, second_kernel, norm_gain):
    both = ("gx", "gy")
    ny = lax.axis_size("gy")
    ix, iy = lax.axis_index("gx"), lax.axis_index("gy")
    core = iy % 2
    orders, perms = stages()
    halvings = min(len(perms), 4)
    chunks = 1 << halvings
    me_a = chunk_index(orders[0], halvings, ix, iy)
    me_b = chunk_index(orders[1], halvings, ix, iy)
    meta = jnp.stack([core, jnp.where(core == 0, me_a, me_b), jnp.where(core == 0, me_b, me_a)])
    partner = [(i, i ^ 1) for i in range(ny)]
    n = TAPS * C
    size = n // chunks

    hbm = lambda v: pltpu.with_memory_space_constraint(v, pltpu.HBM)
    features, cotangent, sent, lo, hi = call(
        load_body,
        [sds((2, 512, C), bf16)] * 3 + [sds((2, 128, C), bf16)] * 2,
        [],
        (brick_pos, core.reshape(1), hbm(features), hbm(cotangent)),
        2,
    )
    xl, xr = shift(lo, hi, "gx")
    ppos = lax.ppermute(brick_pos, "gy", partner)
    other = lax.ppermute(sent, "gy", partner)
    straight, turned = sds((9 * C, 3 * C), bf16), sds((3 * C, 9 * C), bf16)
    w1, w2, t1, t2, gain = call(
        prep_body,
        [straight, straight, turned, turned, sds((1, C), f32)],
        [],
        (hbm(first_kernel), hbm(second_kernel), hbm(norm_gain.reshape(1, C))),
        0,
    )
    lo, hi = y_faces(brick_pos, after(features, gain), cotangent, xl, xr)
    lo = after(lo, ppos, other, meta)
    edge = xl, xr, *shift(lo, hi, "gy")
    grid = pltpu.VMEM((2, 18, 18, 8, C), f32)
    cols = pltpu.VMEM((512, 9 * C), bf16)
    hid, pre, msg, gain_part = call(
        main_body,
        [sds((2, 512, C), bf16)] * 2 + [sds((P_ROWS + sum(FACES), C), bf16), sds((8, C), f32)],
        [grid, cols, pltpu.VMEM((512, C), f32)],
        (brick_pos, meta, features, cotangent, *edge, w1, t2, gain),
        2,
        14,
    )
    pmsg = lax.ppermute(msg, "gy", partner)
    keep_b, keep_a, out_b, out_a, g = call(
        functools.partial(grads_body, chunks=chunks),
        [sds((n // 4, C), f32)] * 2 + [sds((n // 4, C), bf16)] * 2 + [sds((8, C), f32)],
        [
            grid,
            pltpu.VMEM((2048, 9 * C), bf16),
            pltpu.VMEM((3 * C, 2048), bf16),
            pltpu.VMEM((n, C), f32),
        ],
        (brick_pos, ppos, meta, features, cotangent, *edge, other, hid, pre, pmsg, gain_part),
        3,
        20,
    )
    g = g[0:1]

    lo, hi = call(pack_x_body, [sds((2, 128, C), bf16)] * 2, [], (brick_pos, after(hid, out_a), pre), 1)
    xl, xr = shift(lo, hi, "gx")
    lo, hi = y_faces(brick_pos, hid, pre, xl, xr)
    around = xl, xr, *shift(lo, hi, "gy")
    results = []
    for f, (src, w, base) in enumerate(((hid, w2, features), (pre, t1, cotangent))):
        (res,) = call(
            functools.partial(out_body, field=f),
            [sds((2, 512, C), bf16)],
            [pltpu.VMEM((1, 18, 18, 8, C), f32), cols],
            (brick_pos, src, *around, w, base),
            1,
            10,
        )
        results.append(res)

    swap = lambda v, s: lax.ppermute(v, both, perms[s])
    got_a, got_b = swap(out_a, 0), swap(out_b, 0)
    out = (keep_a + got_a.astype(f32)).astype(bf16)
    got = swap(out, 1)
    low = keep_b + got_b.astype(f32) + got.astype(f32)
    for s in range(2, halvings):
        half = low.shape[0] // 2
        out = low[half:]
        if s + 1 < halvings:
            out = out.astype(bf16)
        got = swap(out, s)
        low = low[:half] + got.astype(f32)
    for s in range(halvings, len(perms)):
        got = swap(jnp.concatenate([low, jnp.broadcast_to(g, (8, C))]), s)
        low, g = low + got[:size], g + got[size : size + 1]

    (full,) = call(seal_body, [sds((size + 8, C), bf16)], [], (low, g), 0)
    for s in reversed(range(2, halvings)):
        got = swap(full, s)
        full = join(full, got)
    own = [full]
    own.append(swap(full, 1))
    own.append(swap(full, 0))
    own.append(swap(own[1], 0))
    part = [lax.ppermute(v, "gy", partner) for v in own]
    k_up, g_up = call(
        functools.partial(final_body, chunks=chunks),
        [sds((2, TAPS, C, C), f32), sds((1, C), f32)],
        [pltpu.VMEM((n, C), f32), pltpu.VMEM((n, C), f32), pltpu.VMEM((chunks, 8, C), f32)],
        (meta, *own, *part),
        1,
        14,
    )
    return (*results, k_up, g_up.reshape(C))


def solution(mesh):
    rows = P(("gx", "gy"), None, None)

    return jax.shard_map(
        per_device,
        mesh=mesh,
        in_specs=(rows, P(("gx", "gy")), rows, P(), P(), P()),
        out_specs=(rows, rows, P(), P()),
        check_vma=False,
    )
```

```python
import functools

import jax
import jax.numpy as jnp
from jax import lax
from jax.experimental import pallas as pl
from jax.experimental.pallas import tpu as pltpu
from jax.sharding import PartitionSpec as P


BY = 2
POS = 4
TAPS = 27
P_ROWS = 1040
FACES = (128, 128, 144, 144)
C = 128
clip_level = 0.5
f32, bf16 = jnp.float32, jnp.bfloat16
VMEM = pl.BlockSpec(memory_space=pltpu.VMEM)
SMEM = pl.BlockSpec(memory_space=pltpu.SMEM)


def sds(shape, dtype):
    return jax.ShapeDtypeStruct(shape, dtype)


def place(pos_ref, slot):
    p = pos_ref[slot]
    q = jnp.minimum(p, POS - 1)
    return p < POS, q // BY, q % BY


def call(body, outs, scratch, args, n_smem, mib=4):
    return pl.pallas_call(
        body,
        out_shape=outs,
        in_specs=[SMEM] * n_smem + [VMEM] * (len(args) - n_smem),
        out_specs=[VMEM] * len(outs),
        scratch_shapes=scratch,
        compiler_params=pltpu.CompilerParams(vmem_limit_bytes=mib << 20),
    )(*args)


def sides(odd, a, b):
    return jnp.where(odd == 0, b, a), jnp.where(odd == 0, a, b)


def pack_x(pos, odd, srcs, outs):
    for f, src in enumerate(srcs):
        for out, d in zip(outs, (1 - odd, odd)):
            out[f] = jnp.zeros(out.shape[1:], bf16)
            at = pl.multiple_of(d * 448, 64)
            for s in range(2):
                live, bx, by = place(pos, s)

                @pl.when(live & (bx == d))
                def _():
                    out[f, pl.ds(pl.multiple_of(by * 64, 64), 64)] = src[s, pl.ds(at, 64)]


def pack_x_body(pos, odd, a, b, *outs):
    pack_x(pos, odd[0], (a, b), outs)


def load_body(pos, core, odd, a, b, a_out, b_out, sent, *outs):
    pack_x(pos, odd[0], (a, b), outs)
    a_out[...] = a[...]
    b_out[...] = b[...]
    sent[...] = jnp.where(core[0] == 0, b[...], a[...])


def pack_y_body(pos, meta, a, b, xa, xb, ya, yb, tmp):
    def edge_rows(v, d):
        v = v.astype(f32)
        return jnp.where(d == 0, v[0:8], v[8:16])

    for f, src in enumerate((a, b)):
        for out, d in ((ya, 1 - meta[0]), (yb, meta[0])):
            tmp[...] = jnp.zeros_like(tmp)
            rows = pl.ds(pl.multiple_of(d * 112, 16), 16)
            xl, xr = sides(meta[3], xa[f, rows], xb[f, rows])
            tmp[0] = edge_rows(xl, d)
            tmp[17] = edge_rows(xr, d)
            for s in range(2):
                live, bx, by = place(pos, s)

                @pl.when(live & (by == d))
                def _():
                    for x in range(8):
                        at = pl.multiple_of(x * 64 + d * 48, 16)
                        tmp[1 + bx * 8 + x] = edge_rows(src[s, pl.ds(at, 16)], d)

            out[f] = tmp[...].reshape(144, C).astype(bf16)


def build(grid, f, pos, src, xl, xr, yl, yr):
    grid[f] = jnp.zeros(grid.shape[1:], f32)
    for s in range(2):
        live, bx, by = place(pos, s)

        @pl.when(live)
        def _():
            grid[f, pl.ds(1 + bx * 8, 8), pl.ds(1 + by * 8, 8)] = (
                src[s].astype(f32).reshape(8, 8, 8, C)
            )

    grid[f, 0, 1:17] = xl.astype(f32).reshape(16, 8, C)
    grid[f, 17, 1:17] = xr.astype(f32).reshape(16, 8, C)
    grid[f, :, 0] = yl.astype(f32).reshape(18, 8, C)
    grid[f, :, 17] = yr.astype(f32).reshape(18, 8, C)


def faces(meta, f, xa, xb, ya, yb):
    return *sides(meta[3], xa[f], xb[f]), *sides(meta[0], ya[f], yb[f])


def window(grid, f, bx, by, j):
    sx, sy = j // 3, j % 3
    w = grid[f, pl.ds(bx * 8 + sx, 8), pl.ds(by * 8 + sy, 8)]
    return w.reshape(512, C).astype(bf16)


def up_z(v):
    z = lax.broadcasted_iota(jnp.int32, v.shape, 1)
    return jnp.where(z == 7, 0.0, pltpu.roll(v, 7, 1))


def down_z(v):
    z = lax.broadcasted_iota(jnp.int32, v.shape, 1)
    return jnp.where(z == 0, 0.0, pltpu.roll(v, 1, 1))


def prep_body(k1, k2, gain, w1, w2, t1, t2, gain_out):
    for k, w, t in ((k1, w1, t1), (k2, w2, t2)):
        for j in range(9):
            for oz in range(3):
                w[j * C : (j + 1) * C, oz * C : (oz + 1) * C] = k[3 * j + oz]
                t[oz * C : (oz + 1) * C, j * C : (j + 1) * C] = k[3 * (8 - j) + oz]
    gain_out[...] = gain[...]


def convolve(grid, f, bx, by, cols, w, flipped):
    for j in range(9):
        cols[:, j * C : (j + 1) * C] = window(grid, f, bx, by, j)
    dims = (((1,), (1,)), ((), ())) if flipped else (((1,), (0,)), ((), ()))
    y = lax.dot_general(cols[...], w[...], dims, preferred_element_type=f32)
    lower, mid, upper = (y[:, i * C : (i + 1) * C].reshape(64, 8, C) for i in range(3))
    if flipped:
        out = mid + up_z(lower) + down_z(upper)
    else:
        out = mid + down_z(lower) + up_z(upper)
    return out.reshape(512, C)


def split3(v):
    hi = v.astype(bf16).astype(f32)
    rest = v - hi
    mid = rest.astype(bf16).astype(f32)
    return hi, mid, rest - mid


def main_body(
    pos, meta, a, b, xa, xb, ya, yb, w1, w2, gain,
    hid, pre, msg, gain_part, grid, cols, hg
):
    core = meta[0]
    for f, src in enumerate((a, b)):
        build(grid, f, pos, src, *faces(meta, f, xa, xb, ya, yb))
    at = P_ROWS
    for face in faces(meta, 1 - core, xa, xb, ya, yb):
        msg[at : at + face.shape[0]] = face
        at += face.shape[0]
    g = gain[...]
    total = jnp.zeros((1, C), f32)
    for s in range(2):
        live, bx, by = place(pos, s)
        hg[...] = convolve(grid, 1, bx, by, cols, w2, True)
        first = convolve(grid, 0, bx, by, cols, w1, False)
        center = first - jnp.mean(first, axis=1, keepdims=True)
        spread = jnp.mean(center * center, axis=1, keepdims=True)
        inv = lax.rsqrt(spread + 1e-05)
        n = center * inv
        v = n * g
        sig = jax.nn.sigmoid(v)
        on = jnp.where(live, 1.0, 0.0)
        h = jnp.where(live, v * sig, 0.0).astype(bf16)
        grad = jnp.where(live, hg[...], 0.0)
        dv = grad * (sig * (1.0 + v * (1.0 - sig)))
        total = total + jnp.sum(dv * n, axis=0, keepdims=True)
        dn = dv * g
        m1 = jnp.mean(dn, axis=1, keepdims=True)
        m2 = jnp.mean(dn * n, axis=1, keepdims=True)
        p = (inv * (dn - m1 - n * m2)).astype(bf16)
        hid[s] = h
        pre[s] = p
        msg[s * 512 : (s + 1) * 512] = jnp.where(core == 0, h, p)
    gain_part[...] = jnp.broadcast_to(total, (8, C))
    msg[1024:P_ROWS] = pack3(total)


def out_body(pos, meta, src, xa, xb, ya, yb, w, base, out, grid, cols, *, field):
    build(grid, 0, pos, src, *faces(meta, field, xa, xb, ya, yb))
    for s in range(2):
        live, bx, by = place(pos, s)
        y = convolve(grid, 0, bx, by, cols, w, field == 1)
        out[s] = jnp.where(live, base[s].astype(f32) + y, 0.0).astype(bf16)


def grads_body(
    pos, ppos, meta, a, b, xa, xb, ya, yb, other, hid, pre, msg, gain_part,
    keep_b, keep_a, out_b, out_a, gsum, grid, cols, pt, acc, *, chunks
):
    core, mine = meta[0], meta[1]

    for f, src in enumerate((a, b)):

        @pl.when(core == f)
        def _():
            build(grid, 0, pos, src, *faces(meta, f, xa, xb, ya, yb))

    theirs, at = [], P_ROWS
    for rows in FACES:
        theirs.append(msg[at : at + rows])
        at += rows
    build(grid, 1, ppos, other, *theirs)
    for k in range(4):
        s = k % 2
        _, bx, by = place(pos if k < 2 else ppos, s)
        rows = slice(k * 512, (k + 1) * 512)
        for j in range(9):
            cols[rows, j * C : (j + 1) * C] = window(grid, k // 2, bx, by, j)
        if k < 2:
            v = jnp.where(core == 0, pre[s], hid[s])
        else:
            v = msg[s * 512 : (s + 1) * 512]
        v = v.astype(f32).reshape(64, 8, C)
        for i, t in enumerate((up_z(v), v, down_z(v))):
            pt[i * C : (i + 1) * C, rows] = t.reshape(512, C).T.astype(bf16)
    y = jnp.dot(pt[...], cols[...], preferred_element_type=f32)
    for j in range(9):
        acc[j * 384 : (j + 1) * 384] = y[:, j * C : (j + 1) * C]
    size = acc.shape[0] // chunks
    quarter = chunks // 4
    for k, dst in enumerate((keep_b, keep_a, out_b, out_a)):
        for p in range(0, quarter, 2):
            at = [pl.multiple_of((mine ^ (k * quarter + p + i)) * size, 8) for i in range(2)]
            two = jnp.concatenate([acc[pl.ds(a, size)] for a in at])
            dst[p * size : (p + 2) * size] = two.astype(dst.dtype)
    tile = msg[1024:P_ROWS].astype(f32)
    total = gain_part[0:1] + ((tile[2:3] + tile[1:2]) + tile[0:1])
    gsum[...] = jnp.broadcast_to(total, (8, C))


def pack3(v):
    hi, mid, low = split3(v)
    row = lax.broadcasted_iota(jnp.int32, (16, C), 0)
    return jnp.where(row == 0, hi, jnp.where(row == 1, mid, jnp.where(row == 2, low, 0.0))).astype(bf16)


def seal_body(low, g, out):
    hi, mid, rest = split3(g[0:1])
    row = lax.broadcasted_iota(jnp.int32, (8, C), 0)
    tile = jnp.where(row == 0, hi, jnp.where(row == 1, mid, jnp.where(row == 2, rest, 0.0)))
    out[...] = jnp.concatenate([low[...], tile]).astype(bf16)


def join_body(*refs):
    out, at = refs[-1], 0
    for ref in refs[:-1]:
        out[at : at + ref.shape[0]] = ref[...]
        at += ref.shape[0]


def join(*parts):
    rows = sum(p.shape[0] for p in parts)
    (out,) = call(join_body, [sds((rows, C), bf16)], [], parts, 0)
    return out


def final_body(meta, o0, o1, o2, o3, p0, p1, p2, p3, k_out, g_out, first, second, gains, *, chunks):
    own, part = (o0, o1, o2, o3), (p0, p1, p2, p3)
    core, mine, theirs = meta[0], meta[1], meta[2]
    n = TAPS * C
    size = n // chunks
    quarter = chunks // 4

    def spread(dst, srcs, me, gain):
        for p in range(chunks):
            src, q = srcs[p // quarter], p % quarter
            piece = src[q * (size + 8) : (q + 1) * (size + 8)].astype(f32)
            dst[pl.ds(pl.multiple_of((me ^ p) * size, 8), size)] = piece[:size]
            if gain:
                t = piece[size:]
                gains[me ^ p] = jnp.broadcast_to((t[2:3] + t[1:2]) + t[0:1], (8, C))

    @pl.when(core == 0)
    def _():
        spread(first, own, mine, True)
        spread(second, part, theirs, False)

    @pl.when(core != 0)
    def _():
        spread(first, part, theirs, True)
        spread(second, own, mine, False)

    g = jnp.sum(gains[...], axis=0)[0:1]
    total = jnp.sum(g * g)
    for ref in (first, second):
        v = ref[...].reshape(n // 8, 8, C)
        total = total + jnp.sum(jnp.sum(v * v, axis=0))
    entries = 2.0 * n * C + C
    norm = jnp.full((8, C), total / entries + 1e-06, f32)
    shrink = jnp.minimum(1.0, clip_level / jnp.sqrt(norm))[0:1]
    g_out[...] = g * shrink
    for t in range(TAPS):
        k_out[0, t] = first[t * C : (t + 1) * C].T * shrink
        u = TAPS - 1 - t
        k_out[1, t] = second[u * C : (u + 1) * C] * shrink


def across(a, b, axis):
    n = lax.axis_size(axis)
    even, odd = (
        [p for i in range(first, n - 1, 2) for p in ((i, i + 1), (i + 1, i))] for first in (0, 1)
    )
    return lax.ppermute(a, axis, even), lax.ppermute(b, axis, odd)


def y_faces(pos, meta, a, b, xa, xb):
    return call(
        pack_y_body,
        [sds((2, 144, C), bf16)] * 2,
        [pltpu.VMEM((18, 8, C), f32)],
        (pos, meta, a, b, xa, xb),
        2,
    )


def plan():
    nx, ny = lax.axis_size("gx"), lax.axis_size("gy")
    xs = [(1 << i, 0) for i in range(nx.bit_length() - 1)]
    zs = [(0, 1 << i) for i in range(1, ny.bit_length() - 1)]
    k = min(len(zs), 4 - len(xs))
    orders = (xs + zs[:k], xs[1:] + xs[:1] + zs[:k])
    group = []
    for m in range(1, 1 << k):
        group.append(sum(zs[i][1] for i in range(k) if m >> (k - 1 - i) & 1))
    return orders, len(xs), group, [z for _, z in zs[k:]]


def pairs(dx, dy):
    nx, ny = lax.axis_size("gx"), lax.axis_size("gy")
    return [(i * ny + j, (i ^ dx[j % 2]) * ny + (j ^ dy)) for i in range(nx) for j in range(ny)]


def chunk_index(order, halvings, ix, iy):
    out = 0
    for s, (dx, dy) in enumerate(order[:halvings]):
        bit = ((ix & dx) | (iy & dy)) != 0
        out = out + bit.astype(jnp.int32) * (1 << (halvings - 1 - s))
    return jnp.asarray(out, jnp.int32)


def after(value, *done):
    return lax.optimization_barrier((value, *done))[0]


def per_device(features, brick_pos, cotangent, first_kernel, second_kernel, norm_gain):
    both = ("gx", "gy")
    ny = lax.axis_size("gy")
    ix, iy = lax.axis_index("gx"), lax.axis_index("gy")
    core = iy % 2
    orders, halvings, group, copies = plan()
    chunks = 1 << len(orders[0])
    me_a = chunk_index(orders[0], len(orders[0]), ix, iy)
    me_b = chunk_index(orders[1], len(orders[1]), ix, iy)
    meta = jnp.stack([core, jnp.where(core == 0, me_a, me_b), jnp.where(core == 0, me_b, me_a), ix % 2])
    partner = [(i, i ^ 1) for i in range(ny)]
    n = TAPS * C
    size = n // chunks

    hbm = lambda v: pltpu.with_memory_space_constraint(v, pltpu.HBM)
    features, cotangent, sent, fa, fb = call(
        load_body,
        [sds((2, 512, C), bf16)] * 3 + [sds((2, 128, C), bf16)] * 2,
        [],
        (brick_pos, core.reshape(1), (ix % 2).reshape(1), hbm(features), hbm(cotangent)),
        3,
    )
    xa, xb = across(fa, fb, "gx")
    ppos = lax.ppermute(brick_pos, "gy", partner)
    other = lax.ppermute(sent, "gy", partner)
    straight, turned = sds((9 * C, 3 * C), bf16), sds((3 * C, 9 * C), bf16)
    w1, w2, t1, t2, gain = call(
        prep_body,
        [straight, straight, turned, turned, sds((1, C), f32)],
        [],
        (hbm(first_kernel), hbm(second_kernel), hbm(norm_gain.reshape(1, C))),
        0,
    )
    fa, fb = y_faces(brick_pos, meta, after(features, gain), cotangent, xa, xb)
    fa = after(fa, ppos, other)
    edge = xa, xb, *across(fa, fb, "gy")
    grid = pltpu.VMEM((2, 18, 18, 8, C), f32)
    cols = pltpu.VMEM((512, 9 * C), bf16)
    hid, pre, msg, gain_part = call(
        main_body,
        [sds((2, 512, C), bf16)] * 2 + [sds((P_ROWS + sum(FACES), C), bf16), sds((8, C), f32)],
        [grid, cols, pltpu.VMEM((512, C), f32)],
        (brick_pos, meta, features, cotangent, *edge, w1, t2, gain),
        2,
        14,
    )
    pmsg = lax.ppermute(msg, "gy", partner)
    keep_b, keep_a, out_b, out_a, g = call(
        functools.partial(grads_body, chunks=chunks),
        [sds((n // 4, C), f32)] * 2 + [sds((n // 4, C), bf16)] * 2 + [sds((8, C), f32)],
        [
            grid,
            pltpu.VMEM((2048, 9 * C), bf16),
            pltpu.VMEM((3 * C, 2048), bf16),
            pltpu.VMEM((n, C), f32),
        ],
        (brick_pos, ppos, meta, features, cotangent, *edge, other, hid, pre, pmsg, gain_part),
        3,
        20,
    )
    g = g[0:1]

    fa, fb = call(
        pack_x_body,
        [sds((2, 128, C), bf16)] * 2,
        [],
        (brick_pos, (ix % 2).reshape(1), after(hid, out_a), pre),
        2,
    )
    xa, xb = across(fa, fb, "gx")
    fa, fb = y_faces(brick_pos, meta, hid, pre, xa, xb)
    around = xa, xb, *across(fa, fb, "gy")
    results = []
    for f, (src, w, base) in enumerate(((hid, w2, features), (pre, t1, cotangent))):
        (res,) = call(
            functools.partial(out_body, field=f),
            [sds((2, 512, C), bf16)],
            [pltpu.VMEM((1, 18, 18, 8, C), f32), cols],
            (brick_pos, meta, src, *around, w, base),
            2,
            10,
        )
        results.append(res)

    swap = lambda v, dx, dy=0: lax.ppermute(v, both, pairs(dx, dy))
    steps = [(a[0], b[0]) for a, b in zip(*orders)][:halvings]
    got_a, got_b = swap(out_a, steps[0]), swap(out_b, steps[0])
    out = (keep_a + got_a.astype(f32)).astype(bf16)
    got = swap(out, steps[1])
    low = keep_b + got_b.astype(f32) + got.astype(f32)
    for step in steps[2:]:
        half = low.shape[0] // 2
        got = swap(low[half:].astype(bf16), step)
        low = low[:half] + got.astype(f32)
    got = []
    for m, dy in enumerate(group, 1):
        out = low[m * size : (m + 1) * size]
        got.append(swap(out if dy == 2 else out.astype(bf16), (0, 0), dy))
    low = low[:size]
    for v in got:
        low = low + v.astype(f32)
    for dy in copies:
        got = swap(jnp.concatenate([low, jnp.broadcast_to(g, (8, C))]), (0, 0), dy)
        low, g = low + got[:size], g + got[size : size + 1]

    (full,) = call(seal_body, [sds((size + 8, C), bf16)], [], (low, g), 0)
    full = join(full, *(swap(full, (0, 0), dy) for dy in group))
    for step in reversed(steps[2:]):
        full = join(full, swap(full, step))
    own = [full]
    own.append(swap(full, steps[1]))
    own.append(swap(full, steps[0]))
    own.append(swap(own[1], steps[0]))
    part = [lax.ppermute(v, "gy", partner) for v in own]
    k_up, g_up = call(
        functools.partial(final_body, chunks=chunks),
        [sds((2, TAPS, C, C), f32), sds((1, C), f32)],
        [pltpu.VMEM((n, C), f32), pltpu.VMEM((n, C), f32), pltpu.VMEM((chunks, 8, C), f32)],
        (meta, *own, *part),
        1,
        14,
    )
    return (*results, k_up, g_up.reshape(C))


def solution(mesh):
    rows = P(("gx", "gy"), None, None)

    return jax.shard_map(
        per_device,
        mesh=mesh,
        in_specs=(rows, P(("gx", "gy")), rows, P(), P(), P()),
        out_specs=(rows, rows, P(), P()),
        check_vma=False,
    )
```

```python
import functools

import jax
import jax.numpy as jnp
from jax import lax
from jax.experimental import pallas as pl
from jax.experimental.pallas import tpu as pltpu
from jax.sharding import PartitionSpec as P


BY = 2
POS = 4
TAPS = 27
P_ROWS = 1040
FACES = (128, 128, 144, 144)
C = 128
clip_level = 0.5
f32, bf16 = jnp.float32, jnp.bfloat16
VMEM = pl.BlockSpec(memory_space=pltpu.VMEM)
SMEM = pl.BlockSpec(memory_space=pltpu.SMEM)


def sds(shape, dtype):
    return jax.ShapeDtypeStruct(shape, dtype)


def place(pos_ref, slot):
    p = pos_ref[slot]
    q = jnp.minimum(p, POS - 1)
    return p < POS, q // BY, q % BY


def call(body, outs, scratch, args, n_smem, mib=4):
    return pl.pallas_call(
        body,
        out_shape=outs,
        in_specs=[SMEM] * n_smem + [VMEM] * (len(args) - n_smem),
        out_specs=[VMEM] * len(outs),
        scratch_shapes=scratch,
        compiler_params=pltpu.CompilerParams(vmem_limit_bytes=mib << 20),
    )(*args)


def sides(odd, a, b):
    return jnp.where(odd == 0, b, a), jnp.where(odd == 0, a, b)


def pack_x(pos, odd, srcs, outs):
    for f, src in enumerate(srcs):
        for out, d in zip(outs, (1 - odd, odd)):
            out[f] = jnp.zeros(out.shape[1:], bf16)
            at = pl.multiple_of(d * 448, 64)
            for s in range(2):
                live, bx, by = place(pos, s)

                @pl.when(live & (bx == d))
                def _():
                    out[f, pl.ds(pl.multiple_of(by * 64, 64), 64)] = src[s, pl.ds(at, 64)]


def pack_x_body(pos, odd, a, b, *outs):
    pack_x(pos, odd[0], (a, b), outs)


def load_body(pos, core, odd, a, b, a_out, b_out, sent, *outs):
    pack_x(pos, odd[0], (a, b), outs)
    a_out[...] = a[...]
    b_out[...] = b[...]
    sent[...] = jnp.where(core[0] == 0, b[...], a[...])


def pack_y_body(pos, meta, a, b, xa, xb, ya, yb, tmp):
    def edge_rows(v, d):
        v = v.astype(f32)
        return jnp.where(d == 0, v[0:8], v[8:16])

    for f, src in enumerate((a, b)):
        for out, d in ((ya, 1 - meta[0]), (yb, meta[0])):
            tmp[...] = jnp.zeros_like(tmp)
            rows = pl.ds(pl.multiple_of(d * 112, 16), 16)
            xl, xr = sides(meta[3], xa[f, rows], xb[f, rows])
            tmp[0] = edge_rows(xl, d)
            tmp[17] = edge_rows(xr, d)
            for s in range(2):
                live, bx, by = place(pos, s)

                @pl.when(live & (by == d))
                def _():
                    for x in range(8):
                        at = pl.multiple_of(x * 64 + d * 48, 16)
                        tmp[1 + bx * 8 + x] = edge_rows(src[s, pl.ds(at, 16)], d)

            out[f] = tmp[...].reshape(144, C).astype(bf16)


def build(grid, f, pos, src, xl, xr, yl, yr):
    grid = grid.at[f] if isinstance(f, int) else grid
    grid[...] = jnp.zeros(grid.shape, f32)
    for s in range(2):
        live, bx, by = place(pos, s)

        @pl.when(live)
        def _():
            grid[pl.ds(1 + bx * 8, 8), pl.ds(1 + by * 8, 8)] = src[s].astype(f32).reshape(8, 8, 8, C)

    grid[0, 1:17] = xl.astype(f32).reshape(16, 8, C)
    grid[17, 1:17] = xr.astype(f32).reshape(16, 8, C)
    grid[:, 0] = yl.astype(f32).reshape(18, 8, C)
    grid[:, 17] = yr.astype(f32).reshape(18, 8, C)


def faces(meta, f, xa, xb, ya, yb):
    return *sides(meta[3], xa[f], xb[f]), *sides(meta[0], ya[f], yb[f])


def window(grid, f, bx, by, j):
    sx, sy = j // 3, j % 3
    w = grid[f, pl.ds(bx * 8 + sx, 8), pl.ds(by * 8 + sy, 8)]
    return w.reshape(512, C).astype(bf16)


def up_z(v):
    z = lax.broadcasted_iota(jnp.int32, v.shape, 1)
    return jnp.where(z == 7, 0.0, pltpu.roll(v, 7, 1))


def down_z(v):
    z = lax.broadcasted_iota(jnp.int32, v.shape, 1)
    return jnp.where(z == 0, 0.0, pltpu.roll(v, 1, 1))


def prep_body(k1, k2, gain, w1, w2, t1, t2, gain_out):
    for k, w, t in ((k1, w1, t1), (k2, w2, t2)):
        for j in range(9):
            for oz in range(3):
                w[j * C : (j + 1) * C, oz * C : (oz + 1) * C] = k[3 * j + oz]
                t[oz * C : (oz + 1) * C, j * C : (j + 1) * C] = k[3 * (8 - j) + oz]
    gain_out[...] = gain[...]


def convolve(grid, f, bx, by, cols, w, flipped):
    for j in range(9):
        cols[:, j * C : (j + 1) * C] = window(grid, f, bx, by, j)
    dims = (((1,), (1,)), ((), ())) if flipped else (((1,), (0,)), ((), ()))
    y = lax.dot_general(cols[...], w[...], dims, preferred_element_type=f32)
    lower, mid, upper = (y[:, i * C : (i + 1) * C].reshape(64, 8, C) for i in range(3))
    if flipped:
        out = mid + up_z(lower) + down_z(upper)
    else:
        out = mid + down_z(lower) + up_z(upper)
    return out.reshape(512, C)


def split3(v):
    hi = v.astype(bf16).astype(f32)
    rest = v - hi
    mid = rest.astype(bf16).astype(f32)
    return hi, mid, rest - mid


def main_body(
    pos, meta, a, b, xa, xb, ya, yb, w1, w2, gain,
    hid, pre, msg, gain_part, grid, cols, hg
):
    core = meta[0]
    for f, src in enumerate((a, b)):
        build(grid, f, pos, src, *faces(meta, f, xa, xb, ya, yb))
    at = P_ROWS
    for face in faces(meta, 1 - core, xa, xb, ya, yb):
        msg[at : at + face.shape[0]] = face
        at += face.shape[0]
    g = gain[...]
    total = jnp.zeros((1, C), f32)
    for s in range(2):
        live, bx, by = place(pos, s)
        hg[...] = convolve(grid, 1, bx, by, cols, w2, True)
        first = convolve(grid, 0, bx, by, cols, w1, False)
        center = first - jnp.mean(first, axis=1, keepdims=True)
        spread = jnp.mean(center * center, axis=1, keepdims=True)
        inv = lax.rsqrt(spread + 1e-05)
        n = center * inv
        v = n * g
        sig = jax.nn.sigmoid(v)
        on = jnp.where(live, 1.0, 0.0)
        h = jnp.where(live, v * sig, 0.0).astype(bf16)
        grad = jnp.where(live, hg[...], 0.0)
        dv = grad * (sig * (1.0 + v * (1.0 - sig)))
        total = total + jnp.sum(dv * n, axis=0, keepdims=True)
        dn = dv * g
        m1 = jnp.mean(dn, axis=1, keepdims=True)
        m2 = jnp.mean(dn * n, axis=1, keepdims=True)
        p = (inv * (dn - m1 - n * m2)).astype(bf16)
        hid[s] = h
        pre[s] = p
        msg[s * 512 : (s + 1) * 512] = jnp.where(core == 0, h, p)
    gain_part[...] = jnp.broadcast_to(total, (8, C))
    msg[1024:P_ROWS] = pack3(total)


def out_body(pos, meta, src, xa, xb, ya, yb, w, base, out, grid, cols, *, field):
    build(grid, 0, pos, src, *faces(meta, field, xa, xb, ya, yb))
    for s in range(2):
        live, bx, by = place(pos, s)
        y = convolve(grid, 0, bx, by, cols, w, field == 1)
        out[s] = jnp.where(live, base[s].astype(f32) + y, 0.0).astype(bf16)


JS = 5


def shifted(pt, slot, v):
    v = v.astype(f32).reshape(64, 8, C)
    for i, t in enumerate((up_z(v), v, down_z(v))):
        pt[i * C : (i + 1) * C, slot * 512 : (slot + 1) * 512] = t.reshape(512, C).T.astype(bf16)


def product(grid, pos, pt, upper, cols):
    for s in range(2):
        _, bx, by = place(pos, s)
        for i in range(JS):
            sx = jnp.where(upper, (i + 9 - JS) // 3, i // 3)
            sy = jnp.where(upper, (i + 9 - JS) % 3, i % 3)
            w = grid[pl.ds(bx * 8 + sx, 8), pl.ds(by * 8 + sy, 8)]
            cols[s * 512 : (s + 1) * 512, i * C : (i + 1) * C] = w.reshape(512, C).astype(bf16)
    return jnp.dot(pt[...], cols[...], preferred_element_type=f32)


def pieces(y, acc, dsts, mine, upper, first, chunks):
    for i in range(JS):
        acc[i * 3 * C : (i + 1) * 3 * C] = y[:, i * C : (i + 1) * C]
    size = TAPS * C // chunks
    skip = jnp.where(upper, (9 - JS) * 3 * C, 0)
    p = first
    for dst in dsts:
        for q in range(0, dst.shape[0] // size, 2):
            starts = [pl.multiple_of((mine ^ (p + i)) * size - skip, 8) for i in range(2)]
            two = jnp.concatenate([acc[pl.ds(a, size)] for a in starts])
            dst[q * size : (q + 2) * size] = two.astype(dst.dtype)
            p += 2


def sends_upper(mine, chunks):
    return mine < chunks // 2


def own_body(pos, meta, a, b, xa, xb, ya, yb, hid, pre, grid, pt, part, cols, *, chunks):
    core = meta[0]
    for f, src in enumerate((a, b)):

        @pl.when(core == f)
        def _():
            build(grid, None, pos, src, *faces(meta, f, xa, xb, ya, yb))

    for s in range(2):
        shifted(pt, s, jnp.where(core == 0, pre[s], hid[s]))
    part[...] = product(grid, pos, pt, sends_upper(meta[1], chunks), cols)


def send_body(
    ppos, meta, other, msg, gain_part, part, grid, pt, out_b, out_a, gsum, cols, acc, *, chunks
):
    theirs, at = [], P_ROWS
    for rows in FACES:
        theirs.append(msg[at : at + rows])
        at += rows
    build(grid, None, ppos, other, *theirs)
    for s in range(2):
        shifted(pt, s, msg[s * 512 : (s + 1) * 512])
    upper = sends_upper(meta[1], chunks)
    y = part[...] + product(grid, ppos, pt, upper, cols)
    pieces(y, acc, (out_b, out_a), meta[1], upper, chunks // 2, chunks)
    tile = msg[1024:P_ROWS].astype(f32)
    total = gain_part[0:1] + ((tile[2:3] + tile[1:2]) + tile[0:1])
    gsum[...] = jnp.broadcast_to(total, (8, C))


def keep_body(pos, ppos, meta, grid_a, grid_b, pt_a, pt_b, keep_b, keep_a, cols_a, cols_b, acc, *, chunks):
    upper = jnp.logical_not(sends_upper(meta[1], chunks))
    y = product(grid_a, pos, pt_a, upper, cols_a) + product(grid_b, ppos, pt_b, upper, cols_b)
    pieces(y, acc, (keep_b, keep_a), meta[1], upper, 0, chunks)


def pack3(v):
    hi, mid, low = split3(v)
    row = lax.broadcasted_iota(jnp.int32, (16, C), 0)
    return jnp.where(row == 0, hi, jnp.where(row == 1, mid, jnp.where(row == 2, low, 0.0))).astype(bf16)


def seal_body(low, g, out):
    hi, mid, rest = split3(g[0:1])
    row = lax.broadcasted_iota(jnp.int32, (8, C), 0)
    tile = jnp.where(row == 0, hi, jnp.where(row == 1, mid, jnp.where(row == 2, rest, 0.0)))
    out[...] = jnp.concatenate([low[...], tile]).astype(bf16)


def join_body(*refs):
    out, at = refs[-1], 0
    for ref in refs[:-1]:
        out[at : at + ref.shape[0]] = ref[...]
        at += ref.shape[0]


def join(*parts):
    rows = sum(p.shape[0] for p in parts)
    (out,) = call(join_body, [sds((rows, C), bf16)], [], parts, 0)
    return out


def collect(core, sources, mine, theirs, joined, squares, gains, first_piece, chunks):
    size = TAPS * C // chunks
    for own in (0, 1):

        @pl.when(core == own)
        def _():
            for k in (0, 1):
                srcs, me = (sources[0], mine) if k == own else (sources[1], theirs)
                p = first_piece
                for src in srcs:
                    joined[k][p * (size + 8) : p * (size + 8) + src.shape[0]] = src[...]
                    for q in range(src.shape[0] // (size + 8)):
                        v = src[q * (size + 8) : (q + 1) * (size + 8)].astype(f32)
                        cube = v[:size].reshape(size // 8, 8, C)
                        squares[k, me ^ p] = jnp.sum(cube * cube, axis=0)
                        if k == 0:
                            t = v[size:]
                            gains[me ^ p] = jnp.broadcast_to((t[2:3] + t[1:2]) + t[0:1], (8, C))
                        p += 1


def gathered_body(meta, o0, o1, o2, p0, p1, p2, first, second, squares, gains, *, chunks):
    collect(
        meta[0], ((o0, o1, o2), (p0, p1, p2)), meta[1], meta[2], (first, second), squares, gains, 0, chunks
    )


def final_body(
    meta, o3, p3, first_in, second_in, squares_in, gains_in,
    k_out, g_out, first, second, squares, gains, stage, sems, *, chunks
):
    core, mine, theirs = meta[0], meta[1], meta[2]
    n = TAPS * C
    size = n // chunks
    collect(
        core, ((o3,), (p3,)), mine, theirs, (first, second), squares, gains, chunks // 4 * 3, chunks
    )
    g = jnp.sum(gains[...], axis=0)[0:1]
    total = jnp.sum(g * g) + jnp.sum(jnp.sum(squares[...].reshape(2 * chunks, 8, C), axis=0))
    entries = 2.0 * n * C + C
    norm = jnp.full((8, C), total / entries + 1e-06, f32)
    shrink = jnp.minimum(1.0, clip_level / jnp.sqrt(norm))[0:1]
    g_out[...] = g * shrink

    def tap(joined, me, t):
        parts, row = [], t * C
        while row < (t + 1) * C:
            chunk, at = row // size, row % size
            rows = min(size - at, (t + 1) * C - row)
            start = pl.multiple_of((me ^ chunk) * (size + 8) + at, 8)
            parts.append(joined[pl.ds(start, rows)].astype(f32))
            row += rows
        return jnp.concatenate(parts) if len(parts) > 1 else parts[0]

    copies = []
    for k, joined in ((1, second), (0, first)):
        me = jnp.where(core == k, mine, theirs)
        for part in range(3):
            for t in range(part * 9, part * 9 + 9):
                v = tap(joined, me, t if k == 0 else TAPS - 1 - t)
                stage[k, t] = (v.T if k == 0 else v) * shrink
            block = (k, pl.ds(part * 9, 9))
            copies.append(
                pltpu.make_async_copy(stage.at[block], k_out.at[block], sems.at[len(copies)])
            )
            copies[-1].start()
    for copy in copies:
        copy.wait()


def across(a, b, axis):
    n = lax.axis_size(axis)
    even, odd = (
        [p for i in range(first, n - 1, 2) for p in ((i, i + 1), (i + 1, i))] for first in (0, 1)
    )
    b = lax.ppermute(b, axis, odd)
    a = lax.ppermute(a, axis, even)
    return a, b


def y_faces(pos, meta, a, b, xa, xb):
    return call(
        pack_y_body,
        [sds((2, 144, C), bf16)] * 2,
        [pltpu.VMEM((18, 8, C), f32)],
        (pos, meta, a, b, xa, xb),
        2,
    )


def plan():
    nx, ny = lax.axis_size("gx"), lax.axis_size("gy")
    xs = [(1 << i, 0) for i in range(nx.bit_length() - 1)]
    zs = [(0, 1 << i) for i in range(1, ny.bit_length() - 1)]
    k = min(len(zs), 4 - len(xs))
    orders = (xs + zs[:k], xs[1:] + xs[:1] + zs[:k])
    group = []
    for m in range(1, 1 << k):
        group.append(sum(zs[i][1] for i in range(k) if m >> (k - 1 - i) & 1))
    return orders, len(xs), group, [z for _, z in zs[k:]]


def pairs(dx, dy):
    nx, ny = lax.axis_size("gx"), lax.axis_size("gy")
    return [(i * ny + j, (i ^ dx[j % 2]) * ny + (j ^ dy)) for i in range(nx) for j in range(ny)]


def chunk_index(order, halvings, ix, iy):
    out = 0
    for s, (dx, dy) in enumerate(order[:halvings]):
        bit = ((ix & dx) | (iy & dy)) != 0
        out = out + bit.astype(jnp.int32) * (1 << (halvings - 1 - s))
    return jnp.asarray(out, jnp.int32)


def after(value, *done):
    return lax.optimization_barrier((value, *done))[0]


def per_device(features, brick_pos, cotangent, first_kernel, second_kernel, norm_gain):
    both = ("gx", "gy")
    ny = lax.axis_size("gy")
    ix, iy = lax.axis_index("gx"), lax.axis_index("gy")
    core = iy % 2
    orders, halvings, group, copies = plan()
    chunks = 1 << len(orders[0])
    me_a = chunk_index(orders[0], len(orders[0]), ix, iy)
    me_b = chunk_index(orders[1], len(orders[1]), ix, iy)
    meta = jnp.stack([core, jnp.where(core == 0, me_a, me_b), jnp.where(core == 0, me_b, me_a), ix % 2])
    partner = [(i, i ^ 1) for i in range(ny)]
    n = TAPS * C
    size = n // chunks

    hbm = lambda v: pltpu.with_memory_space_constraint(v, pltpu.HBM)
    features, cotangent, sent, fa, fb = call(
        load_body,
        [sds((2, 512, C), bf16)] * 3 + [sds((2, 128, C), bf16)] * 2,
        [],
        (brick_pos, core.reshape(1), (ix % 2).reshape(1), hbm(features), hbm(cotangent)),
        3,
    )
    xa, xb = across(fa, fb, "gx")
    ppos = lax.ppermute(brick_pos, "gy", partner)
    other = lax.ppermute(sent, "gy", partner)
    straight, turned = sds((9 * C, 3 * C), bf16), sds((3 * C, 9 * C), bf16)
    w1, w2, t1, t2, gain = call(
        prep_body,
        [straight, straight, turned, turned, sds((1, C), f32)],
        [],
        (hbm(first_kernel), hbm(second_kernel), hbm(norm_gain.reshape(1, C))),
        0,
    )
    fa, fb = y_faces(brick_pos, meta, after(features, gain), cotangent, xa, xb)
    fa = after(fa, ppos, other)
    edge = xa, xb, *across(fa, fb, "gy")
    grid = pltpu.VMEM((2, 18, 18, 8, C), f32)
    cols = pltpu.VMEM((512, 9 * C), bf16)
    hid, pre, msg, gain_part = call(
        main_body,
        [sds((2, 512, C), bf16)] * 2 + [sds((P_ROWS + sum(FACES), C), bf16), sds((8, C), f32)],
        [grid, cols, pltpu.VMEM((512, C), f32)],
        (brick_pos, meta, features, cotangent, *edge, w1, t2, gain),
        2,
        14,
    )
    pmsg = lax.ppermute(msg, "gy", partner)
    held = [sds((18, 18, 8, C), f32), sds((3 * C, 1024), bf16)]
    wide = pltpu.VMEM((1024, JS * C), bf16)
    acc = pltpu.VMEM((JS * 3 * C, C), f32)
    grid_a, pt_a, part = call(
        functools.partial(own_body, chunks=chunks),
        held + [sds((3 * C, JS * C), f32)],
        [wide],
        (brick_pos, meta, features, cotangent, *edge, hid, pre),
        2,
        10,
    )
    quarter = [sds((n // 4, C), bf16)] * 2
    grid_b, pt_b, out_b, out_a, g = call(
        functools.partial(send_body, chunks=chunks),
        held + quarter + [sds((8, C), f32)],
        [wide, acc],
        (ppos, meta, other, pmsg, gain_part, part),
        2,
        10,
    )
    keep_b, keep_a = call(
        functools.partial(keep_body, chunks=chunks),
        [sds((n // 4, C), f32)] * 2,
        [wide, wide, acc],
        (brick_pos, ppos, meta, grid_a, grid_b, pt_a, pt_b),
        3,
        12,
    )
    g = g[0:1]

    fa, fb = call(
        pack_x_body,
        [sds((2, 128, C), bf16)] * 2,
        [],
        (brick_pos, (ix % 2).reshape(1), after(hid, out_a), pre),
        2,
    )
    xa, xb = across(fa, fb, "gx")
    fa, fb = y_faces(brick_pos, meta, hid, pre, xa, xb)
    around = xa, xb, *across(fa, fb, "gy")
    results = []
    for f, (src, w, base) in enumerate(((hid, w2, features), (pre, t1, cotangent))):
        (res,) = call(
            functools.partial(out_body, field=f),
            [sds((2, 512, C), bf16)],
            [pltpu.VMEM((1, 18, 18, 8, C), f32), cols],
            (brick_pos, meta, src, *around, w, base),
            2,
            10,
        )
        results.append(res)

    swap = lambda v, dx, dy=0: lax.ppermute(v, both, pairs(dx, dy))
    steps = [(a[0], b[0]) for a, b in zip(*orders)][:halvings]
    got_a = swap(out_a, steps[0])
    got_b = swap(out_b, steps[0])
    out = (keep_a + got_a.astype(f32)).astype(bf16)
    got = swap(out, steps[1])
    low = keep_b + got_b.astype(f32) + got.astype(f32)
    for step in steps[2:]:
        half = low.shape[0] // 2
        got = swap(low[half:].astype(bf16), step)
        low = low[:half] + got.astype(f32)
    got = []
    for m, dy in enumerate(group, 1):
        out = low[m * size : (m + 1) * size]
        got.append(swap(out if dy == 2 else out.astype(bf16), (0, 0), dy))
    low = low[:size]
    for v in got:
        low = low + v.astype(f32)
    for dy in copies:
        got = swap(jnp.concatenate([low, jnp.broadcast_to(g, (8, C))]), (0, 0), dy)
        low, g = low + got[:size], g + got[size : size + 1]

    (full,) = call(seal_body, [sds((size + 8, C), bf16)], [], (low, g), 0)
    full = join(full, *(swap(full, (0, 0), dy) for dy in group))
    for step in reversed(steps[2:]):
        full = join(full, swap(full, step))
    own = [full]
    own.append(swap(full, steps[1]))
    own.append(swap(full, steps[0]))
    own.append(swap(own[1], steps[0]))
    part = [lax.ppermute(v, "gy", partner) for v in own]
    rows = chunks * (size + 8)
    gathered = [
        sds((rows, C), bf16), sds((rows, C), bf16), sds((2, chunks, 8, C), f32), sds((chunks, 8, C), f32)
    ]
    held = call(
        functools.partial(gathered_body, chunks=chunks),
        gathered,
        [],
        (meta, *own[:3], *part[:3]),
        1,
    )
    k_up, g_up = pl.pallas_call(
        functools.partial(final_body, chunks=chunks),
        out_shape=[sds((2, TAPS, C, C), f32), sds((1, C), f32), *gathered],
        in_specs=[SMEM] + [VMEM] * 6,
        out_specs=[pl.BlockSpec(memory_space=pl.ANY)] + [VMEM] * 5,
        scratch_shapes=[pltpu.VMEM((2, TAPS, C, C), f32), pltpu.SemaphoreType.DMA((6,))],
        input_output_aliases={3: 2, 4: 3, 5: 4, 6: 5},
        compiler_params=pltpu.CompilerParams(vmem_limit_bytes=10 << 20),
    )(meta, own[3], part[3], *held)[:2]
    return (*results, k_up, g_up.reshape(C))


def solution(mesh):
    rows = P(("gx", "gy"), None, None)

    return jax.shard_map(
        per_device,
        mesh=mesh,
        in_specs=(rows, P(("gx", "gy")), rows, P(), P(), P()),
        out_specs=(rows, rows, P(), P()),
        check_vma=False,
    )
```

```python
import functools

import jax
import jax.numpy as jnp
from jax import lax
from jax.experimental import pallas as pl
from jax.experimental.pallas import tpu as pltpu
from jax.sharding import PartitionSpec as P


BY = 2
POS = 4
TAPS = 27
P_ROWS = 1040
FACES = (128, 128, 144, 144)
C = 128
clip_level = 0.5
f32, bf16 = jnp.float32, jnp.bfloat16
VMEM = pl.BlockSpec(memory_space=pltpu.VMEM)
SMEM = pl.BlockSpec(memory_space=pltpu.SMEM)


def sds(shape, dtype):
    return jax.ShapeDtypeStruct(shape, dtype)


def place(pos_ref, slot):
    p = pos_ref[slot]
    q = jnp.minimum(p, POS - 1)
    return p < POS, q // BY, q % BY


def call(body, outs, scratch, args, n_smem, mib=4):
    return pl.pallas_call(
        body,
        out_shape=outs,
        in_specs=[SMEM] * n_smem + [VMEM] * (len(args) - n_smem),
        out_specs=[VMEM] * len(outs),
        scratch_shapes=scratch,
        compiler_params=pltpu.CompilerParams(vmem_limit_bytes=mib << 20),
    )(*args)


def sides(odd, a, b):
    return jnp.where(odd == 0, b, a), jnp.where(odd == 0, a, b)


def pack_x(pos, odd, srcs, outs):
    for f, src in enumerate(srcs):
        for out, d in zip(outs, (1 - odd, odd)):
            out[f] = jnp.zeros(out.shape[1:], bf16)
            at = pl.multiple_of(d * 448, 64)
            for s in range(2):
                live, bx, by = place(pos, s)

                @pl.when(live & (bx == d))
                def _():
                    out[f, pl.ds(pl.multiple_of(by * 64, 64), 64)] = src[s, pl.ds(at, 64)]


def pack_x_body(pos, odd, a, b, *outs):
    pack_x(pos, odd[0], (a, b), outs)


def load_body(pos, core, odd, a, b, a_out, b_out, sent, *outs):
    pack_x(pos, odd[0], (a, b), outs)
    a_out[...] = a[...]
    b_out[...] = b[...]
    sent[...] = jnp.where(core[0] == 0, b[...], a[...])


def pack_y_body(pos, meta, a, b, xa, xb, ya, yb, tmp):
    def edge_rows(v, d):
        v = v.astype(f32)
        return jnp.where(d == 0, v[0:8], v[8:16])

    for f, src in enumerate((a, b)):
        for out, d in ((ya, 1 - meta[0]), (yb, meta[0])):
            tmp[...] = jnp.zeros_like(tmp)
            rows = pl.ds(pl.multiple_of(d * 112, 16), 16)
            xl, xr = sides(meta[3], xa[f, rows], xb[f, rows])
            tmp[0] = edge_rows(xl, d)
            tmp[17] = edge_rows(xr, d)
            for s in range(2):
                live, bx, by = place(pos, s)

                @pl.when(live & (by == d))
                def _():
                    for x in range(8):
                        at = pl.multiple_of(x * 64 + d * 48, 16)
                        tmp[1 + bx * 8 + x] = edge_rows(src[s, pl.ds(at, 16)], d)

            out[f] = tmp[...].reshape(144, C).astype(bf16)


def build(grid, f, pos, src, xl, xr, yl, yr):
    grid = grid.at[f] if isinstance(f, int) else grid
    grid[...] = jnp.zeros(grid.shape, f32)
    for s in range(2):
        live, bx, by = place(pos, s)

        @pl.when(live)
        def _():
            grid[pl.ds(1 + bx * 8, 8), pl.ds(1 + by * 8, 8)] = src[s].astype(f32).reshape(8, 8, 8, C)

    grid[0, 1:17] = xl.astype(f32).reshape(16, 8, C)
    grid[17, 1:17] = xr.astype(f32).reshape(16, 8, C)
    grid[:, 0] = yl.astype(f32).reshape(18, 8, C)
    grid[:, 17] = yr.astype(f32).reshape(18, 8, C)


def faces(meta, f, xa, xb, ya, yb):
    return *sides(meta[3], xa[f], xb[f]), *sides(meta[0], ya[f], yb[f])


def window(grid, f, bx, by, j):
    sx, sy = j // 3, j % 3
    w = grid[f, pl.ds(bx * 8 + sx, 8), pl.ds(by * 8 + sy, 8)]
    return w.reshape(512, C).astype(bf16)


def up_z(v):
    z = lax.broadcasted_iota(jnp.int32, v.shape, 1)
    return jnp.where(z == 7, 0.0, pltpu.roll(v, 7, 1))


def down_z(v):
    z = lax.broadcasted_iota(jnp.int32, v.shape, 1)
    return jnp.where(z == 0, 0.0, pltpu.roll(v, 1, 1))


def prep_body(k1, k2, gain, w1, w2, t1, t2, gain_out):
    for k, w, t in ((k1, w1, t1), (k2, w2, t2)):
        for j in range(9):
            for oz in range(3):
                w[j * C : (j + 1) * C, oz * C : (oz + 1) * C] = k[3 * j + oz]
                t[oz * C : (oz + 1) * C, j * C : (j + 1) * C] = k[3 * (8 - j) + oz]
    gain_out[...] = gain[...]


def convolve(grid, f, bx, by, cols, w, flipped):
    for j in range(9):
        cols[:, j * C : (j + 1) * C] = window(grid, f, bx, by, j)
    dims = (((1,), (1,)), ((), ())) if flipped else (((1,), (0,)), ((), ()))
    y = lax.dot_general(cols[...], w[...], dims, preferred_element_type=f32)
    lower, mid, upper = (y[:, i * C : (i + 1) * C].reshape(64, 8, C) for i in range(3))
    if flipped:
        out = mid + up_z(lower) + down_z(upper)
    else:
        out = mid + down_z(lower) + up_z(upper)
    return out.reshape(512, C)


def split3(v):
    hi = v.astype(bf16).astype(f32)
    rest = v - hi
    mid = rest.astype(bf16).astype(f32)
    return hi, mid, rest - mid


def main_body(
    pos, meta, a, b, xa, xb, ya, yb, w1, w2, gain,
    hid, pre, msg, gain_part, grid, cols, hg
):
    core = meta[0]
    for f, src in enumerate((a, b)):
        build(grid, f, pos, src, *faces(meta, f, xa, xb, ya, yb))
    at = P_ROWS
    for face in faces(meta, 1 - core, xa, xb, ya, yb):
        msg[at : at + face.shape[0]] = face
        at += face.shape[0]
    g = gain[...]
    total = jnp.zeros((1, C), f32)
    for s in range(2):
        live, bx, by = place(pos, s)
        hg[...] = convolve(grid, 1, bx, by, cols, w2, True)
        first = convolve(grid, 0, bx, by, cols, w1, False)
        center = first - jnp.mean(first, axis=1, keepdims=True)
        spread = jnp.mean(center * center, axis=1, keepdims=True)
        inv = lax.rsqrt(spread + 1e-05)
        n = center * inv
        v = n * g
        sig = jax.nn.sigmoid(v)
        on = jnp.where(live, 1.0, 0.0)
        h = jnp.where(live, v * sig, 0.0).astype(bf16)
        grad = jnp.where(live, hg[...], 0.0)
        dv = grad * (sig * (1.0 + v * (1.0 - sig)))
        total = total + jnp.sum(dv * n, axis=0, keepdims=True)
        dn = dv * g
        m1 = jnp.mean(dn, axis=1, keepdims=True)
        m2 = jnp.mean(dn * n, axis=1, keepdims=True)
        p = (inv * (dn - m1 - n * m2)).astype(bf16)
        hid[s] = h
        pre[s] = p
        msg[s * 512 : (s + 1) * 512] = jnp.where(core == 0, h, p)
    gain_part[...] = jnp.broadcast_to(total, (8, C))
    msg[1024:P_ROWS] = pack3(total)


def out_body(pos, meta, src, xa, xb, ya, yb, w, base, out, grid, cols, *, field):
    build(grid, 0, pos, src, *faces(meta, field, xa, xb, ya, yb))
    for s in range(2):
        live, bx, by = place(pos, s)
        y = convolve(grid, 0, bx, by, cols, w, field == 1)
        out[s] = jnp.where(live, base[s].astype(f32) + y, 0.0).astype(bf16)


JS = 5


def shifted(pt, slot, v):
    v = v.astype(f32).reshape(64, 8, C)
    for i, t in enumerate((up_z(v), v, down_z(v))):
        pt[i * C : (i + 1) * C, slot * 512 : (slot + 1) * 512] = t.reshape(512, C).T.astype(bf16)


def product(core, grid, pos, pt, upper, cols):
    for s in range(2):
        _, bx, by = place(pos, s)
        for i in range(JS):
            sx = jnp.where(upper, (i + 9 - JS) // 3, i // 3)
            sy = jnp.where(upper, (i + 9 - JS) % 3, i % 3)
            sx, sy = jnp.where(core == 0, sx, 2 - sx), jnp.where(core == 0, sy, 2 - sy)
            w = grid[pl.ds(bx * 8 + sx, 8), pl.ds(by * 8 + sy, 8)]
            cols[s * 512 : (s + 1) * 512, i * C : (i + 1) * C] = w.reshape(512, C).astype(bf16)
    return jnp.dot(pt[...], cols[...], preferred_element_type=f32)


def pieces(core, sums, acc, dsts, mine, upper, first, chunks):
    def block(i, oz):
        return sums[oz * C : (oz + 1) * C, i * C : (i + 1) * C]

    @pl.when(core == 0)
    def _():
        for i in range(JS):
            for oz in range(3):
                acc[(3 * i + oz) * C : (3 * i + oz + 1) * C] = block(i, oz).T

    @pl.when(core != 0)
    def _():
        for i in range(JS):
            for oz in range(3):
                acc[(3 * i + oz) * C : (3 * i + oz + 1) * C] = block(i, 2 - oz)

    size = TAPS * C // chunks
    skip = jnp.where(upper, (9 - JS) * 3 * C, 0)
    p = first
    for dst in dsts:
        for q in range(0, dst.shape[0] // size, 2):
            starts = [pl.multiple_of((mine ^ (p + i)) * size - skip, 8) for i in range(2)]
            two = jnp.concatenate([acc[pl.ds(a, size)] for a in starts])
            dst[q * size : (q + 2) * size] = two.astype(dst.dtype)
            p += 2


def sends_upper(mine, chunks):
    return mine < chunks // 2


def own_body(pos, meta, a, b, xa, xb, ya, yb, hid, pre, grid, pt, part, cols, *, chunks):
    core = meta[0]
    for f, src in enumerate((a, b)):

        @pl.when(core == f)
        def _():
            build(grid, None, pos, src, *faces(meta, f, xa, xb, ya, yb))

    for s in range(2):
        shifted(pt, s, jnp.where(core == 0, pre[s], hid[s]))
    part[...] = product(core, grid, pos, pt, sends_upper(meta[1], chunks), cols)


def send_body(
    ppos, meta, other, msg, gain_part, part, grid, pt, out_b, out_a, gsum, cols, sums, acc, *, chunks
):
    theirs, at = [], P_ROWS
    for rows in FACES:
        theirs.append(msg[at : at + rows])
        at += rows
    build(grid, None, ppos, other, *theirs)
    for s in range(2):
        shifted(pt, s, msg[s * 512 : (s + 1) * 512])
    upper = sends_upper(meta[1], chunks)
    sums[...] = part[...] + product(meta[0], grid, ppos, pt, upper, cols)
    pieces(meta[0], sums, acc, (out_b, out_a), meta[1], upper, chunks // 2, chunks)
    tile = msg[1024:P_ROWS].astype(f32)
    total = gain_part[0:1] + ((tile[2:3] + tile[1:2]) + tile[0:1])
    gsum[...] = jnp.broadcast_to(total, (8, C))


def keep_body(pos, ppos, meta, grid_a, grid_b, pt_a, pt_b, keep_b, keep_a, cols_a, cols_b, sums, acc, *, chunks):
    upper = jnp.logical_not(sends_upper(meta[1], chunks))
    sums[...] = product(meta[0], grid_a, pos, pt_a, upper, cols_a)
    sums[...] += product(meta[0], grid_b, ppos, pt_b, upper, cols_b)
    pieces(meta[0], sums, acc, (keep_b, keep_a), meta[1], upper, 0, chunks)


def pack3(v):
    hi, mid, low = split3(v)
    row = lax.broadcasted_iota(jnp.int32, (16, C), 0)
    return jnp.where(row == 0, hi, jnp.where(row == 1, mid, jnp.where(row == 2, low, 0.0))).astype(bf16)


def seal_body(low, g, out):
    v = low[...].astype(bf16).astype(f32)
    squares = jnp.sum(jnp.sum((v * v).reshape(-1, 8, C), axis=0), axis=0, keepdims=True)
    row = lax.broadcasted_iota(jnp.int32, (8, C), 0)
    tile = jnp.zeros((8, C), f32)
    for i, part in enumerate((*split3(g[0:1]), *split3(squares))):
        tile = jnp.where(row == i, part, tile)
    out[...] = jnp.concatenate([v, tile]).astype(bf16)


def tiles_body(pieces, out):
    n = out.shape[0] // 8
    step = pieces.shape[0] // n
    for i in range(n):
        out[i * 8 : (i + 1) * 8] = pieces[(i + 1) * step - 8 : (i + 1) * step]


def join_body(*refs):
    out, at = refs[-1], 0
    for ref in refs[:-1]:
        out[at : at + ref.shape[0]] = ref[...]
        at += ref.shape[0]


def join(*parts):
    rows = sum(p.shape[0] for p in parts)
    (out,) = call(join_body, [sds((rows, C), bf16)], [], parts, 0)
    return out


def put(pieces, k, me, first, shrink, stage, sems, out, copies):
    size = stage.shape[1]
    for src in pieces:
        for q in range(src.shape[0] // (size + 8)):
            n = len(copies)
            v = src[q * (size + 8) : (q + 1) * (size + 8)].astype(f32)
            stage[n] = v[:size] * shrink
            rows = pl.ds(pl.multiple_of((me ^ (first + q)) * size, 8), size)
            copies.append(pltpu.make_async_copy(stage.at[n], out.at[k, rows], sems.at[n]))
            copies[-1].start()
        first += src.shape[0] // (size + 8)


def gathered_body(
    meta, o0, o1, o2, o3, p0, p1, p2, p3, k_out, g_out, shrink_out, gains, squares, stage, g_stage, sems, *, chunks
):
    core, mine, theirs = meta[0], meta[1], meta[2]
    n = TAPS * C
    step = n // chunks + 8
    for k, me, pieces, tiles in (
        (core, mine, (o0, o1, o2), o3), (1 - core, theirs, (p0, p1, p2), p3)
    ):
        quarter = chunks // 4
        for p in range(chunks):
            q = p % quarter
            ref, at = (tiles, q * 8) if p >= 3 * quarter else (pieces[p // quarter], (q + 1) * step - 8)
            t = ref[at : at + 8].astype(f32)
            gains[k, me ^ p] = jnp.broadcast_to((t[2:3] + t[1:2]) + t[0:1], (8, C))
            squares[k, me ^ p] = jnp.broadcast_to((t[5:6] + t[4:5]) + t[3:4], (8, C))
    g = jnp.sum(gains[0], axis=0)[0:1]
    total = jnp.sum(g * g) + jnp.sum(jnp.sum(squares[...].reshape(2 * chunks, 8, C), axis=0)[0:1])
    entries = 2.0 * n * C + C
    norm = jnp.full((8, C), total / entries + 1e-06, f32)
    shrink = jnp.minimum(1.0, clip_level / jnp.sqrt(norm))
    shrink_out[...] = shrink
    g_stage[...] = g * shrink[0:1]
    copy = pltpu.make_async_copy(g_stage, g_out, sems.at[stage.shape[0]])
    copy.start()
    copies = []
    put((o0, o1, o2), core, mine, 0, shrink[0:1], stage, sems, k_out, copies)
    put((p0, p1, p2), 1 - core, theirs, 0, shrink[0:1], stage, sems, k_out, copies)
    for c in (copy, *copies):
        c.wait()


def final_body(meta, o3, p3, shrink, k_in, k_out, stage, sems, *, chunks):
    core, mine, theirs = meta[0], meta[1], meta[2]
    first = chunks // 4 * 3
    copies = []
    put((o3,), core, mine, first, shrink[0:1], stage, sems, k_out, copies)
    put((p3,), 1 - core, theirs, first, shrink[0:1], stage, sems, k_out, copies)
    for c in copies:
        c.wait()


def across(a, b, axis):
    n = lax.axis_size(axis)
    even, odd = (
        [p for i in range(first, n - 1, 2) for p in ((i, i + 1), (i + 1, i))] for first in (0, 1)
    )
    b = lax.ppermute(b, axis, odd)
    a = lax.ppermute(a, axis, even)
    return a, b


def y_faces(pos, meta, a, b, xa, xb):
    return call(
        pack_y_body,
        [sds((2, 144, C), bf16)] * 2,
        [pltpu.VMEM((18, 8, C), f32)],
        (pos, meta, a, b, xa, xb),
        2,
    )


def plan():
    nx, ny = lax.axis_size("gx"), lax.axis_size("gy")
    xs = [(1 << i, 0) for i in range(nx.bit_length() - 1)]
    zs = [(0, 1 << i) for i in range(1, ny.bit_length() - 1)]
    k = min(len(zs), 4 - len(xs))
    orders = (xs + zs[:k], xs[1:] + xs[:1] + zs[:k])
    group = []
    for m in range(1, 1 << k):
        group.append(sum(zs[i][1] for i in range(k) if m >> (k - 1 - i) & 1))
    return orders, len(xs), group, [z for _, z in zs[k:]]


def pairs(dx, dy):
    nx, ny = lax.axis_size("gx"), lax.axis_size("gy")
    return [(i * ny + j, (i ^ dx[j % 2]) * ny + (j ^ dy)) for i in range(nx) for j in range(ny)]


def chunk_index(order, halvings, ix, iy):
    out = 0
    for s, (dx, dy) in enumerate(order[:halvings]):
        bit = ((ix & dx) | (iy & dy)) != 0
        out = out + bit.astype(jnp.int32) * (1 << (halvings - 1 - s))
    return jnp.asarray(out, jnp.int32)


def after(value, *done):
    return lax.optimization_barrier((value, *done))[0]


def per_device(features, brick_pos, cotangent, first_kernel, second_kernel, norm_gain):
    both = ("gx", "gy")
    ny = lax.axis_size("gy")
    ix, iy = lax.axis_index("gx"), lax.axis_index("gy")
    core = iy % 2
    orders, halvings, group, copies = plan()
    chunks = 1 << len(orders[0])
    me_a = chunk_index(orders[0], len(orders[0]), ix, iy)
    me_b = chunk_index(orders[1], len(orders[1]), ix, iy)
    meta = jnp.stack([core, jnp.where(core == 0, me_a, me_b), jnp.where(core == 0, me_b, me_a), ix % 2])
    partner = [(i, i ^ 1) for i in range(ny)]
    n = TAPS * C
    size = n // chunks

    hbm = lambda v: pltpu.with_memory_space_constraint(v, pltpu.HBM)
    features, cotangent, sent, fa, fb = call(
        load_body,
        [sds((2, 512, C), bf16)] * 3 + [sds((2, 128, C), bf16)] * 2,
        [],
        (brick_pos, core.reshape(1), (ix % 2).reshape(1), hbm(features), hbm(cotangent)),
        3,
    )
    xa, xb = across(fa, fb, "gx")
    ppos = lax.ppermute(brick_pos, "gy", partner)
    other = lax.ppermute(sent, "gy", partner)
    straight, turned = sds((9 * C, 3 * C), bf16), sds((3 * C, 9 * C), bf16)
    w1, w2, t1, t2, gain = call(
        prep_body,
        [straight, straight, turned, turned, sds((1, C), f32)],
        [],
        (hbm(first_kernel), hbm(second_kernel), hbm(norm_gain.reshape(1, C))),
        0,
    )
    fa, fb = y_faces(brick_pos, meta, after(features, gain), cotangent, xa, xb)
    fa = after(fa, ppos, other)
    edge = xa, xb, *across(fa, fb, "gy")
    grid = pltpu.VMEM((2, 18, 18, 8, C), f32)
    cols = pltpu.VMEM((512, 9 * C), bf16)
    hid, pre, msg, gain_part = call(
        main_body,
        [sds((2, 512, C), bf16)] * 2 + [sds((P_ROWS + sum(FACES), C), bf16), sds((8, C), f32)],
        [grid, cols, pltpu.VMEM((512, C), f32)],
        (brick_pos, meta, features, cotangent, *edge, w1, t2, gain),
        2,
        14,
    )
    pmsg = lax.ppermute(msg, "gy", partner)
    held = [sds((18, 18, 8, C), f32), sds((3 * C, 1024), bf16)]
    wide = pltpu.VMEM((1024, JS * C), bf16)
    acc = pltpu.VMEM((JS * 3 * C, C), f32)
    grid_a, pt_a, part = call(
        functools.partial(own_body, chunks=chunks),
        held + [sds((3 * C, JS * C), f32)],
        [wide],
        (brick_pos, meta, features, cotangent, *edge, hid, pre),
        2,
        10,
    )
    quarter = [sds((n // 4, C), bf16)] * 2
    grid_b, pt_b, out_b, out_a, g = call(
        functools.partial(send_body, chunks=chunks),
        held + quarter + [sds((8, C), f32)],
        [wide, pltpu.VMEM((3 * C, JS * C), f32), acc],
        (ppos, meta, other, pmsg, gain_part, part),
        2,
        10,
    )
    keep_b, keep_a = call(
        functools.partial(keep_body, chunks=chunks),
        [sds((n // 4, C), f32)] * 2,
        [wide, wide, pltpu.VMEM((3 * C, JS * C), f32), acc],
        (brick_pos, ppos, meta, grid_a, grid_b, pt_a, pt_b),
        3,
        12,
    )
    g = g[0:1]

    fa, fb = call(
        pack_x_body,
        [sds((2, 128, C), bf16)] * 2,
        [],
        (brick_pos, (ix % 2).reshape(1), after(hid, out_a), pre),
        2,
    )
    xa, xb = across(fa, fb, "gx")
    fa, fb = y_faces(brick_pos, meta, hid, pre, xa, xb)
    around = xa, xb, *across(fa, fb, "gy")
    results = []
    for f, (src, w, base) in enumerate(((hid, w2, features), (pre, t1, cotangent))):
        (res,) = call(
            functools.partial(out_body, field=f),
            [sds((2, 512, C), bf16)],
            [pltpu.VMEM((1, 18, 18, 8, C), f32), cols],
            (brick_pos, meta, src, *around, w, base),
            2,
            10,
        )
        results.append(res)

    swap = lambda v, dx, dy=0: lax.ppermute(v, both, pairs(dx, dy))
    steps = [(a[0], b[0]) for a, b in zip(*orders)][:halvings]
    got_a = swap(out_a, steps[0])
    got_b = swap(out_b, steps[0])
    out = (keep_a + got_a.astype(f32)).astype(bf16)
    got = swap(out, steps[1])
    low = keep_b + got_b.astype(f32) + got.astype(f32)
    for step in steps[2:]:
        half = low.shape[0] // 2
        got = swap(low[half:].astype(bf16), step)
        low = low[:half] + got.astype(f32)
    got = []
    for m, dy in enumerate(group, 1):
        out = low[m * size : (m + 1) * size]
        got.append(swap(out if dy == 2 else out.astype(bf16), (0, 0), dy))
    low = low[:size]
    for v in got:
        low = low + v.astype(f32)
    for dy in copies:
        got = swap(jnp.concatenate([low, jnp.broadcast_to(g, (8, C))]), (0, 0), dy)
        low, g = low + got[:size], g + got[size : size + 1]

    (full,) = call(seal_body, [sds((size + 8, C), bf16)], [], (low, g), 0)
    full = join(full, *(swap(full, (0, 0), dy) for dy in group))
    for step in reversed(steps[2:]):
        full = join(full, swap(full, step))
    own = [full]
    own.append(swap(full, steps[1]))
    own.append(swap(full, steps[0]))
    (tiles,) = call(tiles_body, [sds((chunks // 4 * 8, C), bf16)], [], (full,), 0)
    far = swap(tiles, tuple(a ^ b for a, b in zip(*steps[:2])))
    far_part = lax.ppermute(far, "gy", partner)
    own.append(swap(own[1], steps[0]))
    part = [lax.ppermute(v, "gy", partner) for v in own]
    any_space = pl.BlockSpec(memory_space=pl.ANY)

    def pieces_call(body, count, outs, out_specs, scratch, args, in_specs, aliases):
        return pl.pallas_call(
            functools.partial(body, chunks=chunks),
            out_shape=outs,
            in_specs=[SMEM] + in_specs,
            out_specs=out_specs,
            scratch_shapes=scratch
            + [pltpu.VMEM((count, size, C), f32)]
            + ([pltpu.VMEM((1, C), f32)] if scratch else [])
            + [pltpu.SemaphoreType.DMA((count + 1,))],
            input_output_aliases=aliases,
            compiler_params=pltpu.CompilerParams(vmem_limit_bytes=8 << 20),
        )(meta, *args)

    table = pltpu.VMEM((2, chunks, 8, C), f32)
    k_up, g_up, shrink = pieces_call(
        gathered_body,
        chunks // 2 * 3,
        [sds((2, n, C), f32), sds((1, C), f32), sds((8, C), f32)],
        [any_space, any_space, VMEM],
        [table, table],
        (*own[:3], far, *part[:3], far_part),
        [VMEM] * 8,
        {},
    )
    (k_up,) = pieces_call(
        final_body,
        chunks // 2,
        [sds((2, n, C), f32)],
        [any_space],
        [],
        (own[3], part[3], shrink, k_up),
        [VMEM] * 3 + [any_space],
        {4: 0},
    )
    return (*results, k_up.reshape(2, TAPS, C, C), g_up.reshape(C))


def solution(mesh):
    rows = P(("gx", "gy"), None, None)

    return jax.shard_map(
        per_device,
        mesh=mesh,
        in_specs=(rows, P(("gx", "gy")), rows, P(), P(), P()),
        out_specs=(rows, rows, P(), P()),
        check_vma=False,
    )
```

```python
import functools

import jax
import jax.numpy as jnp
from jax import lax
from jax.experimental import pallas as pl
from jax.experimental.pallas import tpu as pltpu
from jax.sharding import PartitionSpec as P


BY = 2
POS = 4
TAPS = 27
P_ROWS = 1040
FACES = (128, 128, 144, 144)
C = 128
clip_level = 0.5
f32, bf16 = jnp.float32, jnp.bfloat16
VMEM = pl.BlockSpec(memory_space=pltpu.VMEM)
SMEM = pl.BlockSpec(memory_space=pltpu.SMEM)


def sds(shape, dtype):
    return jax.ShapeDtypeStruct(shape, dtype)


def place(pos_ref, slot):
    p = pos_ref[slot]
    q = jnp.minimum(p, POS - 1)
    return p < POS, q // BY, q % BY


def call(body, outs, scratch, args, n_smem, mib=4, who=None):
    def kernel(*refs):
        known = () if who is None else (who(),)
        body(*refs[:n_smem], *known, *refs[n_smem:])

    return pl.pallas_call(
        kernel,
        out_shape=outs,
        in_specs=[SMEM] * n_smem + [VMEM] * (len(args) - n_smem),
        out_specs=[VMEM] * len(outs),
        scratch_shapes=scratch,
        compiler_params=pltpu.CompilerParams(vmem_limit_bytes=mib << 20),
    )(*args)


def sides(odd, a, b):
    return jnp.where(odd == 0, b, a), jnp.where(odd == 0, a, b)


def pack_x(pos, odd, srcs, outs):
    for f, src in enumerate(srcs):
        for out, d in zip(outs, (1 - odd, odd)):
            out[f] = jnp.zeros(out.shape[1:], bf16)
            at = pl.multiple_of(d * 448, 64)
            for s in range(2):
                live, bx, by = place(pos, s)

                @pl.when(live & (bx == d))
                def _():
                    out[f, pl.ds(pl.multiple_of(by * 64, 64), 64)] = src[s, pl.ds(at, 64)]


def pack_x_body(pos, meta, a, b, *outs):
    pack_x(pos, meta[3], (a, b), outs)


def load_body(pos, meta, a, b, a_out, b_out, sent, *outs):
    pack_x(pos, meta[3], (a, b), outs)
    a_out[...] = a[...]
    b_out[...] = b[...]
    sent[...] = jnp.where(meta[0] == 0, b[...], a[...])


def pack_y_body(pos, meta, a, b, xa, xb, ya, yb, tmp):
    def edge_rows(v, d):
        v = v.astype(f32)
        return jnp.where(d == 0, v[0:8], v[8:16])

    for f, src in enumerate((a, b)):
        for out, d in ((ya, 1 - meta[0]), (yb, meta[0])):
            tmp[...] = jnp.zeros_like(tmp)
            rows = pl.ds(pl.multiple_of(d * 112, 16), 16)
            xl, xr = sides(meta[3], xa[f, rows], xb[f, rows])
            tmp[0] = edge_rows(xl, d)
            tmp[17] = edge_rows(xr, d)
            for s in range(2):
                live, bx, by = place(pos, s)

                @pl.when(live & (by == d))
                def _():
                    for x in range(8):
                        at = pl.multiple_of(x * 64 + d * 48, 16)
                        tmp[1 + bx * 8 + x] = edge_rows(src[s, pl.ds(at, 16)], d)

            out[f] = tmp[...].reshape(144, C).astype(bf16)


def build(grid, f, pos, src, xl, xr, yl, yr):
    grid = grid.at[f] if isinstance(f, int) else grid
    grid[...] = jnp.zeros(grid.shape, f32)
    for s in range(2):
        live, bx, by = place(pos, s)

        @pl.when(live)
        def _():
            grid[pl.ds(1 + bx * 8, 8), pl.ds(1 + by * 8, 8)] = src[s].astype(f32).reshape(8, 8, 8, C)

    grid[0, 1:17] = xl.astype(f32).reshape(16, 8, C)
    grid[17, 1:17] = xr.astype(f32).reshape(16, 8, C)
    grid[:, 0] = yl.astype(f32).reshape(18, 8, C)
    grid[:, 17] = yr.astype(f32).reshape(18, 8, C)


def faces(meta, f, xa, xb, ya, yb):
    return *sides(meta[3], xa[f], xb[f]), *sides(meta[0], ya[f], yb[f])


def window(grid, f, bx, by, j):
    sx, sy = j // 3, j % 3
    w = grid[f, pl.ds(bx * 8 + sx, 8), pl.ds(by * 8 + sy, 8)]
    return w.reshape(512, C).astype(bf16)


def up_z(v):
    z = lax.broadcasted_iota(jnp.int32, v.shape, 1)
    return jnp.where(z == 7, 0.0, pltpu.roll(v, 7, 1))


def down_z(v):
    z = lax.broadcasted_iota(jnp.int32, v.shape, 1)
    return jnp.where(z == 0, 0.0, pltpu.roll(v, 1, 1))


def prep_body(k1, k2, gain, w1, w2, t1, t2, gain_out):
    for k, w, t in ((k1, w1, t1), (k2, w2, t2)):
        for j in range(9):
            for oz in range(3):
                w[j * C : (j + 1) * C, oz * C : (oz + 1) * C] = k[3 * j + oz]
                t[oz * C : (oz + 1) * C, j * C : (j + 1) * C] = k[3 * (8 - j) + oz]
    gain_out[...] = gain[...]


def convolve(grid, f, bx, by, cols, w, flipped):
    for j in range(9):
        cols[:, j * C : (j + 1) * C] = window(grid, f, bx, by, j)
    dims = (((1,), (1,)), ((), ())) if flipped else (((1,), (0,)), ((), ()))
    y = lax.dot_general(cols[...], w[...], dims, preferred_element_type=f32)
    lower, mid, upper = (y[:, i * C : (i + 1) * C].reshape(64, 8, C) for i in range(3))
    if flipped:
        out = mid + up_z(lower) + down_z(upper)
    else:
        out = mid + down_z(lower) + up_z(upper)
    return out.reshape(512, C)


def split3(v):
    hi = v.astype(bf16).astype(f32)
    rest = v - hi
    mid = rest.astype(bf16).astype(f32)
    return hi, mid, rest - mid


def main_body(
    pos, meta, a, b, xa, xb, ya, yb, w1, w2, gain,
    hid, pre, msg, gain_part, grid, cols, hg
):
    core = meta[0]
    for f, src in enumerate((a, b)):
        build(grid, f, pos, src, *faces(meta, f, xa, xb, ya, yb))
    at = P_ROWS
    for face in faces(meta, 1 - core, xa, xb, ya, yb):
        msg[at : at + face.shape[0]] = face
        at += face.shape[0]
    g = gain[...]
    total = jnp.zeros((1, C), f32)
    for s in range(2):
        live, bx, by = place(pos, s)
        hg[...] = convolve(grid, 1, bx, by, cols, w2, True)
        first = convolve(grid, 0, bx, by, cols, w1, False)
        center = first - jnp.mean(first, axis=1, keepdims=True)
        spread = jnp.mean(center * center, axis=1, keepdims=True)
        inv = lax.rsqrt(spread + 1e-05)
        n = center * inv
        v = n * g
        sig = jax.nn.sigmoid(v)
        on = jnp.where(live, 1.0, 0.0)
        h = jnp.where(live, v * sig, 0.0).astype(bf16)
        grad = jnp.where(live, hg[...], 0.0)
        dv = grad * (sig * (1.0 + v * (1.0 - sig)))
        total = total + jnp.sum(dv * n, axis=0, keepdims=True)
        dn = dv * g
        m1 = jnp.mean(dn, axis=1, keepdims=True)
        m2 = jnp.mean(dn * n, axis=1, keepdims=True)
        p = (inv * (dn - m1 - n * m2)).astype(bf16)
        hid[s] = h
        pre[s] = p
        msg[s * 512 : (s + 1) * 512] = jnp.where(core == 0, h, p)
    gain_part[...] = jnp.broadcast_to(total, (8, C))
    msg[1024:P_ROWS] = pack3(total)


def out_body(pos, meta, src, xa, xb, ya, yb, w, base, out, grid, cols, *, field):
    build(grid, 0, pos, src, *faces(meta, field, xa, xb, ya, yb))
    for s in range(2):
        live, bx, by = place(pos, s)
        y = convolve(grid, 0, bx, by, cols, w, field == 1)
        out[s] = jnp.where(live, base[s].astype(f32) + y, 0.0).astype(bf16)


JS = 5


def shifted(pt, slot, v):
    v = v.astype(f32).reshape(64, 8, C)
    for i, t in enumerate((up_z(v), v, down_z(v))):
        pt[i * C : (i + 1) * C, slot * 512 : (slot + 1) * 512] = t.reshape(512, C).T.astype(bf16)


def product(core, grid, pos, pt, upper, cols):
    for s in range(2):
        _, bx, by = place(pos, s)
        for i in range(JS):
            sx = jnp.where(upper, (i + 9 - JS) // 3, i // 3)
            sy = jnp.where(upper, (i + 9 - JS) % 3, i % 3)
            sx, sy = jnp.where(core == 0, sx, 2 - sx), jnp.where(core == 0, sy, 2 - sy)
            w = grid[pl.ds(bx * 8 + sx, 8), pl.ds(by * 8 + sy, 8)]
            cols[s * 512 : (s + 1) * 512, i * C : (i + 1) * C] = w.reshape(512, C).astype(bf16)
    return jnp.dot(pt[...], cols[...], preferred_element_type=f32)


def pieces(core, sums, acc, dsts, mine, upper, first, chunks):
    def block(i, oz):
        return sums[oz * C : (oz + 1) * C, i * C : (i + 1) * C]

    @pl.when(core == 0)
    def _():
        for i in range(JS):
            for oz in range(3):
                acc[(3 * i + oz) * C : (3 * i + oz + 1) * C] = block(i, oz).T

    @pl.when(core != 0)
    def _():
        for i in range(JS):
            for oz in range(3):
                acc[(3 * i + oz) * C : (3 * i + oz + 1) * C] = block(i, 2 - oz)

    size = TAPS * C // chunks
    skip = jnp.where(upper, (9 - JS) * 3 * C, 0)
    p = first
    for dst in dsts:
        for q in range(0, dst.shape[0] // size, 2):
            starts = [pl.multiple_of((mine ^ (p + i)) * size - skip, 8) for i in range(2)]
            two = jnp.concatenate([acc[pl.ds(a, size)] for a in starts])
            dst[q * size : (q + 2) * size] = two.astype(dst.dtype)
            p += 2


def sends_upper(mine, chunks):
    return mine < chunks // 2


def own_body(pos, meta, a, b, xa, xb, ya, yb, hid, pre, grid, pt, part, cols, *, chunks):
    core = meta[0]
    for f, src in enumerate((a, b)):

        @pl.when(core == f)
        def _():
            build(grid, None, pos, src, *faces(meta, f, xa, xb, ya, yb))

    for s in range(2):
        shifted(pt, s, jnp.where(core == 0, pre[s], hid[s]))
    part[...] = product(core, grid, pos, pt, sends_upper(meta[1], chunks), cols)


def send_body(
    ppos, meta, other, msg, gain_part, part, grid, pt, out_b, out_a, gsum, cols, sums, acc, *, chunks
):
    theirs, at = [], P_ROWS
    for rows in FACES:
        theirs.append(msg[at : at + rows])
        at += rows
    build(grid, None, ppos, other, *theirs)
    for s in range(2):
        shifted(pt, s, msg[s * 512 : (s + 1) * 512])
    upper = sends_upper(meta[1], chunks)
    sums[...] = part[...] + product(meta[0], grid, ppos, pt, upper, cols)
    pieces(meta[0], sums, acc, (out_b, out_a), meta[1], upper, chunks // 2, chunks)
    tile = msg[1024:P_ROWS].astype(f32)
    total = gain_part[0:1] + ((tile[2:3] + tile[1:2]) + tile[0:1])
    gsum[...] = jnp.broadcast_to(total, (8, C))


def keep_body(pos, ppos, meta, grid_a, grid_b, pt_a, pt_b, keep_b, keep_a, cols_a, cols_b, sums, acc, *, chunks):
    upper = jnp.logical_not(sends_upper(meta[1], chunks))
    sums[...] = product(meta[0], grid_a, pos, pt_a, upper, cols_a)
    sums[...] += product(meta[0], grid_b, ppos, pt_b, upper, cols_b)
    pieces(meta[0], sums, acc, (keep_b, keep_a), meta[1], upper, 0, chunks)


def pack3(v):
    hi, mid, low = split3(v)
    row = lax.broadcasted_iota(jnp.int32, (16, C), 0)
    return jnp.where(row == 0, hi, jnp.where(row == 1, mid, jnp.where(row == 2, low, 0.0))).astype(bf16)


def seal_body(low, g, out):
    v = low[...].astype(bf16).astype(f32)
    squares = jnp.sum(jnp.sum((v * v).reshape(-1, 8, C), axis=0), axis=0, keepdims=True)
    row = lax.broadcasted_iota(jnp.int32, (8, C), 0)
    tile = jnp.zeros((8, C), f32)
    for i, part in enumerate((*split3(g[0:1]), *split3(squares))):
        tile = jnp.where(row == i, part, tile)
    out[...] = jnp.concatenate([v, tile]).astype(bf16)


def tiles_body(pieces, out):
    n = out.shape[0] // 8
    step = pieces.shape[0] // n
    for i in range(n):
        out[i * 8 : (i + 1) * 8] = pieces[(i + 1) * step - 8 : (i + 1) * step]


def join_body(*refs):
    out, at = refs[-1], 0
    for ref in refs[:-1]:
        out[at : at + ref.shape[0]] = ref[...]
        at += ref.shape[0]


def join(*parts):
    rows = sum(p.shape[0] for p in parts)
    (out,) = call(join_body, [sds((rows, C), bf16)], [], parts, 0)
    return out


def put(pieces, k, me, first, shrink, stage, sems, out, copies):
    size = stage.shape[1]
    for src in pieces:
        for q in range(src.shape[0] // (size + 8)):
            n = len(copies)
            v = src[q * (size + 8) : (q + 1) * (size + 8)].astype(f32)
            stage[n] = v[:size] * shrink
            rows = pl.ds(pl.multiple_of((me ^ (first + q)) * size, 8), size)
            copies.append(pltpu.make_async_copy(stage.at[n], out.at[k, rows], sems.at[n]))
            copies[-1].start()
        first += src.shape[0] // (size + 8)


def gathered_body(
    meta, o0, o1, o2, o3, p0, p1, p2, p3, k_out, g_out, shrink_out, gains, squares, stage, g_stage, sems, *, chunks
):
    core, mine, theirs = meta[0], meta[1], meta[2]
    n = TAPS * C
    step = n // chunks + 8
    for k, me, pieces, tiles in (
        (core, mine, (o0, o1, o2), o3), (1 - core, theirs, (p0, p1, p2), p3)
    ):
        quarter = chunks // 4
        for p in range(chunks):
            q = p % quarter
            ref, at = (tiles, q * 8) if p >= 3 * quarter else (pieces[p // quarter], (q + 1) * step - 8)
            t = ref[at : at + 8].astype(f32)
            gains[k, me ^ p] = jnp.broadcast_to((t[2:3] + t[1:2]) + t[0:1], (8, C))
            squares[k, me ^ p] = jnp.broadcast_to((t[5:6] + t[4:5]) + t[3:4], (8, C))
    g = jnp.sum(gains[0], axis=0)[0:1]
    total = jnp.sum(g * g) + jnp.sum(jnp.sum(squares[...].reshape(2 * chunks, 8, C), axis=0)[0:1])
    entries = 2.0 * n * C + C
    norm = jnp.full((8, C), total / entries + 1e-06, f32)
    shrink = jnp.minimum(1.0, clip_level / jnp.sqrt(norm))
    shrink_out[...] = shrink
    g_stage[...] = g * shrink[0:1]
    copy = pltpu.make_async_copy(g_stage, g_out, sems.at[stage.shape[0]])
    copy.start()
    copies = []
    put((o0, o1, o2), core, mine, 0, shrink[0:1], stage, sems, k_out, copies)
    put((p0, p1, p2), 1 - core, theirs, 0, shrink[0:1], stage, sems, k_out, copies)
    for c in (copy, *copies):
        c.wait()


def final_body(meta, o3, p3, shrink, k_in, k_out, stage, sems, *, chunks):
    core, mine, theirs = meta[0], meta[1], meta[2]
    first = chunks // 4 * 3
    copies = []
    put((o3,), core, mine, first, shrink[0:1], stage, sems, k_out, copies)
    put((p3,), 1 - core, theirs, first, shrink[0:1], stage, sems, k_out, copies)
    for c in copies:
        c.wait()


def across(a, b, axis):
    n = lax.axis_size(axis)
    even, odd = (
        [p for i in range(first, n - 1, 2) for p in ((i, i + 1), (i + 1, i))] for first in (0, 1)
    )
    b = lax.ppermute(b, axis, odd)
    a = lax.ppermute(a, axis, even)
    return a, b


def y_faces(pos, who, a, b, xa, xb):
    return call(
        pack_y_body,
        [sds((2, 144, C), bf16)] * 2,
        [pltpu.VMEM((18, 8, C), f32)],
        (pos, a, b, xa, xb),
        1,
        who=who,
    )


def plan():
    nx, ny = lax.axis_size("gx"), lax.axis_size("gy")
    xs = [(1 << i, 0) for i in range(nx.bit_length() - 1)]
    zs = [(0, 1 << i) for i in range(1, ny.bit_length() - 1)]
    k = min(len(zs), 4 - len(xs))
    orders = (xs + zs[:k], xs[1:] + xs[:1] + zs[:k])
    group = []
    for m in range(1, 1 << k):
        group.append(sum(zs[i][1] for i in range(k) if m >> (k - 1 - i) & 1))
    return orders, len(xs), group, [z for _, z in zs[k:]]


def pairs(dx, dy):
    nx, ny = lax.axis_size("gx"), lax.axis_size("gy")
    return [(i * ny + j, (i ^ dx[j % 2]) * ny + (j ^ dy)) for i in range(nx) for j in range(ny)]


def chunk_index(order, halvings, ix, iy):
    out = 0
    for s, (dx, dy) in enumerate(order[:halvings]):
        bit = ((ix & dx) | (iy & dy)) != 0
        out = out + bit.astype(jnp.int32) * (1 << (halvings - 1 - s))
    return jnp.asarray(out, jnp.int32)


def after(value, *done):
    return lax.optimization_barrier((value, *done))[0]


def per_device(features, brick_pos, cotangent, first_kernel, second_kernel, norm_gain):
    both = ("gx", "gy")
    ny = lax.axis_size("gy")
    orders, halvings, group, copies = plan()
    chunks = 1 << len(orders[0])

    def who():
        ix, iy = lax.axis_index("gx"), lax.axis_index("gy")
        core = iy % 2
        a, b = (chunk_index(o, len(o), ix, iy) for o in orders)
        return core, jnp.where(core == 0, a, b), jnp.where(core == 0, b, a), ix % 2

    partner = [(i, i ^ 1) for i in range(ny)]
    hbm = lambda v: pltpu.with_memory_space_constraint(v, pltpu.HBM)
    slots, brick_pos = brick_pos, hbm(brick_pos)
    n = TAPS * C
    size = n // chunks

    features, cotangent, sent, fa, fb = call(
        load_body,
        [sds((2, 512, C), bf16)] * 3 + [sds((2, 128, C), bf16)] * 2,
        [],
        (brick_pos, hbm(features), hbm(cotangent)),
        1,
        who=who,
    )
    xa, xb = across(fa, fb, "gx")
    ppos = lax.ppermute(slots, "gy", partner)
    other = lax.ppermute(sent, "gy", partner)
    straight, turned = sds((9 * C, 3 * C), bf16), sds((3 * C, 9 * C), bf16)
    w1, w2, t1, t2, gain = call(
        prep_body,
        [straight, straight, turned, turned, sds((1, C), f32)],
        [],
        (hbm(first_kernel), hbm(second_kernel), hbm(norm_gain.reshape(1, C))),
        0,
    )
    fa, fb = y_faces(brick_pos, who, after(features, gain), cotangent, xa, xb)
    fa = after(fa, ppos, other)
    edge = xa, xb, *across(fa, fb, "gy")
    grid = pltpu.VMEM((2, 18, 18, 8, C), f32)
    cols = pltpu.VMEM((512, 9 * C), bf16)
    hid, pre, msg, gain_part = call(
        main_body,
        [sds((2, 512, C), bf16)] * 2 + [sds((P_ROWS + sum(FACES), C), bf16), sds((8, C), f32)],
        [grid, cols, pltpu.VMEM((512, C), f32)],
        (brick_pos, features, cotangent, *edge, w1, t2, gain),
        1,
        14,
        who,
    )
    pmsg = lax.ppermute(msg, "gy", partner)
    held = [sds((18, 18, 8, C), f32), sds((3 * C, 1024), bf16)]
    wide = pltpu.VMEM((1024, JS * C), bf16)
    acc = pltpu.VMEM((JS * 3 * C, C), f32)
    grid_a, pt_a, part = call(
        functools.partial(own_body, chunks=chunks),
        held + [sds((3 * C, JS * C), f32)],
        [wide],
        (brick_pos, features, cotangent, *edge, hid, pre),
        1,
        10,
        who,
    )
    quarter = [sds((n // 4, C), bf16)] * 2
    grid_b, pt_b, out_b, out_a, g = call(
        functools.partial(send_body, chunks=chunks),
        held + quarter + [sds((8, C), f32)],
        [wide, pltpu.VMEM((3 * C, JS * C), f32), acc],
        (ppos, other, pmsg, gain_part, part),
        1,
        10,
        who,
    )
    keep_b, keep_a = call(
        functools.partial(keep_body, chunks=chunks),
        [sds((n // 4, C), f32)] * 2,
        [wide, wide, pltpu.VMEM((3 * C, JS * C), f32), acc],
        (brick_pos, ppos, grid_a, grid_b, pt_a, pt_b),
        2,
        12,
        who,
    )
    g = g[0:1]

    fa, fb = call(
        pack_x_body,
        [sds((2, 128, C), bf16)] * 2,
        [],
        (brick_pos, after(hid, out_a), pre),
        1,
        who=who,
    )
    xa, xb = across(fa, fb, "gx")
    fa, fb = y_faces(brick_pos, who, hid, pre, xa, xb)
    around = xa, xb, *across(fa, fb, "gy")
    results = []
    for f, (src, w, base) in enumerate(((hid, w2, features), (pre, t1, cotangent))):
        (res,) = call(
            functools.partial(out_body, field=f),
            [sds((2, 512, C), bf16)],
            [pltpu.VMEM((1, 18, 18, 8, C), f32), cols],
            (brick_pos, src, *around, w, base),
            1,
            10,
            who,
        )
        results.append(res)

    swap = lambda v, dx, dy=0: lax.ppermute(v, both, pairs(dx, dy))
    steps = [(a[0], b[0]) for a, b in zip(*orders)][:halvings]
    got_a = swap(out_a, steps[0])
    got_b = swap(out_b, steps[0])
    out = (keep_a + got_a.astype(f32)).astype(bf16)
    got = swap(out, steps[1])
    low = keep_b + got_b.astype(f32) + got.astype(f32)
    for step in steps[2:]:
        half = low.shape[0] // 2
        got = swap(low[half:].astype(bf16), step)
        low = low[:half] + got.astype(f32)
    got = []
    for m, dy in enumerate(group, 1):
        out = low[m * size : (m + 1) * size]
        got.append(swap(out if dy == 2 else out.astype(bf16), (0, 0), dy))
    low = low[:size]
    for v in got:
        low = low + v.astype(f32)
    for dy in copies:
        got = swap(jnp.concatenate([low, jnp.broadcast_to(g, (8, C))]), (0, 0), dy)
        low, g = low + got[:size], g + got[size : size + 1]

    (full,) = call(seal_body, [sds((size + 8, C), bf16)], [], (low, g), 0)
    full = join(full, *(swap(full, (0, 0), dy) for dy in group))
    for step in reversed(steps[2:]):
        full = join(full, swap(full, step))
    own = [full]
    own.append(swap(full, steps[1]))
    own.append(swap(full, steps[0]))
    (tiles,) = call(tiles_body, [sds((chunks // 4 * 8, C), bf16)], [], (full,), 0)
    far = swap(tiles, tuple(a ^ b for a, b in zip(*steps[:2])))
    far_part = lax.ppermute(far, "gy", partner)
    own.append(swap(own[1], steps[0]))
    part = [lax.ppermute(v, "gy", partner) for v in own]
    any_space = pl.BlockSpec(memory_space=pl.ANY)

    def pieces_call(body, count, outs, out_specs, scratch, args, in_specs, aliases):
        return pl.pallas_call(
            lambda *refs: body(who(), *refs, chunks=chunks),
            out_shape=outs,
            in_specs=in_specs,
            out_specs=out_specs,
            scratch_shapes=scratch
            + [pltpu.VMEM((count, size, C), f32)]
            + ([pltpu.VMEM((1, C), f32)] if scratch else [])
            + [pltpu.SemaphoreType.DMA((count + 1,))],
            input_output_aliases=aliases,
            compiler_params=pltpu.CompilerParams(vmem_limit_bytes=8 << 20),
        )(*args)

    table = pltpu.VMEM((2, chunks, 8, C), f32)
    k_up, g_up, shrink = pieces_call(
        gathered_body,
        chunks // 2 * 3,
        [sds((2, n, C), f32), sds((1, C), f32), sds((8, C), f32)],
        [any_space, any_space, VMEM],
        [table, table],
        (*own[:3], far, *part[:3], far_part),
        [VMEM] * 8,
        {},
    )
    (k_up,) = pieces_call(
        final_body,
        chunks // 2,
        [sds((2, n, C), f32)],
        [any_space],
        [],
        (own[3], part[3], shrink, k_up),
        [VMEM] * 3 + [any_space],
        {3: 0},
    )
    return (*results, k_up.reshape(2, TAPS, C, C), g_up.reshape(C))


def solution(mesh):
    rows = P(("gx", "gy"), None, None)

    return jax.shard_map(
        per_device,
        mesh=mesh,
        in_specs=(rows, P(("gx", "gy")), rows, P(), P(), P()),
        out_specs=(rows, rows, P(), P()),
        check_vma=False,
    )
```

```python
import functools

import jax
import jax.numpy as jnp
from jax import lax
from jax.experimental import pallas as pl
from jax.experimental.pallas import tpu as pltpu
from jax.sharding import PartitionSpec as P


BY = 2
POS = 4
TAPS = 27
P_ROWS = 1040
FACES = (128, 128, 144, 144)
C = 128
clip_level = 0.5
f32, bf16 = jnp.float32, jnp.bfloat16
VMEM = pl.BlockSpec(memory_space=pltpu.VMEM)
SMEM = pl.BlockSpec(memory_space=pltpu.SMEM)


def sds(shape, dtype):
    return jax.ShapeDtypeStruct(shape, dtype)


def place(pos_ref, slot):
    p = pos_ref[slot]
    q = jnp.minimum(p, POS - 1)
    return p < POS, q // BY, q % BY


def call(body, outs, scratch, args, n_smem, mib=4, who=None):
    def kernel(*refs):
        known = () if who is None else (who(),)
        body(*refs[:n_smem], *known, *refs[n_smem:])

    return pl.pallas_call(
        kernel,
        out_shape=outs,
        in_specs=[SMEM] * n_smem + [VMEM] * (len(args) - n_smem),
        out_specs=[VMEM] * len(outs),
        scratch_shapes=scratch,
        compiler_params=pltpu.CompilerParams(vmem_limit_bytes=mib << 20),
    )(*args)


def sides(odd, a, b):
    return jnp.where(odd == 0, b, a), jnp.where(odd == 0, a, b)


def pack_x(pos, odd, srcs, outs):
    for f, src in enumerate(srcs):
        for out, d in zip(outs, (1 - odd, odd)):
            out[f] = jnp.zeros(out.shape[1:], bf16)
            at = pl.multiple_of(d * 448, 64)
            for s in range(2):
                live, bx, by = place(pos, s)

                @pl.when(live & (bx == d))
                def _():
                    out[f, pl.ds(pl.multiple_of(by * 64, 64), 64)] = src[s, pl.ds(at, 64)]


def pack_x_body(pos, meta, a, b, *outs):
    pack_x(pos, meta[3], (a, b), outs)


def load_body(pos, meta, a, b, a_out, b_out, sent, *outs):
    pack_x(pos, meta[3], (a, b), outs)
    a_out[...] = a[...]
    b_out[...] = b[...]
    sent[...] = jnp.where(meta[0] == 0, b[...], a[...])


def pack_y_body(pos, meta, a, b, xa, xb, ya, yb, tmp):
    def edge_rows(v, d):
        v = v.astype(f32)
        return jnp.where(d == 0, v[0:8], v[8:16])

    for f, src in enumerate((a, b)):
        for out, d in ((ya, 1 - meta[0]), (yb, meta[0])):
            tmp[...] = jnp.zeros_like(tmp)
            rows = pl.ds(pl.multiple_of(d * 112, 16), 16)
            xl, xr = sides(meta[3], xa[f, rows], xb[f, rows])
            tmp[0] = edge_rows(xl, d)
            tmp[17] = edge_rows(xr, d)
            for s in range(2):
                live, bx, by = place(pos, s)

                @pl.when(live & (by == d))
                def _():
                    for x in range(8):
                        at = pl.multiple_of(x * 64 + d * 48, 16)
                        tmp[1 + bx * 8 + x] = edge_rows(src[s, pl.ds(at, 16)], d)

            out[f] = tmp[...].reshape(144, C).astype(bf16)


def build(grid, f, pos, src, xl, xr, yl, yr):
    grid = grid.at[f] if isinstance(f, int) else grid
    grid[...] = jnp.zeros(grid.shape, f32)
    for s in range(2):
        live, bx, by = place(pos, s)

        @pl.when(live)
        def _():
            grid[pl.ds(1 + bx * 8, 8), pl.ds(1 + by * 8, 8)] = src[s].astype(f32).reshape(8, 8, 8, C)

    grid[0, 1:17] = xl.astype(f32).reshape(16, 8, C)
    grid[17, 1:17] = xr.astype(f32).reshape(16, 8, C)
    grid[:, 0] = yl.astype(f32).reshape(18, 8, C)
    grid[:, 17] = yr.astype(f32).reshape(18, 8, C)


def faces(meta, f, xa, xb, ya, yb):
    return *sides(meta[3], xa[f], xb[f]), *sides(meta[0], ya[f], yb[f])


def window(grid, f, bx, by, j):
    sx, sy = j // 3, j % 3
    w = grid[f, pl.ds(bx * 8 + sx, 8), pl.ds(by * 8 + sy, 8)]
    return w.reshape(512, C).astype(bf16)


def up_z(v):
    z = lax.broadcasted_iota(jnp.int32, v.shape, 1)
    return jnp.where(z == 7, 0.0, pltpu.roll(v, 7, 1))


def down_z(v):
    z = lax.broadcasted_iota(jnp.int32, v.shape, 1)
    return jnp.where(z == 0, 0.0, pltpu.roll(v, 1, 1))


def prep_body(k1, k2, gain, w1, w2, t1, t2, gain_out):
    for k, w, t in ((k1, w1, t1), (k2, w2, t2)):
        for j in range(9):
            for oz in range(3):
                w[j * C : (j + 1) * C, oz * C : (oz + 1) * C] = k[3 * j + oz]
                t[oz * C : (oz + 1) * C, j * C : (j + 1) * C] = k[3 * (8 - j) + oz]
    gain_out[...] = gain[...]


def convolve(grid, f, bx, by, cols, w, flipped):
    for j in range(9):
        cols[:, j * C : (j + 1) * C] = window(grid, f, bx, by, j)
    dims = (((1,), (1,)), ((), ())) if flipped else (((1,), (0,)), ((), ()))
    y = lax.dot_general(cols[...], w[...], dims, preferred_element_type=f32)
    lower, mid, upper = (y[:, i * C : (i + 1) * C].reshape(64, 8, C) for i in range(3))
    if flipped:
        out = mid + up_z(lower) + down_z(upper)
    else:
        out = mid + down_z(lower) + up_z(upper)
    return out.reshape(512, C)


def split3(v):
    hi = v.astype(bf16).astype(f32)
    rest = v - hi
    mid = rest.astype(bf16).astype(f32)
    return hi, mid, rest - mid


def main_body(
    pos, meta, a, b, xa, xb, ya, yb, w1, w2, gain,
    hid, pre, msg, gain_part, grid, cols, hg
):
    core = meta[0]
    for f, src in enumerate((a, b)):
        build(grid, f, pos, src, *faces(meta, f, xa, xb, ya, yb))
    at = P_ROWS
    for face in faces(meta, 1 - core, xa, xb, ya, yb):
        msg[at : at + face.shape[0]] = face
        at += face.shape[0]
    g = gain[...]
    total = jnp.zeros((1, C), f32)
    for s in range(2):
        live, bx, by = place(pos, s)
        hg[...] = convolve(grid, 1, bx, by, cols.at[2 * s], w2, True)
        first = convolve(grid, 0, bx, by, cols.at[2 * s + 1], w1, False)
        center = first - jnp.mean(first, axis=1, keepdims=True)
        spread = jnp.mean(center * center, axis=1, keepdims=True)
        inv = lax.rsqrt(spread + 1e-05)
        n = center * inv
        v = n * g
        sig = jax.nn.sigmoid(v)
        on = jnp.where(live, 1.0, 0.0)
        h = jnp.where(live, v * sig, 0.0).astype(bf16)
        grad = jnp.where(live, hg[...], 0.0)
        dv = grad * (sig * (1.0 + v * (1.0 - sig)))
        total = total + jnp.sum(dv * n, axis=0, keepdims=True)
        dn = dv * g
        m1 = jnp.mean(dn, axis=1, keepdims=True)
        m2 = jnp.mean(dn * n, axis=1, keepdims=True)
        p = (inv * (dn - m1 - n * m2)).astype(bf16)
        hid[s] = h
        pre[s] = p
        msg[s * 512 : (s + 1) * 512] = jnp.where(core == 0, h, p)
    gain_part[...] = jnp.broadcast_to(total, (8, C))
    msg[1024:P_ROWS] = pack3(total)


def out_body(pos, meta, src, xa, xb, ya, yb, w, base, out, grid, cols, *, field):
    build(grid, 0, pos, src, *faces(meta, field, xa, xb, ya, yb))
    for s in range(2):
        live, bx, by = place(pos, s)
        y = convolve(grid, 0, bx, by, cols, w, field == 1)
        out[s] = jnp.where(live, base[s].astype(f32) + y, 0.0).astype(bf16)


JS = 5


def shifted(pt, slot, v):
    v = v.astype(f32).reshape(64, 8, C)
    for i, t in enumerate((up_z(v), v, down_z(v))):
        pt[i * C : (i + 1) * C, slot * 512 : (slot + 1) * 512] = t.reshape(512, C).T.astype(bf16)


def product(core, grid, pos, pt, upper, cols):
    for s in range(2):
        _, bx, by = place(pos, s)
        for i in range(JS):
            sx = jnp.where(upper, (i + 9 - JS) // 3, i // 3)
            sy = jnp.where(upper, (i + 9 - JS) % 3, i % 3)
            sx, sy = jnp.where(core == 0, sx, 2 - sx), jnp.where(core == 0, sy, 2 - sy)
            w = grid[pl.ds(bx * 8 + sx, 8), pl.ds(by * 8 + sy, 8)]
            cols[s * 512 : (s + 1) * 512, i * C : (i + 1) * C] = w.reshape(512, C).astype(bf16)
    return jnp.dot(pt[...], cols[...], preferred_element_type=f32)


def pieces(core, sums, acc, dsts, mine, upper, first, chunks):
    def block(i, oz):
        return sums[oz * C : (oz + 1) * C, i * C : (i + 1) * C]

    @pl.when(core == 0)
    def _():
        for i in range(JS):
            for oz in range(3):
                acc[(3 * i + oz) * C : (3 * i + oz + 1) * C] = block(i, oz).T

    @pl.when(core != 0)
    def _():
        for i in range(JS):
            for oz in range(3):
                acc[(3 * i + oz) * C : (3 * i + oz + 1) * C] = block(i, 2 - oz)

    size = TAPS * C // chunks
    skip = jnp.where(upper, (9 - JS) * 3 * C, 0)
    p = first
    for dst in dsts:
        for q in range(0, dst.shape[0] // size, 2):
            starts = [pl.multiple_of((mine ^ (p + i)) * size - skip, 8) for i in range(2)]
            two = jnp.concatenate([acc[pl.ds(a, size)] for a in starts])
            dst[q * size : (q + 2) * size] = two.astype(dst.dtype)
            p += 2


def sends_upper(mine, chunks):
    return mine < chunks // 2


def own_body(pos, meta, a, b, xa, xb, ya, yb, hid, pre, grid, pt, part, cols, *, chunks):
    core = meta[0]
    for f, src in enumerate((a, b)):

        @pl.when(core == f)
        def _():
            build(grid, None, pos, src, *faces(meta, f, xa, xb, ya, yb))

    for s in range(2):
        shifted(pt, s, jnp.where(core == 0, pre[s], hid[s]))
    part[...] = product(core, grid, pos, pt, sends_upper(meta[1], chunks), cols)


def send_body(
    ppos, meta, other, msg, gain_part, part, grid, pt, out_b, out_a, gsum, cols, sums, acc, *, chunks
):
    theirs, at = [], P_ROWS
    for rows in FACES:
        theirs.append(msg[at : at + rows])
        at += rows
    build(grid, None, ppos, other, *theirs)
    for s in range(2):
        shifted(pt, s, msg[s * 512 : (s + 1) * 512])
    upper = sends_upper(meta[1], chunks)
    sums[...] = part[...] + product(meta[0], grid, ppos, pt, upper, cols)
    pieces(meta[0], sums, acc, (out_b, out_a), meta[1], upper, chunks // 2, chunks)
    tile = msg[1024:P_ROWS].astype(f32)
    total = gain_part[0:1] + ((tile[2:3] + tile[1:2]) + tile[0:1])
    gsum[...] = jnp.broadcast_to(total, (8, C))


def keep_body(pos, ppos, meta, grid_a, grid_b, pt_a, pt_b, keep_b, keep_a, cols_a, cols_b, sums, acc, *, chunks):
    upper = jnp.logical_not(sends_upper(meta[1], chunks))
    sums[...] = product(meta[0], grid_a, pos, pt_a, upper, cols_a)
    sums[...] += product(meta[0], grid_b, ppos, pt_b, upper, cols_b)
    pieces(meta[0], sums, acc, (keep_b, keep_a), meta[1], upper, 0, chunks)


def pack3(v):
    hi, mid, low = split3(v)
    row = lax.broadcasted_iota(jnp.int32, (16, C), 0)
    return jnp.where(row == 0, hi, jnp.where(row == 1, mid, jnp.where(row == 2, low, 0.0))).astype(bf16)


def seal_body(low, g, out):
    v = low[...].astype(bf16).astype(f32)
    squares = jnp.sum(jnp.sum((v * v).reshape(-1, 8, C), axis=0), axis=0, keepdims=True)
    row = lax.broadcasted_iota(jnp.int32, (8, C), 0)
    tile = jnp.zeros((8, C), f32)
    for i, part in enumerate((*split3(g[0:1]), *split3(squares))):
        tile = jnp.where(row == i, part, tile)
    out[...] = jnp.concatenate([v, tile]).astype(bf16)


def tiles_body(pieces, out):
    n = out.shape[0] // 8
    step = pieces.shape[0] // n
    for i in range(n):
        out[i * 8 : (i + 1) * 8] = pieces[(i + 1) * step - 8 : (i + 1) * step]


def join_body(*refs):
    out, at = refs[-1], 0
    for ref in refs[:-1]:
        out[at : at + ref.shape[0]] = ref[...]
        at += ref.shape[0]


def join(*parts):
    rows = sum(p.shape[0] for p in parts)
    (out,) = call(join_body, [sds((rows, C), bf16)], [], parts, 0)
    return out


def put(pieces, k, me, first, shrink, stage, sems, out, copies):
    size = stage.shape[1]
    for src in pieces:
        for q in range(src.shape[0] // (size + 8)):
            n = len(copies)
            v = src[q * (size + 8) : (q + 1) * (size + 8)].astype(f32)
            stage[n] = v[:size] * shrink
            rows = pl.ds(pl.multiple_of((me ^ (first + q)) * size, 8), size)
            copies.append(pltpu.make_async_copy(stage.at[n], out.at[k, rows], sems.at[n]))
            copies[-1].start()
        first += src.shape[0] // (size + 8)


def gathered_body(
    meta, o0, o1, o2, o3, p0, p1, p2, p3, k_out, g_out, shrink_out, gains, squares, stage, g_stage, sems, *, chunks
):
    core, mine, theirs = meta[0], meta[1], meta[2]
    n = TAPS * C
    step = n // chunks + 8
    for k, me, pieces, tiles in (
        (core, mine, (o0, o1, o2), o3), (1 - core, theirs, (p0, p1, p2), p3)
    ):
        quarter = chunks // 4
        for p in range(chunks):
            q = p % quarter
            ref, at = (tiles, q * 8) if p >= 3 * quarter else (pieces[p // quarter], (q + 1) * step - 8)
            t = ref[at : at + 8].astype(f32)
            gains[k, me ^ p] = jnp.broadcast_to((t[2:3] + t[1:2]) + t[0:1], (8, C))
            squares[k, me ^ p] = jnp.broadcast_to((t[5:6] + t[4:5]) + t[3:4], (8, C))
    g = jnp.sum(gains[0], axis=0)[0:1]
    total = jnp.sum(g * g) + jnp.sum(jnp.sum(squares[...].reshape(2 * chunks, 8, C), axis=0)[0:1])
    entries = 2.0 * n * C + C
    norm = jnp.full((8, C), total / entries + 1e-06, f32)
    shrink = jnp.minimum(1.0, clip_level / jnp.sqrt(norm))
    shrink_out[...] = shrink
    g_stage[...] = g * shrink[0:1]
    copy = pltpu.make_async_copy(g_stage, g_out, sems.at[stage.shape[0]])
    copy.start()
    copies = []
    put((o0, o1, o2), core, mine, 0, shrink[0:1], stage, sems, k_out, copies)
    put((p0, p1, p2), 1 - core, theirs, 0, shrink[0:1], stage, sems, k_out, copies)
    for c in (copy, *copies):
        c.wait()


def final_body(meta, o3, p3, shrink, k_in, k_out, stage, sems, *, chunks):
    core, mine, theirs = meta[0], meta[1], meta[2]
    first = chunks // 4 * 3
    copies = []
    put((o3,), core, mine, first, shrink[0:1], stage, sems, k_out, copies)
    put((p3,), 1 - core, theirs, first, shrink[0:1], stage, sems, k_out, copies)
    for c in copies:
        c.wait()


def across(a, b, axis):
    n = lax.axis_size(axis)
    even, odd = (
        [p for i in range(first, n - 1, 2) for p in ((i, i + 1), (i + 1, i))] for first in (0, 1)
    )
    b = lax.ppermute(b, axis, odd)
    a = lax.ppermute(a, axis, even)
    return a, b


def y_faces(pos, who, a, b, xa, xb):
    return call(
        pack_y_body,
        [sds((2, 144, C), bf16)] * 2,
        [pltpu.VMEM((18, 8, C), f32)],
        (pos, a, b, xa, xb),
        1,
        who=who,
    )


def plan():
    nx, ny = lax.axis_size("gx"), lax.axis_size("gy")
    xs = [(1 << i, 0) for i in range(nx.bit_length() - 1)]
    zs = [(0, 1 << i) for i in range(1, ny.bit_length() - 1)]
    k = min(len(zs), 4 - len(xs))
    orders = (xs + zs[:k], xs[1:] + xs[:1] + zs[:k])
    group = []
    for m in range(1, 1 << k):
        group.append(sum(zs[i][1] for i in range(k) if m >> (k - 1 - i) & 1))
    return orders, len(xs), group, [z for _, z in zs[k:]]


def pairs(dx, dy):
    nx, ny = lax.axis_size("gx"), lax.axis_size("gy")
    return [(i * ny + j, (i ^ dx[j % 2]) * ny + (j ^ dy)) for i in range(nx) for j in range(ny)]


def chunk_index(order, halvings, ix, iy):
    out = 0
    for s, (dx, dy) in enumerate(order[:halvings]):
        bit = ((ix & dx) | (iy & dy)) != 0
        out = out + bit.astype(jnp.int32) * (1 << (halvings - 1 - s))
    return jnp.asarray(out, jnp.int32)


def after(value, *done):
    return lax.optimization_barrier((value, *done))[0]


def per_device(features, brick_pos, cotangent, first_kernel, second_kernel, norm_gain):
    both = ("gx", "gy")
    ny = lax.axis_size("gy")
    orders, halvings, group, copies = plan()
    chunks = 1 << len(orders[0])

    def who():
        ix, iy = lax.axis_index("gx"), lax.axis_index("gy")
        core = iy % 2
        a, b = (chunk_index(o, len(o), ix, iy) for o in orders)
        return core, jnp.where(core == 0, a, b), jnp.where(core == 0, b, a), ix % 2

    partner = [(i, i ^ 1) for i in range(ny)]
    hbm = lambda v: pltpu.with_memory_space_constraint(v, pltpu.HBM)
    slots, brick_pos = brick_pos, hbm(brick_pos)
    n = TAPS * C
    size = n // chunks

    features, cotangent, sent, fa, fb = call(
        load_body,
        [sds((2, 512, C), bf16)] * 3 + [sds((2, 128, C), bf16)] * 2,
        [],
        (brick_pos, hbm(features), hbm(cotangent)),
        1,
        who=who,
    )
    xa, xb = across(fa, fb, "gx")
    ppos = lax.ppermute(slots, "gy", partner)
    other = lax.ppermute(sent, "gy", partner)
    straight, turned = sds((9 * C, 3 * C), bf16), sds((3 * C, 9 * C), bf16)
    w1, w2, t1, t2, gain = call(
        prep_body,
        [straight, straight, turned, turned, sds((1, C), f32)],
        [],
        (hbm(first_kernel), hbm(second_kernel), hbm(norm_gain.reshape(1, C))),
        0,
    )
    fa, fb = y_faces(brick_pos, who, after(features, gain), cotangent, xa, xb)
    fa = after(fa, ppos, other)
    edge = xa, xb, *across(fa, fb, "gy")
    grid = pltpu.VMEM((2, 18, 18, 8, C), f32)
    cols = pltpu.VMEM((512, 9 * C), bf16)
    hid, pre, msg, gain_part = call(
        main_body,
        [sds((2, 512, C), bf16)] * 2 + [sds((P_ROWS + sum(FACES), C), bf16), sds((8, C), f32)],
        [grid, pltpu.VMEM((4, 512, 9 * C), bf16), pltpu.VMEM((512, C), f32)],
        (brick_pos, features, cotangent, *edge, w1, t2, gain),
        1,
        14,
        who,
    )
    pmsg = lax.ppermute(msg, "gy", partner)
    held = [sds((18, 18, 8, C), f32), sds((3 * C, 1024), bf16)]
    wide = pltpu.VMEM((1024, JS * C), bf16)
    acc = pltpu.VMEM((JS * 3 * C, C), f32)
    grid_a, pt_a, part = call(
        functools.partial(own_body, chunks=chunks),
        held + [sds((3 * C, JS * C), f32)],
        [wide],
        (brick_pos, features, cotangent, *edge, hid, pre),
        1,
        10,
        who,
    )
    quarter = [sds((n // 4, C), bf16)] * 2
    grid_b, pt_b, out_b, out_a, g = call(
        functools.partial(send_body, chunks=chunks),
        held + quarter + [sds((8, C), f32)],
        [wide, pltpu.VMEM((3 * C, JS * C), f32), acc],
        (ppos, other, pmsg, gain_part, part),
        1,
        10,
        who,
    )
    keep_b, keep_a = call(
        functools.partial(keep_body, chunks=chunks),
        [sds((n // 4, C), f32)] * 2,
        [wide, wide, pltpu.VMEM((3 * C, JS * C), f32), acc],
        (brick_pos, ppos, grid_a, grid_b, pt_a, pt_b),
        2,
        12,
        who,
    )
    g = g[0:1]

    fa, fb = call(
        pack_x_body,
        [sds((2, 128, C), bf16)] * 2,
        [],
        (brick_pos, after(hid, out_a), pre),
        1,
        who=who,
    )
    xa, xb = across(fa, fb, "gx")
    fa, fb = y_faces(brick_pos, who, hid, pre, xa, xb)
    around = xa, xb, *across(fa, fb, "gy")
    results = []
    for f, (src, w, base) in enumerate(((hid, w2, features), (pre, t1, cotangent))):
        (res,) = call(
            functools.partial(out_body, field=f),
            [sds((2, 512, C), bf16)],
            [pltpu.VMEM((1, 18, 18, 8, C), f32), cols],
            (brick_pos, src, *around, w, base),
            1,
            10,
            who,
        )
        results.append(res)

    swap = lambda v, dx, dy=0: lax.ppermute(v, both, pairs(dx, dy))
    steps = [(a[0], b[0]) for a, b in zip(*orders)][:halvings]
    got_a = swap(out_a, steps[0])
    got_b = swap(out_b, steps[0])
    out = (keep_a + got_a.astype(f32)).astype(bf16)
    got = swap(out, steps[1])
    low = keep_b + got_b.astype(f32) + got.astype(f32)
    for step in steps[2:]:
        half = low.shape[0] // 2
        got = swap(low[half:].astype(bf16), step)
        low = low[:half] + got.astype(f32)
    got = []
    for m, dy in enumerate(group, 1):
        out = low[m * size : (m + 1) * size]
        got.append(swap(out if dy == 2 else out.astype(bf16), (0, 0), dy))
    low = low[:size]
    for v in got:
        low = low + v.astype(f32)
    for dy in copies:
        got = swap(jnp.concatenate([low, jnp.broadcast_to(g, (8, C))]), (0, 0), dy)
        low, g = low + got[:size], g + got[size : size + 1]

    (full,) = call(seal_body, [sds((size + 8, C), bf16)], [], (low, g), 0)
    full = join(full, *(swap(full, (0, 0), dy) for dy in group))
    for step in reversed(steps[2:]):
        full = join(full, swap(full, step))
    own = [full]
    own.append(swap(full, steps[1]))
    own.append(swap(full, steps[0]))
    (tiles,) = call(tiles_body, [sds((chunks // 4 * 8, C), bf16)], [], (full,), 0)
    far = swap(tiles, tuple(a ^ b for a, b in zip(*steps[:2])))
    far_part = lax.ppermute(far, "gy", partner)
    own.append(swap(own[1], steps[0]))
    part = [lax.ppermute(v, "gy", partner) for v in own]
    any_space = pl.BlockSpec(memory_space=pl.ANY)

    def pieces_call(body, count, outs, out_specs, scratch, args, in_specs, aliases):
        return pl.pallas_call(
            lambda *refs: body(who(), *refs, chunks=chunks),
            out_shape=outs,
            in_specs=in_specs,
            out_specs=out_specs,
            scratch_shapes=scratch
            + [pltpu.VMEM((count, size, C), f32)]
            + ([pltpu.VMEM((1, C), f32)] if scratch else [])
            + [pltpu.SemaphoreType.DMA((count + 1,))],
            input_output_aliases=aliases,
            compiler_params=pltpu.CompilerParams(vmem_limit_bytes=8 << 20),
        )(*args)

    table = pltpu.VMEM((2, chunks, 8, C), f32)
    k_up, g_up, shrink = pieces_call(
        gathered_body,
        chunks // 2 * 3,
        [sds((2, n, C), f32), sds((1, C), f32), sds((8, C), f32)],
        [any_space, any_space, VMEM],
        [table, table],
        (*own[:3], far, *part[:3], far_part),
        [VMEM] * 8,
        {},
    )
    (k_up,) = pieces_call(
        final_body,
        chunks // 2,
        [sds((2, n, C), f32)],
        [any_space],
        [],
        (own[3], part[3], shrink, k_up),
        [VMEM] * 3 + [any_space],
        {3: 0},
    )
    return (*results, k_up.reshape(2, TAPS, C, C), g_up.reshape(C))


def solution(mesh):
    rows = P(("gx", "gy"), None, None)

    return jax.shard_map(
        per_device,
        mesh=mesh,
        in_specs=(rows, P(("gx", "gy")), rows, P(), P(), P()),
        out_specs=(rows, rows, P(), P()),
        check_vma=False,
    )
```

```python
import functools

import jax
import jax.numpy as jnp
from jax import lax
from jax.experimental import pallas as pl
from jax.experimental.pallas import tpu as pltpu
from jax.sharding import PartitionSpec as P


BY = 2
POS = 4
TAPS = 27
P_ROWS = 1040
FACES = (128, 128, 144, 144)
C = 128
clip_level = 0.5
f32, bf16 = jnp.float32, jnp.bfloat16
VMEM = pl.BlockSpec(memory_space=pltpu.VMEM)
SMEM = pl.BlockSpec(memory_space=pltpu.SMEM)


def sds(shape, dtype):
    return jax.ShapeDtypeStruct(shape, dtype)


def place(pos_ref, slot):
    p = pos_ref[slot]
    q = jnp.minimum(p, POS - 1)
    return p < POS, q // BY, q % BY


def call(body, outs, scratch, args, n_smem, mib=4, who=None):
    def kernel(*refs):
        known = () if who is None else (who(),)
        body(*refs[:n_smem], *known, *refs[n_smem:])

    return pl.pallas_call(
        kernel,
        out_shape=outs,
        in_specs=[SMEM] * n_smem + [VMEM] * (len(args) - n_smem),
        out_specs=[VMEM] * len(outs),
        scratch_shapes=scratch,
        compiler_params=pltpu.CompilerParams(vmem_limit_bytes=mib << 20),
    )(*args)


def sides(odd, a, b):
    return jnp.where(odd == 0, b, a), jnp.where(odd == 0, a, b)


def pack_x(pos, odd, srcs, outs):
    for f, src in enumerate(srcs):
        for out, d in zip(outs, (1 - odd, odd)):
            out[f] = jnp.zeros(out.shape[1:], bf16)
            at = pl.multiple_of(d * 448, 64)
            for s in range(2):
                live, bx, by = place(pos, s)

                @pl.when(live & (bx == d))
                def _():
                    out[f, pl.ds(pl.multiple_of(by * 64, 64), 64)] = src[s, pl.ds(at, 64)]


def pack_x_body(pos, meta, a, b, *outs):
    pack_x(pos, meta[3], (a, b), outs)


def load_body(pos, meta, a, b, a_out, b_out, sent, *outs):
    pack_x(pos, meta[3], (a, b), outs)
    a_out[...] = a[...]
    b_out[...] = b[...]
    sent[...] = jnp.where(meta[0] == 0, b[...], a[...])


def pack_y_body(pos, meta, a, b, xa, xb, ya, yb, tmp):
    def edge_rows(v, d):
        v = v.astype(f32)
        return jnp.where(d == 0, v[0:8], v[8:16])

    for f, src in enumerate((a, b)):
        for out, d in ((ya, 1 - meta[0]), (yb, meta[0])):
            tmp[...] = jnp.zeros_like(tmp)
            rows = pl.ds(pl.multiple_of(d * 112, 16), 16)
            xl, xr = sides(meta[3], xa[f, rows], xb[f, rows])
            tmp[0] = edge_rows(xl, d)
            tmp[17] = edge_rows(xr, d)
            for s in range(2):
                live, bx, by = place(pos, s)

                @pl.when(live & (by == d))
                def _():
                    for x in range(8):
                        at = pl.multiple_of(x * 64 + d * 48, 16)
                        tmp[1 + bx * 8 + x] = edge_rows(src[s, pl.ds(at, 16)], d)

            out[f] = tmp[...].reshape(144, C).astype(bf16)


def build(grid, f, pos, src, xl, xr, yl, yr):
    grid = grid.at[f] if isinstance(f, int) else grid
    grid[...] = jnp.zeros(grid.shape, f32)
    for s in range(2):
        live, bx, by = place(pos, s)

        @pl.when(live)
        def _():
            grid[pl.ds(1 + bx * 8, 8), pl.ds(1 + by * 8, 8)] = src[s].astype(f32).reshape(8, 8, 8, C)

    grid[0, 1:17] = xl.astype(f32).reshape(16, 8, C)
    grid[17, 1:17] = xr.astype(f32).reshape(16, 8, C)
    grid[:, 0] = yl.astype(f32).reshape(18, 8, C)
    grid[:, 17] = yr.astype(f32).reshape(18, 8, C)


def faces(meta, f, xa, xb, ya, yb):
    return *sides(meta[3], xa[f], xb[f]), *sides(meta[0], ya[f], yb[f])


def window(grid, f, bx, by, j):
    sx, sy = j // 3, j % 3
    w = grid[f, pl.ds(bx * 8 + sx, 8), pl.ds(by * 8 + sy, 8)]
    return w.reshape(512, C).astype(bf16)


def up_z(v):
    z = lax.broadcasted_iota(jnp.int32, v.shape, 1)
    return jnp.where(z == 7, 0.0, pltpu.roll(v, 7, 1))


def down_z(v):
    z = lax.broadcasted_iota(jnp.int32, v.shape, 1)
    return jnp.where(z == 0, 0.0, pltpu.roll(v, 1, 1))


def prep_body(k1, k2, gain, w1, w2, t1, t2, gain_out):
    for k, w, t in ((k1, w1, t1), (k2, w2, t2)):
        for j in range(9):
            for oz in range(3):
                w[j * C : (j + 1) * C, oz * C : (oz + 1) * C] = k[3 * j + oz]
                t[oz * C : (oz + 1) * C, j * C : (j + 1) * C] = k[3 * (8 - j) + oz]
    gain_out[...] = gain[...]


def convolve(grid, f, bx, by, cols, w, flipped):
    for j in range(9):
        cols[:, j * C : (j + 1) * C] = window(grid, f, bx, by, j)
    dims = (((1,), (1,)), ((), ())) if flipped else (((1,), (0,)), ((), ()))
    y = lax.dot_general(cols[...], w[...], dims, preferred_element_type=f32)
    lower, mid, upper = (y[:, i * C : (i + 1) * C].reshape(64, 8, C) for i in range(3))
    if flipped:
        out = mid + up_z(lower) + down_z(upper)
    else:
        out = mid + down_z(lower) + up_z(upper)
    return out.reshape(512, C)


def split3(v):
    hi = v.astype(bf16).astype(f32)
    rest = v - hi
    mid = rest.astype(bf16).astype(f32)
    return hi, mid, rest - mid


def main_body(
    pos, meta, a, b, xa, xb, ya, yb, w1, w2, gain,
    hid, pre, msg, gain_part, grid, cols, hg
):
    core = meta[0]
    for f, src in enumerate((a, b)):
        build(grid, f, pos, src, *faces(meta, f, xa, xb, ya, yb))
    at = P_ROWS
    for face in faces(meta, 1 - core, xa, xb, ya, yb):
        msg[at : at + face.shape[0]] = face
        at += face.shape[0]
    g = gain[...]
    total = jnp.zeros((1, C), f32)
    for s in range(2):
        live, bx, by = place(pos, s)
        hg[s] = convolve(grid, 1, bx, by, cols.at[2 * s], w2, True)
        first = convolve(grid, 0, bx, by, cols.at[2 * s + 1], w1, False)
        center = first - jnp.mean(first, axis=1, keepdims=True)
        spread = jnp.mean(center * center, axis=1, keepdims=True)
        inv = lax.rsqrt(spread + 1e-05)
        n = center * inv
        v = n * g
        sig = jax.nn.sigmoid(v)
        on = jnp.where(live, 1.0, 0.0)
        h = jnp.where(live, v * sig, 0.0).astype(bf16)
        grad = jnp.where(live, hg[s], 0.0)
        dv = grad * (sig * (1.0 + v * (1.0 - sig)))
        total = total + jnp.sum(dv * n, axis=0, keepdims=True)
        dn = dv * g
        m1 = jnp.mean(dn, axis=1, keepdims=True)
        m2 = jnp.mean(dn * n, axis=1, keepdims=True)
        p = (inv * (dn - m1 - n * m2)).astype(bf16)
        hid[s] = h
        pre[s] = p
        msg[s * 512 : (s + 1) * 512] = jnp.where(core == 0, h, p)
    gain_part[...] = jnp.broadcast_to(total, (8, C))
    msg[1024:P_ROWS] = pack3(total)


def out_body(pos, meta, src, xa, xb, ya, yb, w, base, out, grid, cols, *, field):
    build(grid, 0, pos, src, *faces(meta, field, xa, xb, ya, yb))
    for s in range(2):
        live, bx, by = place(pos, s)
        y = convolve(grid, 0, bx, by, cols.at[s], w, field == 1)
        out[s] = jnp.where(live, base[s].astype(f32) + y, 0.0).astype(bf16)


JS = 5


def shifted(pt, slot, v):
    v = v.astype(f32).reshape(64, 8, C)
    for i, t in enumerate((up_z(v), v, down_z(v))):
        pt[i * C : (i + 1) * C, slot * 512 : (slot + 1) * 512] = t.reshape(512, C).T.astype(bf16)


def product(core, grid, pos, pt, upper, cols):
    for s in range(2):
        _, bx, by = place(pos, s)
        for i in range(JS):
            sx = jnp.where(upper, (i + 9 - JS) // 3, i // 3)
            sy = jnp.where(upper, (i + 9 - JS) % 3, i % 3)
            sx, sy = jnp.where(core == 0, sx, 2 - sx), jnp.where(core == 0, sy, 2 - sy)
            w = grid[pl.ds(bx * 8 + sx, 8), pl.ds(by * 8 + sy, 8)]
            cols[s * 512 : (s + 1) * 512, i * C : (i + 1) * C] = w.reshape(512, C).astype(bf16)
    return jnp.dot(pt[...], cols[...], preferred_element_type=f32)


def pieces(core, sums, acc, dsts, mine, upper, first, chunks):
    def block(i, oz):
        return sums[oz * C : (oz + 1) * C, i * C : (i + 1) * C]

    @pl.when(core == 0)
    def _():
        for i in range(JS):
            for oz in range(3):
                acc[(3 * i + oz) * C : (3 * i + oz + 1) * C] = block(i, oz).T

    @pl.when(core != 0)
    def _():
        for i in range(JS):
            for oz in range(3):
                acc[(3 * i + oz) * C : (3 * i + oz + 1) * C] = block(i, 2 - oz)

    size = TAPS * C // chunks
    skip = jnp.where(upper, (9 - JS) * 3 * C, 0)
    p = first
    for dst in dsts:
        for q in range(0, dst.shape[0] // size, 2):
            starts = [pl.multiple_of((mine ^ (p + i)) * size - skip, 8) for i in range(2)]
            two = jnp.concatenate([acc[pl.ds(a, size)] for a in starts])
            dst[q * size : (q + 2) * size] = two.astype(dst.dtype)
            p += 2


def sends_upper(mine, chunks):
    return mine < chunks // 2


def own_body(pos, meta, a, b, xa, xb, ya, yb, hid, pre, grid, pt, part, cols, *, chunks):
    core = meta[0]
    for f, src in enumerate((a, b)):

        @pl.when(core == f)
        def _():
            build(grid, None, pos, src, *faces(meta, f, xa, xb, ya, yb))

    for s in range(2):
        shifted(pt, s, jnp.where(core == 0, pre[s], hid[s]))
    part[...] = product(core, grid, pos, pt, sends_upper(meta[1], chunks), cols)


def send_body(
    ppos, meta, other, msg, gain_part, part, grid, pt, out_b, out_a, gsum, cols, sums, acc, *, chunks
):
    theirs, at = [], P_ROWS
    for rows in FACES:
        theirs.append(msg[at : at + rows])
        at += rows
    build(grid, None, ppos, other, *theirs)
    for s in range(2):
        shifted(pt, s, msg[s * 512 : (s + 1) * 512])
    upper = sends_upper(meta[1], chunks)
    sums[...] = part[...] + product(meta[0], grid, ppos, pt, upper, cols)
    pieces(meta[0], sums, acc, (out_b, out_a), meta[1], upper, chunks // 2, chunks)
    tile = msg[1024:P_ROWS].astype(f32)
    total = gain_part[0:1] + ((tile[2:3] + tile[1:2]) + tile[0:1])
    gsum[...] = jnp.broadcast_to(total, (8, C))


def keep_body(pos, ppos, meta, grid_a, grid_b, pt_a, pt_b, keep_b, keep_a, cols_a, cols_b, sums, acc, *, chunks):
    upper = jnp.logical_not(sends_upper(meta[1], chunks))
    sums[...] = product(meta[0], grid_a, pos, pt_a, upper, cols_a)
    sums[...] += product(meta[0], grid_b, ppos, pt_b, upper, cols_b)
    pieces(meta[0], sums, acc, (keep_b, keep_a), meta[1], upper, 0, chunks)


def pack3(v):
    hi, mid, low = split3(v)
    row = lax.broadcasted_iota(jnp.int32, (16, C), 0)
    return jnp.where(row == 0, hi, jnp.where(row == 1, mid, jnp.where(row == 2, low, 0.0))).astype(bf16)


def seal_body(low, g, out):
    v = low[...].astype(bf16).astype(f32)
    squares = jnp.sum(jnp.sum((v * v).reshape(-1, 8, C), axis=0), axis=0, keepdims=True)
    row = lax.broadcasted_iota(jnp.int32, (8, C), 0)
    tile = jnp.zeros((8, C), f32)
    for i, part in enumerate((*split3(g[0:1]), *split3(squares))):
        tile = jnp.where(row == i, part, tile)
    out[...] = jnp.concatenate([v, tile]).astype(bf16)


def tiles_body(pieces, out):
    n = out.shape[0] // 8
    step = pieces.shape[0] // n
    for i in range(n):
        out[i * 8 : (i + 1) * 8] = pieces[(i + 1) * step - 8 : (i + 1) * step]


def join_body(*refs):
    out, at = refs[-1], 0
    for ref in refs[:-1]:
        out[at : at + ref.shape[0]] = ref[...]
        at += ref.shape[0]


def join(*parts):
    rows = sum(p.shape[0] for p in parts)
    (out,) = call(join_body, [sds((rows, C), bf16)], [], parts, 0)
    return out


def put(pieces, k, me, first, shrink, stage, sems, out, copies):
    size = stage.shape[1]
    for src in pieces:
        for q in range(src.shape[0] // (size + 8)):
            n = len(copies)
            v = src[q * (size + 8) : (q + 1) * (size + 8)].astype(f32)
            stage[n] = v[:size] * shrink
            rows = pl.ds(pl.multiple_of((me ^ (first + q)) * size, 8), size)
            copies.append(pltpu.make_async_copy(stage.at[n], out.at[k, rows], sems.at[n]))
            copies[-1].start()
        first += src.shape[0] // (size + 8)


def gathered_body(
    meta, o0, o1, o2, o3, p0, p1, p2, p3, k_out, g_out, shrink_out, gains, squares, stage, g_stage, sems, *, chunks
):
    core, mine, theirs = meta[0], meta[1], meta[2]
    n = TAPS * C
    step = n // chunks + 8
    for k, me, pieces, tiles in (
        (core, mine, (o0, o1, o2), o3), (1 - core, theirs, (p0, p1, p2), p3)
    ):
        quarter = chunks // 4
        for p in range(chunks):
            q = p % quarter
            ref, at = (tiles, q * 8) if p >= 3 * quarter else (pieces[p // quarter], (q + 1) * step - 8)
            t = ref[at : at + 8].astype(f32)
            gains[k, me ^ p] = jnp.broadcast_to((t[2:3] + t[1:2]) + t[0:1], (8, C))
            squares[k, me ^ p] = jnp.broadcast_to((t[5:6] + t[4:5]) + t[3:4], (8, C))
    g = jnp.sum(gains[0], axis=0)[0:1]
    total = jnp.sum(g * g) + jnp.sum(jnp.sum(squares[...].reshape(2 * chunks, 8, C), axis=0)[0:1])
    entries = 2.0 * n * C + C
    norm = jnp.full((8, C), total / entries + 1e-06, f32)
    shrink = jnp.minimum(1.0, clip_level / jnp.sqrt(norm))
    shrink_out[...] = shrink
    g_stage[...] = g * shrink[0:1]
    copy = pltpu.make_async_copy(g_stage, g_out, sems.at[stage.shape[0]])
    copy.start()
    copies = []
    put((o0, o1, o2), core, mine, 0, shrink[0:1], stage, sems, k_out, copies)
    put((p0, p1, p2), 1 - core, theirs, 0, shrink[0:1], stage, sems, k_out, copies)
    for c in (copy, *copies):
        c.wait()


def final_body(meta, o3, p3, shrink, k_in, k_out, stage, sems, *, chunks):
    core, mine, theirs = meta[0], meta[1], meta[2]
    first = chunks // 4 * 3
    copies = []
    put((o3,), core, mine, first, shrink[0:1], stage, sems, k_out, copies)
    put((p3,), 1 - core, theirs, first, shrink[0:1], stage, sems, k_out, copies)
    for c in copies:
        c.wait()


def across(a, b, axis):
    n = lax.axis_size(axis)
    even, odd = (
        [p for i in range(first, n - 1, 2) for p in ((i, i + 1), (i + 1, i))] for first in (0, 1)
    )
    b = lax.ppermute(b, axis, odd)
    a = lax.ppermute(a, axis, even)
    return a, b


def y_faces(pos, who, a, b, xa, xb):
    return call(
        pack_y_body,
        [sds((2, 144, C), bf16)] * 2,
        [pltpu.VMEM((18, 8, C), f32)],
        (pos, a, b, xa, xb),
        1,
        who=who,
    )


def plan():
    nx, ny = lax.axis_size("gx"), lax.axis_size("gy")
    xs = [(1 << i, 0) for i in range(nx.bit_length() - 1)]
    zs = [(0, 1 << i) for i in range(1, ny.bit_length() - 1)]
    k = min(len(zs), 4 - len(xs))
    orders = (xs + zs[:k], xs[1:] + xs[:1] + zs[:k])
    group = []
    for m in range(1, 1 << k):
        group.append(sum(zs[i][1] for i in range(k) if m >> (k - 1 - i) & 1))
    return orders, len(xs), group, [z for _, z in zs[k:]]


def pairs(dx, dy):
    nx, ny = lax.axis_size("gx"), lax.axis_size("gy")
    return [(i * ny + j, (i ^ dx[j % 2]) * ny + (j ^ dy)) for i in range(nx) for j in range(ny)]


def chunk_index(order, halvings, ix, iy):
    out = 0
    for s, (dx, dy) in enumerate(order[:halvings]):
        bit = ((ix & dx) | (iy & dy)) != 0
        out = out + bit.astype(jnp.int32) * (1 << (halvings - 1 - s))
    return jnp.asarray(out, jnp.int32)


def after(value, *done):
    return lax.optimization_barrier((value, *done))[0]


def per_device(features, brick_pos, cotangent, first_kernel, second_kernel, norm_gain):
    both = ("gx", "gy")
    ny = lax.axis_size("gy")
    orders, halvings, group, copies = plan()
    chunks = 1 << len(orders[0])

    def who():
        ix, iy = lax.axis_index("gx"), lax.axis_index("gy")
        core = iy % 2
        a, b = (chunk_index(o, len(o), ix, iy) for o in orders)
        return core, jnp.where(core == 0, a, b), jnp.where(core == 0, b, a), ix % 2

    partner = [(i, i ^ 1) for i in range(ny)]
    hbm = lambda v: pltpu.with_memory_space_constraint(v, pltpu.HBM)
    slots, brick_pos = brick_pos, hbm(brick_pos)
    n = TAPS * C
    size = n // chunks

    features, cotangent, sent, fa, fb = call(
        load_body,
        [sds((2, 512, C), bf16)] * 3 + [sds((2, 128, C), bf16)] * 2,
        [],
        (brick_pos, hbm(features), hbm(cotangent)),
        1,
        who=who,
    )
    xa, xb = across(fa, fb, "gx")
    ppos = lax.ppermute(slots, "gy", partner)
    other = lax.ppermute(sent, "gy", partner)
    straight, turned = sds((9 * C, 3 * C), bf16), sds((3 * C, 9 * C), bf16)
    w1, w2, t1, t2, gain = call(
        prep_body,
        [straight, straight, turned, turned, sds((1, C), f32)],
        [],
        (hbm(first_kernel), hbm(second_kernel), hbm(norm_gain.reshape(1, C))),
        0,
    )
    fa, fb = y_faces(brick_pos, who, after(features, gain), cotangent, xa, xb)
    fa = after(fa, ppos, other)
    edge = xa, xb, *across(fa, fb, "gy")
    grid = pltpu.VMEM((2, 18, 18, 8, C), f32)
    cols = pltpu.VMEM((2, 512, 9 * C), bf16)
    hid, pre, msg, gain_part = call(
        main_body,
        [sds((2, 512, C), bf16)] * 2 + [sds((P_ROWS + sum(FACES), C), bf16), sds((8, C), f32)],
        [grid, pltpu.VMEM((4, 512, 9 * C), bf16), pltpu.VMEM((2, 512, C), f32)],
        (brick_pos, features, cotangent, *edge, w1, t2, gain),
        1,
        14,
        who,
    )
    pmsg = lax.ppermute(msg, "gy", partner)
    held = [sds((18, 18, 8, C), f32), sds((3 * C, 1024), bf16)]
    wide = pltpu.VMEM((1024, JS * C), bf16)
    acc = pltpu.VMEM((JS * 3 * C, C), f32)
    grid_a, pt_a, part = call(
        functools.partial(own_body, chunks=chunks),
        held + [sds((3 * C, JS * C), f32)],
        [wide],
        (brick_pos, features, cotangent, *edge, hid, pre),
        1,
        10,
        who,
    )
    quarter = [sds((n // 4, C), bf16)] * 2
    grid_b, pt_b, out_b, out_a, g = call(
        functools.partial(send_body, chunks=chunks),
        held + quarter + [sds((8, C), f32)],
        [wide, pltpu.VMEM((3 * C, JS * C), f32), acc],
        (ppos, other, pmsg, gain_part, part),
        1,
        10,
        who,
    )
    keep_b, keep_a = call(
        functools.partial(keep_body, chunks=chunks),
        [sds((n // 4, C), f32)] * 2,
        [wide, wide, pltpu.VMEM((3 * C, JS * C), f32), acc],
        (brick_pos, ppos, grid_a, grid_b, pt_a, pt_b),
        2,
        12,
        who,
    )
    g = g[0:1]

    fa, fb = call(
        pack_x_body,
        [sds((2, 128, C), bf16)] * 2,
        [],
        (brick_pos, after(hid, out_a), pre),
        1,
        who=who,
    )
    xa, xb = across(fa, fb, "gx")
    fa, fb = y_faces(brick_pos, who, hid, pre, xa, xb)
    around = xa, xb, *across(fa, fb, "gy")
    results = []
    for f, (src, w, base) in enumerate(((hid, w2, features), (pre, t1, cotangent))):
        (res,) = call(
            functools.partial(out_body, field=f),
            [sds((2, 512, C), bf16)],
            [pltpu.VMEM((1, 18, 18, 8, C), f32), cols],
            (brick_pos, src, *around, w, base),
            1,
            10,
            who,
        )
        results.append(res)

    swap = lambda v, dx, dy=0: lax.ppermute(v, both, pairs(dx, dy))
    steps = [(a[0], b[0]) for a, b in zip(*orders)][:halvings]
    got_a = swap(out_a, steps[0])
    got_b = swap(out_b, steps[0])
    out = (keep_a + got_a.astype(f32)).astype(bf16)
    got = swap(out, steps[1])
    low = keep_b + got_b.astype(f32) + got.astype(f32)
    for step in steps[2:]:
        half = low.shape[0] // 2
        got = swap(low[half:].astype(bf16), step)
        low = low[:half] + got.astype(f32)
    got = []
    for m, dy in enumerate(group, 1):
        out = low[m * size : (m + 1) * size]
        got.append(swap(out if dy == 2 else out.astype(bf16), (0, 0), dy))
    low = low[:size]
    for v in got:
        low = low + v.astype(f32)
    for dy in copies:
        got = swap(jnp.concatenate([low, jnp.broadcast_to(g, (8, C))]), (0, 0), dy)
        low, g = low + got[:size], g + got[size : size + 1]

    (full,) = call(seal_body, [sds((size + 8, C), bf16)], [], (low, g), 0)
    full = join(full, *(swap(full, (0, 0), dy) for dy in group))
    for step in reversed(steps[2:]):
        full = join(full, swap(full, step))
    own = [full]
    own.append(swap(full, steps[1]))
    own.append(swap(full, steps[0]))
    (tiles,) = call(tiles_body, [sds((chunks // 4 * 8, C), bf16)], [], (full,), 0)
    far = swap(tiles, tuple(a ^ b for a, b in zip(*steps[:2])))
    far_part = lax.ppermute(far, "gy", partner)
    own.append(swap(own[1], steps[0]))
    part = [lax.ppermute(v, "gy", partner) for v in own]
    any_space = pl.BlockSpec(memory_space=pl.ANY)

    def pieces_call(body, count, outs, out_specs, scratch, args, in_specs, aliases):
        return pl.pallas_call(
            lambda *refs: body(who(), *refs, chunks=chunks),
            out_shape=outs,
            in_specs=in_specs,
            out_specs=out_specs,
            scratch_shapes=scratch
            + [pltpu.VMEM((count, size, C), f32)]
            + ([pltpu.VMEM((1, C), f32)] if scratch else [])
            + [pltpu.SemaphoreType.DMA((count + 1,))],
            input_output_aliases=aliases,
            compiler_params=pltpu.CompilerParams(vmem_limit_bytes=8 << 20),
        )(*args)

    table = pltpu.VMEM((2, chunks, 8, C), f32)
    k_up, g_up, shrink = pieces_call(
        gathered_body,
        chunks // 2 * 3,
        [sds((2, n, C), f32), sds((1, C), f32), sds((8, C), f32)],
        [any_space, any_space, VMEM],
        [table, table],
        (*own[:3], far, *part[:3], far_part),
        [VMEM] * 8,
        {},
    )
    (k_up,) = pieces_call(
        final_body,
        chunks // 2,
        [sds((2, n, C), f32)],
        [any_space],
        [],
        (own[3], part[3], shrink, k_up),
        [VMEM] * 3 + [any_space],
        {3: 0},
    )
    return (*results, k_up.reshape(2, TAPS, C, C), g_up.reshape(C))


def solution(mesh):
    rows = P(("gx", "gy"), None, None)

    return jax.shard_map(
        per_device,
        mesh=mesh,
        in_specs=(rows, P(("gx", "gy")), rows, P(), P(), P()),
        out_specs=(rows, rows, P(), P()),
        check_vma=False,
    )
```
